32 devices in a mesh: dp: 8 (over y, x, core), mp: 4 (over z).
Axes of the slice: x: 2, y: 2, z: 4, core: 2. Of those that a mesh axis runs over, the one named last changes fastest.
Arguments:
- layer_input: bfloat16 [6464, 768], P(('dp', 'mp')), may hold values from -6 to 6
- lengths: int32 [32], P('dp'), may hold values from 10 to 202, as said below
- ln1_gain: float32 [768], replicated, may hold values from 0.5 to 1.5
- ln1_bias: float32 [768], replicated, may hold values from -1.25 to 1.25
- w_qkv: bfloat16 [768, 2304], P(None, 'mp'), may hold values from -0.21875 to 0.21875
- b_qkv: float32 [2304], P('mp'), may hold values from -1.25 to 1.25
- features: float32 [12, 64, 32], P('mp'), may hold values from -6 to 6
- w_out: bfloat16 [768, 768], P('mp'), may hold values from -1.75 to 1.75
- b_out: float32 [768], replicated, may hold values from -1.25 to 1.25
- ln2_gain: float32 [768], replicated, may hold values from 0.5 to 1.5
- ln2_bias: float32 [768], replicated, may hold values from -1.25 to 1.25
- w_up: bfloat16 [768, 3072], P(None, 'mp'), may hold values from -0.21875 to 0.21875
- b_up: float32 [3072], P('mp'), may hold values from -1.25 to 1.25
- w_down: bfloat16 [3072, 768], P('mp'), may hold values from -0.109375 to 0.109375
- b_down: float32 [768], replicated, may hold values from -1.25 to 1.25
- cotangent: bfloat16 [6464, 768], P(('dp', 'mp')), may hold values from -6 to 6
Outputs:
- layer_output: bfloat16 [6464, 768], P(('dp', 'mp'))
- grad_x: float32 [6464, 768], P(('dp', 'mp'))
- grad_ln1_gain: float32 [768], replicated
- grad_ln1_bias: float32 [768], replicated
- grad_w_qkv: float32 [768, 2304], P('dp', 'mp')
- grad_b_qkv: float32 [2304], P('mp')
- grad_w_out: float32 [768, 768], P('mp', 'dp')
- grad_b_out: float32 [768], replicated
- grad_ln2_gain: float32 [768], replicated
- grad_ln2_bias: float32 [768], replicated
- grad_w_up: float32 [768, 3072], P('dp', 'mp')
- grad_b_up: float32 [3072], P('mp')
- grad_w_down: float32 [3072, 768], P('mp', 'dp')
- grad_b_down: float32 [768], replicated
The draws below stay inside these ranges and needn't reach their ends.
Inputs may be any that keep to these rules, and one draw needn't show every extreme that they name: A molecule's live tokens are the first lengths[m] of its 202 slots; some molecule has exactly 202 and some exactly 10.
All inputs are finite; a program needn't handle non-finite values.
Results may differ from the reference program's by a relative error of at most 0.02.
Values may be sent and summed in bfloat16 or wider, within the bound.
A program may use at most 128 MiB of HBM per device.

```python
import jax
import jax.numpy as jnp
from jax import lax

D = 768
HEADS = 12
HEAD_DIM = 64
FEATS = 32
FF = 3072
MAXLEN = 202
MOL_DEV = 4
MOLS = 32
TOKENS = 6464
N_DP = 8


def draw_lengths(key, part):
    drawn = jax.random.randint(key, (MOLS,), 10, MAXLEN + 1)
    return drawn.at[0].set(MAXLEN).at[1].set(10).astype(jnp.int32)


def shard_levels(own_key, dims, split, low, top_value):
    level = 1.0
    for position, blocks in split:
        steps = jax.random.uniform(jax.random.fold_in(jax.random.fold_in(own_key, 6), position), (blocks,), jnp.float32, low / len(split), top_value / len(split))
        level = level * jnp.repeat(jnp.exp(steps), dims[position] // blocks).reshape((-1,) + (1,) * (len(dims) - 1 - position))
    return level


def normal_values(stream_key, dims, deviation, most, shards=(), held_as=jnp.bfloat16):
    level = shard_levels(stream_key, dims, shards, -0.22, 0.18) if shards else 1.0
    values = jax.random.normal(stream_key, dims, jnp.float32) * deviation * level
    return jnp.minimum(jnp.maximum(values, -most), most).astype(held_as)


def setup_inputs(seed: int = 0) -> dict:
    streams_of = jax.random.split(jax.random.key(seed), 17)
    return {
        "layer_input": normal_values(streams_of[0], (TOKENS, D), 1.0, 6.0, ((0, 32),)),
        "lengths": draw_lengths(jax.random.fold_in(streams_of[16], 71), 0),
        "ln1_gain": jnp.clip(1.0 + 0.1 * jax.random.normal(streams_of[2], (D,), jnp.float32), 0.5, 1.5),
        "ln1_bias": normal_values(streams_of[3], (D,), 0.2, 1.25, (), jnp.float32),
        "w_qkv": normal_values(streams_of[4], (D, 3 * D), D ** -0.5, 0.21875, ((1, 4),)),
        "b_qkv": normal_values(streams_of[5], (3 * D,), 0.2, 1.25, ((0, 4),), jnp.float32),
        "features": normal_values(streams_of[6], (HEADS, HEAD_DIM, FEATS), 1.0, 6.0, ((0, 4),), jnp.float32),
        "w_out": normal_values(streams_of[7], (D, D), (D // 64) ** -0.5, 1.75, ((0, 4),)),
        "b_out": normal_values(streams_of[8], (D,), 0.2, 1.25, (), jnp.float32),
        "ln2_gain": jnp.clip(1.0 + 0.1 * jax.random.normal(streams_of[9], (D,), jnp.float32), 0.5, 1.5),
        "ln2_bias": normal_values(streams_of[10], (D,), 0.2, 1.25, (), jnp.float32),
        "w_up": normal_values(streams_of[11], (D, FF), D ** -0.5, 0.21875, ((1, 4),)),
        "b_up": normal_values(streams_of[12], (FF,), 0.2, 1.25, ((0, 4),), jnp.float32),
        "w_down": normal_values(streams_of[13], (FF, D), FF ** -0.5, 0.109375, ((0, 4),)),
        "b_down": normal_values(streams_of[14], (D,), 0.2, 1.25, (), jnp.float32),
        "cotangent": normal_values(streams_of[15], (TOKENS, D), 1.0, 6.0, ((0, 32),)),
    }


@jax.custom_vjp
def low(v):
    return lax.optimization_barrier(v.astype(jnp.bfloat16)).astype(jnp.float32)

@jax.custom_vjp
def low_back(v):
    return v

def low_keep(v):
    return (low(v), None)

def low_pass(kept, grad):
    return (grad,)

def back_keep(v):
    return (v, None)

def back_low(kept, grad):
    return (low(grad),)
low.defvjp(low_keep, low_pass)
low_back.defvjp(back_keep, back_low)
EPSILON = 1e-05

def matmul(left, right):
    return jnp.dot(left, right, precision=lax.Precision.HIGHEST)

def norm_rows(values, gain, shift):
    centred = values - lax.optimization_barrier(jnp.mean(values, axis=-1, keepdims=True))
    factor = lax.rsqrt(lax.optimization_barrier(jnp.mean(centred * centred, axis=-1, keepdims=True)) + EPSILON)
    return centred * factor * gain + shift

def rotate(values, positions):
    half = values.shape[-1] // 2
    freq = 10000.0 ** (-jnp.arange(half, dtype=jnp.float32) * 2.0 / values.shape[-1])
    angle = positions.astype(jnp.float32)[:, None] * freq[None, :]
    cosine = jnp.concatenate([jnp.cos(angle), jnp.cos(angle)], axis=-1)[:, None, :]
    sine = jnp.concatenate([jnp.sin(angle), jnp.sin(angle)], axis=-1)[:, None, :]
    turned = jnp.concatenate([-values[..., half:], values[..., :half]], axis=-1)
    return values * cosine + turned * sine

def featurize(projected, features, positions):
    heads = features.shape[0]
    head_size = features.shape[1]
    blocks = projected.reshape(projected.shape[0], heads, 3, head_size)
    factor = head_size ** (-0.25)
    query = rotate(blocks[:, :, 0], positions) * factor
    keyed = rotate(blocks[:, :, 1], positions) * factor
    map_q = jax.nn.elu(jnp.einsum('ghe,hef->ghf', query, features, precision=lax.Precision.HIGHEST)) + 1.0
    map_k = jax.nn.elu(jnp.einsum('ghe,hef->ghf', keyed, features, precision=lax.Precision.HIGHEST)) + 1.0
    return (map_q, map_k, blocks[:, :, 2])

def core(map_q, map_k, column_block, key_mask, molecules):
    total_rows, heads, feats = map_q.shape
    head_size = column_block.shape[-1]
    span = total_rows // molecules
    query_maps = map_q.reshape(molecules, span, heads, feats)
    key_maps = (map_k * key_mask[:, None, None]).reshape(molecules, span, heads, feats)
    values_four = column_block.reshape(molecules, span, heads, head_size)
    state = jnp.einsum('mlhf,mlhe->mhfe', key_maps, values_four, precision=lax.Precision.HIGHEST)
    summed = lax.optimization_barrier(jnp.sum(key_maps, axis=1))
    numer = jnp.einsum('mlhf,mhfe->mlhe', query_maps, state, precision=lax.Precision.HIGHEST)
    denom = jnp.einsum('mlhf,mhf->mlh', query_maps, summed, precision=lax.Precision.HIGHEST)
    return (numer / denom[..., None]).reshape(total_rows, heads * head_size)

def forward(inputs, key_mask, positions, features, molecules, ln1_gain, ln1_bias, w_qkv, b_qkv, w_out, b_out, ln2_gain, ln2_bias, w_up, b_up, w_down, b_down):
    first = low(norm_rows(inputs, ln1_gain, ln1_bias))
    projected = low_back(matmul(first, w_qkv) + b_qkv)
    map_q, map_k, column_block = featurize(projected, features, positions)
    attended = core(low(map_q), low(map_k), low(column_block), key_mask, molecules)
    branch = low_back(matmul(low(attended), w_out) + b_out)
    middle = inputs + branch
    second = low(norm_rows(middle, ln2_gain, ln2_bias))
    pre_act = low_back(matmul(second, w_up) + b_up)
    hidden = low(jax.nn.gelu(pre_act, approximate=False))
    ffn_branch = low_back(matmul(hidden, w_down) + b_down)
    return middle + ffn_branch

def reference(layer_input, lengths, ln1_gain, ln1_bias, w_qkv, b_qkv, features, w_out, b_out, ln2_gain, ln2_bias, w_up, b_up, w_down, b_down, cotangent):
    weights = tuple((member.astype(jnp.float32) for member in (ln1_gain, ln1_bias, w_qkv, b_qkv, w_out, b_out, ln2_gain, ln2_bias, w_up, b_up, w_down, b_down)))
    group_rows = MOL_DEV * MAXLEN
    inputs = layer_input.astype(jnp.float32).reshape(N_DP, group_rows, D)
    grads_in = cotangent.astype(jnp.float32).reshape(N_DP, group_rows, D)
    grouped = lengths.reshape(N_DP, MOL_DEV)
    slot_index = jnp.arange(MAXLEN, dtype=jnp.int32)
    positions = jnp.tile(slot_index, MOL_DEV)
    feature_map = features.astype(jnp.float32)

    def step(totals, element):
        block, counts, grad_block = element
        key_mask = (slot_index[None, :] < counts[:, None]).astype(jnp.float32).reshape(group_rows)

        def run(block_in, *params):
            return forward(block_in, key_mask, positions, feature_map, MOL_DEV, *params)
        result, pull = jax.vjp(run, block, *weights)
        grads = pull(grad_block)
        totals = tuple((total + grad for total, grad in zip(totals, grads[1:])))
        return (totals, (result.astype(jnp.bfloat16), grads[0]))
    zeros = tuple((jnp.zeros_like(member) for member in weights))
    totals, (outputs, grad_inputs) = lax.scan(step, zeros, (inputs, grouped, grads_in))
    return (outputs.reshape(N_DP * group_rows, D), grad_inputs.reshape(N_DP * group_rows, D), totals[0], totals[1], totals[2], totals[3], totals[4], totals[5], totals[6], totals[7], totals[8], totals[9], totals[10], totals[11])
```

```python
import functools

import jax
import jax.numpy as jnp
import numpy as np
from jax import lax
from jax.experimental import pallas as pl
from jax.experimental.pallas import tpu as pltpu
from jax.sharding import PartitionSpec as P

MESH = pl.DeviceIdType.MESH
BF16 = jnp.bfloat16
F32 = jnp.float32
EPSILON = 1e-05
GROUP = 8


def dot_nn(left, right):
    return lax.dot_general(left, right, (((1,), (0,)), ((), ())), preferred_element_type=F32)


def dot_nt(left, right):
    return lax.dot_general(left, right, (((1,), (1,)), ((), ())), preferred_element_type=F32)


def dot_tn(left, right):
    return lax.dot_general(left, right, (((0,), (0,)), ((), ())), preferred_element_type=F32)


def split(values):
    high = values.astype(BF16)
    return high, (values - high.astype(F32)).astype(BF16)


def normalize(values):
    centred = values - jnp.mean(values, axis=-1, keepdims=True)
    factor = lax.rsqrt(jnp.mean(centred * centred, axis=-1, keepdims=True) + EPSILON)
    return centred * factor, factor


def norm_back(grad, gain, normed, factor):
    hat = grad * gain
    return factor * (
        hat
        - jnp.mean(hat, axis=-1, keepdims=True)
        - normed * jnp.mean(hat * normed, axis=-1, keepdims=True)
    )


def column_sum(values):
    return jnp.sum(values, axis=0, keepdims=True)


def swap_halves(values):
    width = values.shape[1]
    lane = lax.broadcasted_iota(jnp.int32, values.shape, 1)
    return jnp.where(lane % 64 < 32, pltpu.roll(values, width - 32, 1), pltpu.roll(values, 32, 1))


def layer_kernel(live, *refs):
    (
        x_ref, c_ref, len_ref, vec_ref, feat_ref, trig_ref, wqkv_ref, wout_ref, wup_ref, wdown_ref,
        y_ref, gx_ref, gq_ref, go_ref, gu_ref, gd_ref, sv_ref,
        W, SP, CC, H2, CT, H2T, H1, H1T, GO, GOT, N1, R1, X1, N2, R2, DX1, DH1,
        COS, SIN, FH, FL, PHI, EE, VV, ATT, INV, AP, ST, TT, DA, ACT, DPRE, DQ,
        OS, OR, HS, HR, G, Q0, QX, QY, T2, Q2, U, ZR, AR, SV,
        local_sem, zs, zr, ags, agr, xs, xr, rs, rr, vs, vr,
    ) = refs
    rows = CC.shape[0] // 2
    dp = lax.axis_index("dp")
    z = lax.axis_index("mp")
    member = dp % GROUP
    c = member % 2
    bx = (member // 2) % 2
    by = member // 4
    nx = (dp + 2 - 4 * bx, z)
    ny = (dp + 4 - 8 * by, z)
    nc = (dp + 1 - 2 * c, z)
    nz = (None, (dp, z + 1 - 2 * (z % 2)), (dp, (z + 2) % 4), (dp, 3 - z))

    def place(yy, xx, cc):
        return pl.multiple_of((yy * 4 + xx * 2 + cc) * 96, 96)

    sends = []

    def send(src, dst, send_sem, recv_sem, device):
        copy = pltpu.make_async_remote_copy(
            src_ref=src, dst_ref=dst, send_sem=send_sem, recv_sem=recv_sem,
            device_id=device, device_id_type=MESH,
        )
        copy.start()
        sends.append(copy)

    def arrive(dst, recv_sem):
        pltpu.make_async_remote_copy(
            src_ref=dst, dst_ref=dst, send_sem=recv_sem, recv_sem=recv_sem,
            device_id=nc, device_id_type=MESH,
        ).wait_recv()

    barrier = pltpu.get_barrier_semaphore()
    for device in (nx, ny, nc, nz[1], nz[2], nz[3]):
        pl.semaphore_signal(barrier, inc=1, device_id=device, device_id_type=MESH)

    up_copy = pltpu.make_async_copy(wup_ref, W.at[4], local_sem.at[0])
    up_copy.start()
    down_copy = pltpu.make_async_copy(wdown_ref, W.at[5], local_sem.at[1])
    down_copy.start()

    qkv_own = wqkv_ref[...]
    packed = [qkv_own[:, h * 192 + s * 64:h * 192 + s * 64 + 64] for s in range(3) for h in range(3)]
    W[0] = jnp.concatenate(packed + [wout_ref[...].T], axis=1)
    feat = jnp.concatenate([feat_ref[h] for h in range(3)] + [jnp.zeros((64, 32), F32)], axis=1)
    SP[0, 0:64, :] = feat
    qkv_bias = vec_ref[7:8, 0:576]
    qkv_bias = jnp.concatenate(
        [qkv_bias[:, h * 192 + s * 64:h * 192 + s * 64 + 64] for s in range(3) for h in range(3)]
        + [jnp.zeros((1, 64), F32)], axis=1)
    for i in range(5):
        SP[0, 64 + i:65 + i, :] = qkv_bias[:, i * 128:i * 128 + 128]
    for i in range(6):
        SP[0, 72 + i:73 + i, :] = vec_ref[6:7, i * 128:i * 128 + 128]
    CC[0:rows, :] = jnp.concatenate([c_ref[...].astype(F32), jnp.zeros((rows - live, 768), F32)], axis=0).astype(BF16)

    pl.semaphore_wait(barrier, 6)

    own = pl.ds(place(by, bx, c), 96)
    for r in (1, 2, 3):
        send(SP.at[0], SP.at[r], zs.at[8 + r], zr.at[8 + r], nz[r])
        send(W.at[0, own], W.at[r, own], zs.at[r], agr.at[r, 0], nz[r])
    send(wup_ref.at[own], W.at[6, own], zs.at[6], agr.at[6, 0], nz[2])
    send(CC.at[0:rows], CC.at[rows:2 * rows], xs.at[0], xr.at[0], nz[1])
    send(wdown_ref.at[own], W.at[7, own], zs.at[7], agr.at[7, 0], nz[2])

    at_x = pl.ds(place(by, 1 - bx, c), 96)
    at_y = pl.ds(place(1 - by, bx, c), 96)
    at_d = pl.ds(place(1 - by, 1 - bx, c), 96)
    at_x0 = pl.ds(place(by, 1 - bx, c), 48)
    at_y1 = pl.ds(pl.multiple_of(place(1 - by, bx, c) + 48, 48), 48)
    at_d0 = pl.ds(place(1 - by, 1 - bx, c), 48)
    at_d1 = pl.ds(pl.multiple_of(place(1 - by, 1 - bx, c) + 48, 48), 48)

    def gather_a(b):
        arrive(W.at[b, own], agr.at[b, 0])
        send(W.at[b, own], W.at[b, own], ags.at[b, 0], agr.at[b, 1], nx)
        send(W.at[b, own], W.at[b, own], ags.at[b, 1], agr.at[b, 2], ny)
        send(W.at[b, own], W.at[b, own], ags.at[b, 2], agr.at[b, 5], nc)

    def gather_b(b):
        arrive(W.at[b, at_x], agr.at[b, 1])
        send(W.at[b, at_x0], W.at[b, at_x0], ags.at[b, 3], agr.at[b, 3], ny)
        send(W.at[b, at_x], W.at[b, at_x], ags.at[b, 4], agr.at[b, 6], nc)
        arrive(W.at[b, at_y], agr.at[b, 2])
        send(W.at[b, at_y1], W.at[b, at_y1], ags.at[b, 5], agr.at[b, 4], nx)
        send(W.at[b, at_y], W.at[b, at_y], ags.at[b, 6], agr.at[b, 7], nc)

    def gather_c(b):
        arrive(W.at[b, at_d0], agr.at[b, 3])
        arrive(W.at[b, at_d1], agr.at[b, 4])
        send(W.at[b, at_d], W.at[b, at_d], ags.at[b, 7], agr.at[b, 8], nc)

    def gather_d(b):
        for k, (yy, xx) in enumerate(((by, bx), (by, 1 - bx), (1 - by, bx), (1 - by, 1 - bx))):
            arrive(W.at[b, pl.ds(place(yy, xx, 1 - c), 96)], agr.at[b, 5 + k])

    rank = (0, 2, 0, 2, 0, 1, 2, 3)

    def reduce_1(g):
        send(G.at[g, :, 1 - c], Q0.at[g], rs.at[g, 0], rr.at[g, 0], nc)

    def reduce_2(g):
        arrive(Q0.at[g], rr.at[g, 0])
        for i in range(4):
            Q0[g, i] = (Q0[g, i].astype(F32) + G[g, i, c].astype(F32)).astype(BF16)
        for i in range(2):
            send(Q0.at[g, 2 * i + 1 - bx, 0:48], QX.at[g, i], rs.at[g, 1 + i], rr.at[g, 1 + i], nx)
            send(Q0.at[g, 2 * (1 - by) + i, 48:96], QY.at[g, i], rs.at[g, 3 + i], rr.at[g, 3 + i], ny)

    def reduce_3(g):
        for i in range(2):
            arrive(QX.at[g, i], rr.at[g, 1 + i])
            arrive(QY.at[g, i], rr.at[g, 3 + i])
        T2[g, 0] = (Q0[g, 2 * (1 - by) + bx, 0:48].astype(F32) + QX[g, 1 - by].astype(F32)).astype(BF16)
        T2[g, 1] = (Q0[g, 2 * by + 1 - bx, 48:96].astype(F32) + QY[g, 1 - bx].astype(F32)).astype(BF16)
        send(T2.at[g, 0], Q2.at[g, 0], rs.at[g, 5], rr.at[g, 5], ny)
        send(T2.at[g, 1], Q2.at[g, 1], rs.at[g, 6], rr.at[g, 6], nx)

    def reduce_4(g):
        arrive(Q2.at[g, 0], rr.at[g, 5])
        arrive(Q2.at[g, 1], rr.at[g, 6])
        mine = 2 * by + bx
        first = Q0[g, mine, 0:48].astype(F32) + QX[g, by].astype(F32) + Q2[g, 0].astype(F32)
        second = Q0[g, mine, 48:96].astype(F32) + QY[g, bx].astype(F32) + Q2[g, 1].astype(F32)
        total = jnp.concatenate([first, second], axis=0)
        if rank[g] == 0:
            return total
        U[g] = total.astype(BF16)
        send(U.at[g], ZR.at[g], rs.at[g, 7], rr.at[g, 7], nz[rank[g]])
        return None

    def landed(g):
        arrive(ZR.at[g], rr.at[g, 7])
        return ZR[g].astype(F32)

    ln1_gain, ln1_bias, b_out, ln2_gain, ln2_bias, b_down = (vec_ref[i:i + 1, :] for i in range(6))
    position = lax.broadcasted_iota(jnp.int32, (rows, 1), 0)
    key_mask = (position < len_ref[z]).astype(F32)
    trig = trig_ref[...]
    COS[...] = jnp.concatenate([trig[:, 0:64]] * 6, axis=1)
    SIN[...] = jnp.concatenate([trig[:, 64:128]] * 6, axis=1)
    row_q = lax.broadcasted_iota(jnp.int32, (192, 192), 0)
    col_q = lax.broadcasted_iota(jnp.int32, (192, 192), 1)
    head_mask = jnp.logical_and(row_q < 96, row_q // 32 == col_q // 64)
    row_f = lax.broadcasted_iota(jnp.int32, (384, 192), 0)
    col_f = lax.broadcasted_iota(jnp.int32, (384, 192), 1)
    feat_mask = row_f // 64 == col_f // 32

    X1[...] = jnp.concatenate([x_ref[...].astype(F32), jnp.zeros((rows - live, 768), F32)], axis=0)
    normed, factor = normalize(X1[...])
    N1[...] = normed
    R1[...] = factor
    first = (normed * ln1_gain + ln1_bias).astype(BF16)
    H1[...] = first
    AP[...] = jnp.zeros(AP.shape, BF16)

    def attend(r):
        bias = jnp.concatenate([SP[r, 64 + i:65 + i, :] for i in range(5)], axis=1)[:, 0:576]
        projected = dot_nn(H1[...], W[r, :, 0:576]) + bias
        both = projected[:, 0:384]
        value = projected[:, 384:576].astype(BF16)
        turned = both * COS[...] + swap_halves(both) * SIN[...]
        plain = SP[r, 0:64, :][:, 0:96]
        plain = jnp.concatenate([plain, plain], axis=1)
        block = jnp.where(feat_mask, jnp.concatenate([plain] * 6, axis=0), 0.0)
        f_high, f_low = split(block)
        FH[r] = f_high
        FL[r] = f_low
        t_high, t_low = split(turned)
        u = dot_nn(t_high, f_high) + dot_nn(t_high, f_low) + dot_nn(t_low, f_high)
        decay = jnp.exp(jnp.minimum(u, 0.0))
        EE[r] = decay
        phi32 = jnp.where(u > 0.0, u + 1.0, decay)
        phi = phi32.astype(BF16)
        PHI[r] = phi
        VV[r] = value
        masked = (phi.astype(F32) * key_mask).astype(BF16)
        pad = jnp.zeros((96, 192), F32)
        state = jnp.concatenate([dot_tn(masked, value)[96:192], pad], axis=0)
        total = jnp.concatenate([dot_tn(masked, jnp.ones((rows, 192), BF16))[96:192], pad], axis=0)
        state = jnp.where(head_mask, state, 0.0)
        total = jnp.where(head_mask, total, 0.0)
        ST[r] = state
        TT[r] = total
        s_high, s_low = split(state)
        k_high, k_low = split(total)
        numer = dot_nn(phi, s_high) + dot_nn(phi, s_low)
        inverse = 1.0 / (dot_nn(phi, k_high) + dot_nn(phi, k_low))
        attended = numer * inverse
        ATT[r] = attended
        INV[r] = inverse
        AP[r, :, 64:256] = attended.astype(BF16)
        X1[...] += dot_nt(AP[r], W[r, :, 512:768])

    gather_a(1)
    attend(0)
    gather_b(1)
    gather_a(2)
    gather_c(1)
    gather_b(2)
    gather_a(3)
    gather_d(1)
    arrive(SP.at[1], zr.at[9])
    attend(1)
    gather_c(2)
    gather_b(3)
    gather_a(6)
    gather_d(2)
    arrive(SP.at[2], zr.at[10])
    attend(2)
    gather_c(3)
    gather_b(6)
    gather_a(7)
    gather_d(3)
    arrive(SP.at[3], zr.at[11])
    attend(3)

    middle = X1[...] + b_out
    X1[...] = middle
    normed, factor = normalize(middle)
    N2[...] = normed
    R2[...] = factor
    second = (normed * ln2_gain + ln2_bias).astype(BF16)
    H2[0:rows, :] = second
    send(H2.at[0:rows], H2.at[rows:2 * rows], xs.at[1], xr.at[1], nz[1])

    gather_c(6)
    gather_b(7)
    gather_d(6)
    up_copy.wait()
    down_copy.wait()
    arrive(CC.at[rows:2 * rows], xr.at[0])
    up = (4, 6)
    down = (5, 7)
    DA[0] = dot_nt(CC[...], W[5])
    gather_c(7)

    def feed(q, s):
        part = pl.ds(s * rows, rows)
        bias = jnp.concatenate([SP[2 * q, 72 + i:73 + i, :] for i in range(6)], axis=1)
        pre = dot_nn(H2[part], W[up[q]]) + bias
        half = 0.5 * (1.0 + lax.erf(pre * (0.5 ** 0.5)))
        ACT[q, part] = (pre * half).astype(BF16)
        slope = half + pre * jnp.exp(-0.5 * pre * pre) * (0.5 / np.pi) ** 0.5
        DPRE[q, part] = (DA[q, part] * slope).astype(BF16)

    feed(0, 0)
    gather_d(7)
    DA[1] = dot_nt(CC[...], W[7])
    feed(1, 0)
    CT[...] = CC[...].T
    H1T[...] = H1[...].T
    arrive(H2.at[rows:2 * rows], xr.at[1])
    feed(0, 1)
    feed(1, 1)
    theirs = pl.ds(rows, rows)
    mine = pl.ds(0, rows)
    HS[...] = (dot_nt(DPRE[0, theirs], W[4]) + dot_nt(DPRE[1, theirs], W[6])).astype(BF16)
    send(HS, HR, xs.at[2], xr.at[2], nz[1])

    def store_block(g, left, right):
        for n in range(3):
            cols = slice(n * 256, n * 256 + 256)
            G[g, :, :, :, cols] = dot_nn(left, right[:, cols]).astype(BF16).reshape(4, 2, 96, 256)

    store_block(0, CT[...], ACT[0])
    reduce_1(0)
    store_block(1, CT[...], ACT[1])
    reduce_1(1)
    reduce_2(0)
    H2T[...] = H2[...].T
    store_block(2, H2T[...], DPRE[0])
    reduce_1(2)
    reduce_2(1)
    store_block(3, H2T[...], DPRE[1])
    reduce_1(3)
    reduce_2(2)
    OS[...] = (dot_nn(ACT[0, theirs], W[5]) + dot_nn(ACT[1, theirs], W[7])).astype(BF16)
    SV[...] = jnp.zeros(SV.shape, F32)
    for q in range(2):
        SV[10 + q:11 + q, :] = column_sum(DPRE[q].astype(F32))
    own_back = dot_nt(DPRE[0, mine], W[4]) + dot_nt(DPRE[1, mine], W[6])
    reduce_2(3)

    arrive(HR, xr.at[2])
    send(OS, OR, xs.at[3], xr.at[3], nz[1])
    own_back = own_back + HR[...].astype(F32)
    cot = CC[mine].astype(F32)
    SV[3:4, :] = column_sum(own_back * N2[...])
    SV[4:5, :] = column_sum(own_back)
    SV[5:6, :] = column_sum(cot)
    dx1 = cot + norm_back(own_back, ln2_gain, N2[...], R2[...])
    DX1[...] = dx1
    branch = dx1.astype(BF16)
    GO[...] = branch
    SV[2:3, :] = column_sum(branch.astype(F32))
    reduce_3(0)
    GOT[...] = GO[...].T
    DH1[...] = jnp.zeros(DH1.shape, F32)

    def attend_back(r):
        da = dot_nn(GO[...], W[r, :, 512:768])[:, 64:256]
        phi = PHI[r]
        dnum = da * INV[r]
        drest = -(dnum * ATT[r])
        n_high, n_low = split(dnum)
        d_high, d_low = split(drest)
        s_high, s_low = split(ST[r])
        k_high, k_low = split(TT[r])
        dphi = dot_nt(n_high, s_high) + dot_nt(n_high, s_low) + dot_nt(n_low, s_high)
        dphi += dot_nt(d_high, k_high) + dot_nt(d_high, k_low) + dot_nt(d_low, k_high)
        pad = jnp.zeros((96, 192), F32)
        dstate = jnp.where(head_mask, dot_tn(phi, n_high) + dot_tn(phi, n_low), 0.0)
        dtotal = jnp.where(head_mask, dot_tn(phi, d_high) + dot_tn(phi, d_low), 0.0)
        a_high, a_low = split(jnp.concatenate([pad, dstate[0:96]], axis=0))
        b_high, b_low = split(jnp.concatenate([pad, dtotal[0:96]], axis=0))
        ones = jnp.ones((16, 192), BF16)
        dkey = dot_nt(VV[r], a_high) + dot_nt(VV[r], a_low)
        dkey += (dot_nt(ones, b_high) + dot_nt(ones, b_low))[0:1, :]
        dphi += key_mask * dkey
        dvalue = key_mask * (dot_nn(phi, a_high) + dot_nn(phi, a_low))
        u_high, u_low = split(dphi * EE[r])
        back = dot_nt(u_high, FH[r]) + dot_nt(u_high, FL[r]) + dot_nt(u_low, FH[r])
        back = back * COS[...] - swap_halves(back) * SIN[...]
        DQ[:, 0:384] = back.astype(BF16)
        DQ[:, 384:576] = dvalue.astype(BF16)
        SV[6 + r:7 + r, 0:576] = column_sum(DQ[...].astype(F32))
        DH1[...] += dot_nt(DQ[...], W[r, :, 0:576])

    def store_attention(r):
        g = 4 + r
        for n in range(2):
            cols = slice(n * 256, n * 256 + 256)
            G[g, :, :, :, cols] = dot_nn(H1T[...], DQ[:, cols]).astype(BF16).reshape(4, 2, 96, 256)
        edge = jnp.concatenate(
            [dot_nn(H1T[...], DQ[:, 512:576]), dot_nn(GOT[...], AP[r, :, 64:256])], axis=1)
        G[g, :, :, :, 512:768] = edge.astype(BF16).reshape(4, 2, 96, 256)

    attend_back(3)
    store_attention(3)
    reduce_1(7)
    reduce_3(1)
    down_own = reduce_4(0)
    attend_back(2)
    store_attention(2)
    reduce_1(6)
    reduce_2(7)
    reduce_3(2)
    reduce_4(1)
    attend_back(1)
    store_attention(1)
    reduce_1(5)
    reduce_2(6)
    reduce_3(3)
    up_own = reduce_4(2)
    attend_back(0)
    store_attention(0)
    reduce_1(4)
    reduce_2(5)
    reduce_4(3)
    reduce_3(7)

    first_back = DH1[...]
    SV[0:1, :] = column_sum(first_back * N1[...])
    SV[1:2, :] = column_sum(first_back)
    send(SV, AR.at[0], vs.at[0], vr.at[0], nc)
    gx_ref[...] = (DX1[...] + norm_back(first_back, ln1_gain, N1[...], R1[...]))[0:live]
    reduce_2(4)
    arrive(AR.at[0], vr.at[0])
    AR[1] = SV[...] + AR[0]
    send(AR.at[1], AR.at[2], vs.at[1], vr.at[1], nx)
    reduce_4(7)
    reduce_3(6)
    gd_ref[...] = down_own + landed(1)
    gu_ref[...] = up_own + landed(3)

    output = dot_nn(ACT[0, mine], W[5]) + dot_nn(ACT[1, mine], W[7])
    arrive(OR, xr.at[3])
    output = X1[...] + output + OR[...].astype(F32) + b_down
    y_ref[...] = output[0:live].astype(BF16)

    arrive(AR.at[2], vr.at[1])
    AR[3] = AR[1] + AR[2]
    send(AR.at[3], AR.at[4], vs.at[2], vr.at[2], ny)
    reduce_3(5)
    reduce_4(6)
    arrive(AR.at[4], vr.at[2])
    AR[5] = AR[3] + AR[4]
    for r in (1, 2, 3):
        send(AR.at[5], AR.at[5 + r], vs.at[2 + r], vr.at[2 + r], nz[r])
    reduce_3(4)
    reduce_4(5)
    block = reduce_4(4)
    for r in (1, 2, 3):
        arrive(AR.at[5 + r], vr.at[2 + r])
    sv_ref[0:6, :] = AR[5, 0:6, :] + AR[6, 0:6, :] + AR[7, 0:6, :] + AR[8, 0:6, :]
    sv_ref[6:7, :] = AR[5, 10:11, :] + AR[7, 11:12, :]
    bias = AR[5, 6:7, :] + AR[6, 7:8, :] + AR[7, 8:9, :] + AR[8, 9:10, :]
    bias = [bias[:, s * 192 + h * 64:s * 192 + h * 64 + 64] for h in range(3) for s in range(3)]
    sv_ref[7:8, :] = jnp.concatenate(bias + [jnp.zeros((1, 192), F32)], axis=1)
    for r in (1, 2, 3):
        block = block + landed(4 + r)
    gq_ref[...] = jnp.concatenate(
        [block[:, s * 192 + h * 64:s * 192 + h * 64 + 64] for h in range(3) for s in range(3)], axis=1)
    go_ref[...] = block[:, 576:768]
    for copy in sends:
        copy.wait_send()


def trig_table(live, rows, head_dim):
    half = head_dim // 2
    freq = (10000.0 ** (-np.arange(half, dtype=np.float32) * 2.0 / head_dim)).astype(np.float32)
    angle = (np.arange(rows, dtype=np.float32)[:, None] * freq[None, :]).astype(np.float64)
    cosine, sine = np.cos(angle), np.sin(angle)
    table = np.concatenate([cosine, cosine, -sine, sine], axis=1) * head_dim ** (-0.25)
    return table.astype(np.float32)


def local(
    n_dp, layer_input, lengths, ln1_gain, ln1_bias, w_qkv, b_qkv, features, w_out, b_out,
    ln2_gain, ln2_bias, w_up, b_up, w_down, b_down, cotangent,
):
    live, width = layer_input.shape
    rows = -(-live // 16) * 16
    vectors = jnp.stack([
        ln1_gain, ln1_bias, b_out, ln2_gain, ln2_bias, b_down, b_up,
        jnp.pad(b_qkv, (0, width - b_qkv.shape[0])),
    ])
    trig = jnp.asarray(trig_table(live, rows, features.shape[1]))
    vmem = pl.BlockSpec(memory_space=pltpu.VMEM)
    smem = pl.BlockSpec(memory_space=pltpu.SMEM)
    anywhere = pl.BlockSpec(memory_space=pl.ANY)
    dma = pltpu.SemaphoreType.DMA

    def buf(*shape):
        return pltpu.VMEM(shape, BF16)

    def wide(*shape):
        return pltpu.VMEM(shape, F32)

    outs = pl.pallas_call(
        functools.partial(layer_kernel, live),
        out_shape=[
            jax.ShapeDtypeStruct((live, width), BF16),
            jax.ShapeDtypeStruct((live, width), F32),
            jax.ShapeDtypeStruct((96, 576), F32),
            jax.ShapeDtypeStruct((96, 192), F32),
            jax.ShapeDtypeStruct((96, 768), F32),
            jax.ShapeDtypeStruct((96, 768), F32),
            jax.ShapeDtypeStruct((8, 768), F32),
        ],
        in_specs=[vmem, vmem, smem] + [vmem] * 5 + [anywhere] * 2,
        out_specs=[vmem] * 7,
        scratch_shapes=[
            buf(8, 768, 768), wide(4, 80, 128), buf(2 * rows, 768), buf(2 * rows, 768),
            buf(768, 2 * rows), buf(768, 2 * rows), buf(rows, 768), buf(768, rows),
            buf(rows, 768), buf(768, rows), wide(rows, 768), wide(rows, 1), wide(rows, 768),
            wide(rows, 768), wide(rows, 1), wide(rows, 768), wide(rows, 768),
            wide(rows, 384), wide(rows, 384), buf(4, 384, 192), buf(4, 384, 192),
            buf(4, rows, 192), wide(4, rows, 192), buf(4, rows, 192), wide(4, rows, 192),
            wide(4, rows, 192), buf(4, rows, 256), wide(4, 192, 192), wide(4, 192, 192),
            wide(2, 2 * rows, 768), buf(2, 2 * rows, 768), buf(2, 2 * rows, 768), buf(rows, 576),
            buf(rows, 768), buf(rows, 768), buf(rows, 768), buf(rows, 768),
            buf(8, 4, 2, 96, 768), buf(8, 4, 96, 768), buf(8, 2, 48, 768), buf(8, 2, 48, 768),
            buf(8, 2, 48, 768), buf(8, 2, 48, 768), buf(8, 96, 768), buf(8, 96, 768),
            wide(9, 16, 768), wide(16, 768),
            dma((2,)), dma((12,)), dma((12,)), dma((8, 8)), dma((8, 9)), dma((4,)), dma((4,)),
            dma((8, 8)), dma((8, 8)), dma((6,)), dma((6,)),
        ],
        compiler_params=pltpu.CompilerParams(
            collective_id=0, has_side_effects=True, vmem_limit_bytes=67043328),
    )(layer_input, cotangent, lengths, vectors, features, trig, w_qkv, w_out, w_up, w_down)
    output, grad_x, qkv_piece, out_piece, up_piece, down_piece, small = outs
    common, up_bias, qkv_bias = small[0:6], small[6], small[7, 0:576]
    out_piece, down_piece = out_piece.T, down_piece.T
    if n_dp != GROUP:
        member = lax.axis_index("dp") % GROUP

        def spread(piece, axis):
            shape = list(piece.shape)
            shape[axis] = shape[axis] * GROUP
            start = [0, 0]
            start[axis] = member * piece.shape[axis]
            whole = lax.dynamic_update_slice(jnp.zeros(shape, F32), piece, start)
            return lax.psum_scatter(whole, "dp", scatter_dimension=axis, tiled=True)

        qkv_piece, out_piece = spread(qkv_piece, 0), spread(out_piece, 1)
        up_piece, down_piece = spread(up_piece, 0), spread(down_piece, 1)
        common, up_bias, qkv_bias = jax.tree.map(
            lambda part: lax.psum(part, "dp") / GROUP, (common, up_bias, qkv_bias))
    return (
        output, grad_x, common[0], common[1], qkv_piece, qkv_bias, out_piece, common[2],
        common[3], common[4], up_piece, up_bias, down_piece, common[5],
    )


def solution(mesh):
    rows, cols = P(("dp", "mp"), None), P(None, "mp")
    placed = (
        rows, P("dp"), P(), P(), cols, P("mp"), P("mp", None, None), P("mp", None), P(),
        P(), P(), cols, P("mp"), P("mp", None), P(), rows,
    )
    return jax.shard_map(
        functools.partial(local, mesh.shape["dp"]),
        mesh=mesh,
        in_specs=placed,
        out_specs=(
            rows, rows, P(), P(), P("dp", "mp"), P("mp"), P("mp", "dp"), P(),
            P(), P(), P("dp", "mp"), P("mp"), P("mp", "dp"), P(),
        ),
        check_vma=False,
    )
```

```python
import functools

import jax
import jax.numpy as jnp
import numpy as np
from jax import lax
from jax.experimental import pallas as pl
from jax.experimental.pallas import tpu as pltpu
from jax.sharding import PartitionSpec as P

MESH = pl.DeviceIdType.MESH
BF16 = jnp.bfloat16
F32 = jnp.float32
EPSILON = 1e-05
GROUP = 8


def dot_nn(left, right):
    return lax.dot_general(left, right, (((1,), (0,)), ((), ())), preferred_element_type=F32)


def dot_nt(left, right):
    return lax.dot_general(left, right, (((1,), (1,)), ((), ())), preferred_element_type=F32)


def dot_tn(left, right):
    return lax.dot_general(left, right, (((0,), (0,)), ((), ())), preferred_element_type=F32)


def split(values):
    high = values.astype(BF16)
    return high, (values - high.astype(F32)).astype(BF16)


def normalize(values):
    centred = values - jnp.mean(values, axis=-1, keepdims=True)
    factor = lax.rsqrt(jnp.mean(centred * centred, axis=-1, keepdims=True) + EPSILON)
    return centred * factor, factor


def norm_back(grad, gain, normed, factor):
    hat = grad * gain
    return factor * (
        hat
        - jnp.mean(hat, axis=-1, keepdims=True)
        - normed * jnp.mean(hat * normed, axis=-1, keepdims=True)
    )


def column_sum(values):
    return jnp.sum(values, axis=0, keepdims=True)


def swap_halves(values):
    width = values.shape[1]
    lane = lax.broadcasted_iota(jnp.int32, values.shape, 1)
    return jnp.where(lane % 64 < 32, pltpu.roll(values, width - 32, 1), pltpu.roll(values, 32, 1))


def layer_kernel(live, *refs):
    (
        x_ref, c_ref, len_ref, ln1_gain_ref, ln1_bias_ref, b_out_ref, ln2_gain_ref, ln2_bias_ref,
        b_down_ref, b_up_ref, b_qkv_ref, feat_ref, trig_ref, wqkv_ref, wout_ref, wup_ref, wdown_ref,
        y_ref, gx_ref, gq_ref, go_ref, gu_ref, gd_ref, sv_ref,
        W, SP, CC, H2, CT, H2T, H1, H1T, GO, GOT, N1, R1, X1, N2, R2, DX1, DH1,
        COS, SIN, FH, FL, PHI, EE, VV, ATT, INV, AB, ST, TT, DA, ACT, DPRE, DQ,
        OS, OR, HS, HR, G, Q0, QX, QY, T2, Q2, U, ZR, EV, LV,
        local_sem, zs, zr, ags, agr, xs, xr, rs, rr, vs, vr,
    ) = refs
    rows = CC.shape[0] // 2
    dp = lax.axis_index("dp")
    z = lax.axis_index("mp")
    member = dp % GROUP
    c = member % 2
    bx = (member // 2) % 2
    by = member // 4
    nx = (dp + 2 - 4 * bx, z)
    ny = (dp + 4 - 8 * by, z)
    nc = (dp + 1 - 2 * c, z)
    nz = (None, (dp, z + 1 - 2 * (z % 2)), (dp, (z + 2) % 4), (dp, 3 - z))

    def place(yy, xx, cc):
        return pl.multiple_of((yy * 4 + xx * 2 + cc) * 96, 96)

    sends = []

    def send(src, dst, send_sem, recv_sem, device):
        copy = pltpu.make_async_remote_copy(
            src_ref=src, dst_ref=dst, send_sem=send_sem, recv_sem=recv_sem,
            device_id=device, device_id_type=MESH,
        )
        copy.start()
        sends.append(copy)

    def arrive(dst, recv_sem):
        pltpu.make_async_remote_copy(
            src_ref=dst, dst_ref=dst, send_sem=recv_sem, recv_sem=recv_sem,
            device_id=nc, device_id_type=MESH,
        ).wait_recv()

    barrier = pltpu.get_barrier_semaphore()
    for device in (nx, ny, nc, nz[1], nz[2], nz[3]):
        pl.semaphore_signal(barrier, inc=1, device_id=device, device_id_type=MESH)

    loads = [
        pltpu.make_async_copy(source, target, local_sem.at[i])
        for i, (source, target) in enumerate((
            (wqkv_ref, W.at[0, 0:576]), (wout_ref, W.at[0, 576:768]),
            (wup_ref, W.at[4]), (wdown_ref, W.at[5])))
    ]
    for load in loads:
        load.start()

    SP[0, 0:64, 0:96] = feat_ref[...].reshape(96, 64).T
    qkv_bias = b_qkv_ref[...].reshape(1, 576)
    qkv_bias = jnp.concatenate(
        [qkv_bias[:, h * 192 + s * 64:h * 192 + s * 64 + 64] for s in range(3) for h in range(3)]
        + [jnp.zeros((1, 64), F32)], axis=1)
    for i in range(5):
        SP[0, 64 + i:65 + i, :] = qkv_bias[:, i * 128:i * 128 + 128]
    up_bias = b_up_ref[...].reshape(1, 768)
    for i in range(6):
        SP[0, 72 + i:73 + i, :] = up_bias[:, i * 128:i * 128 + 128]
    CC[0:rows, :] = jnp.concatenate([c_ref[...].astype(F32), jnp.zeros((rows - live, 768), F32)], axis=0).astype(BF16)

    pl.semaphore_wait(barrier, 6)

    own = pl.ds(place(by, bx, c), 96)
    inner = jnp.logical_or(z == 1, z == 2)
    second_rank = jnp.where(inner, 3, 2)
    third_rank = jnp.where(inner, 2, 3)

    def send_if(condition, src, dst, send_sem, recv_sem, device):
        copy = pltpu.make_async_remote_copy(
            src_ref=src, dst_ref=dst, send_sem=send_sem, recv_sem=recv_sem,
            device_id=device, device_id_type=MESH,
        )

        @pl.when(condition)
        def _():
            copy.start()

        late_sends.append((condition, copy))

    late_sends = []
    in_qkv = member < 6
    out_rows = pl.ds(pl.multiple_of(jnp.maximum(own.start - 576, 0), 96), 96)
    qkv_rows = pl.ds(pl.multiple_of(jnp.minimum(own.start, 480), 96), 96)
    for r, condition in ((1, None), (3, inner)):
        for part, source in ((in_qkv, wqkv_ref.at[qkv_rows]), (jnp.logical_not(in_qkv), wout_ref.at[out_rows])):
            both = part if condition is None else jnp.logical_and(part, condition)
            send_if(both, source, W.at[r, own], zs.at[r], agr.at[r, 0], nz[r])
    half = pl.ds(pl.multiple_of(c * 40, 8), 40)
    other_half = pl.ds(pl.multiple_of((1 - c) * 40, 8), 40)
    for r in (1, 2, 3):
        send(SP.at[0, half], SP.at[r, half], zs.at[8 + r], zr.at[r], nz[r])

    def forward(b, to_rank, slot):
        send_if(inner, W.at[b, own], W.at[slot, own], zs.at[3 + slot + to_rank], agr.at[slot, 0], nz[to_rank])

    at_x = pl.ds(place(by, 1 - bx, c), 96)
    at_y = pl.ds(place(1 - by, bx, c), 96)
    at_d = pl.ds(place(1 - by, 1 - bx, c), 96)
    at_x0 = pl.ds(place(by, 1 - bx, c), 48)
    at_y1 = pl.ds(pl.multiple_of(place(1 - by, bx, c) + 48, 48), 48)
    at_d0 = pl.ds(place(1 - by, 1 - bx, c), 48)
    at_d1 = pl.ds(pl.multiple_of(place(1 - by, 1 - bx, c) + 48, 48), 48)

    def gather_a(b):
        arrive(W.at[b, own], agr.at[b, 0])
        send(W.at[b, own], W.at[b, own], ags.at[b, 0], agr.at[b, 1], nx)
        send(W.at[b, own], W.at[b, own], ags.at[b, 1], agr.at[b, 2], ny)
        send(W.at[b, own], W.at[b, own], ags.at[b, 2], agr.at[b, 5], nc)

    def gather_b(b):
        arrive(W.at[b, at_x], agr.at[b, 1])
        send(W.at[b, at_x0], W.at[b, at_x0], ags.at[b, 3], agr.at[b, 3], ny)
        send(W.at[b, at_x], W.at[b, at_x], ags.at[b, 4], agr.at[b, 6], nc)
        arrive(W.at[b, at_y], agr.at[b, 2])
        send(W.at[b, at_y1], W.at[b, at_y1], ags.at[b, 5], agr.at[b, 4], nx)
        send(W.at[b, at_y], W.at[b, at_y], ags.at[b, 6], agr.at[b, 7], nc)

    def gather_c(b):
        arrive(W.at[b, at_d0], agr.at[b, 3])
        arrive(W.at[b, at_d1], agr.at[b, 4])
        send(W.at[b, at_d], W.at[b, at_d], ags.at[b, 7], agr.at[b, 8], nc)

    def gather_small(r):
        arrive(SP.at[r, half], zr.at[r])
        send(SP.at[r, half], SP.at[r, half], zs.at[12 + r], zr.at[4 + r], nc)

    def small_done(r):
        arrive(SP.at[r, other_half], zr.at[4 + r])

    def qkv_rows_of(r):
        return jnp.concatenate(
            [W[r, h * 192 + s * 64:h * 192 + s * 64 + 64, :] for s in range(3) for h in range(3)], axis=0)

    def gather_d(b):
        for k, (yy, xx) in enumerate(((by, bx), (by, 1 - bx), (1 - by, bx), (1 - by, 1 - bx))):
            arrive(W.at[b, pl.ds(place(yy, xx, 1 - c), 96)], agr.at[b, 5 + k])

    rank = (0, 2, 0, 2, 0, 1, 2, 3)

    def reduce_1(g):
        send(G.at[g, :, 1 - c], Q0.at[g], rs.at[g, 0], rr.at[g, 0], nc)

    def reduce_2(g):
        arrive(Q0.at[g], rr.at[g, 0])
        for i in range(4):
            Q0[g, i] = (Q0[g, i].astype(F32) + G[g, i, c].astype(F32)).astype(BF16)
        for i in range(2):
            send(Q0.at[g, 2 * i + 1 - bx, 0:48], QX.at[g, i], rs.at[g, 1 + i], rr.at[g, 1 + i], nx)
            send(Q0.at[g, 2 * (1 - by) + i, 48:96], QY.at[g, i], rs.at[g, 3 + i], rr.at[g, 3 + i], ny)

    def reduce_3(g):
        for i in range(2):
            arrive(QX.at[g, i], rr.at[g, 1 + i])
            arrive(QY.at[g, i], rr.at[g, 3 + i])
        T2[g, 0] = (Q0[g, 2 * (1 - by) + bx, 0:48].astype(F32) + QX[g, 1 - by].astype(F32)).astype(BF16)
        T2[g, 1] = (Q0[g, 2 * by + 1 - bx, 48:96].astype(F32) + QY[g, 1 - bx].astype(F32)).astype(BF16)
        send(T2.at[g, 0], Q2.at[g, 0], rs.at[g, 5], rr.at[g, 5], ny)
        send(T2.at[g, 1], Q2.at[g, 1], rs.at[g, 6], rr.at[g, 6], nx)

    def reduce_4(g):
        arrive(Q2.at[g, 0], rr.at[g, 5])
        arrive(Q2.at[g, 1], rr.at[g, 6])
        mine = 2 * by + bx
        first = Q0[g, mine, 0:48].astype(F32) + QX[g, by].astype(F32) + Q2[g, 0].astype(F32)
        second = Q0[g, mine, 48:96].astype(F32) + QY[g, bx].astype(F32) + Q2[g, 1].astype(F32)
        total = jnp.concatenate([first, second], axis=0)
        if rank[g] == 0:
            return total
        U[g] = total.astype(BF16)
        send(U.at[g], ZR.at[g], rs.at[g, 7], rr.at[g, 7], nz[rank[g]])
        return None

    def landed(g):
        arrive(ZR.at[g], rr.at[g, 7])
        return ZR[g].astype(F32)

    ln1_gain, ln1_bias, b_out, ln2_gain, ln2_bias, b_down = (
        ref[...].reshape(1, 768)
        for ref in (ln1_gain_ref, ln1_bias_ref, b_out_ref, ln2_gain_ref, ln2_bias_ref, b_down_ref))
    position = lax.broadcasted_iota(jnp.int32, (rows, 1), 0)
    key_mask = (position < len_ref[z]).astype(F32)
    trig = trig_ref[...]
    COS[...] = jnp.concatenate([trig[:, 0:64]] * 6, axis=1)
    SIN[...] = jnp.concatenate([trig[:, 64:128]] * 6, axis=1)
    row_q = lax.broadcasted_iota(jnp.int32, (192, 192), 0)
    col_q = lax.broadcasted_iota(jnp.int32, (192, 192), 1)
    head_mask = jnp.logical_and(row_q < 96, row_q // 32 == col_q // 64)
    row_f = lax.broadcasted_iota(jnp.int32, (384, 192), 0)
    col_f = lax.broadcasted_iota(jnp.int32, (384, 192), 1)
    feat_mask = row_f // 64 == col_f // 32

    X1[...] = jnp.concatenate([x_ref[...].astype(F32), jnp.zeros((rows - live, 768), F32)], axis=0)
    normed, factor = normalize(X1[...])
    N1[...] = normed
    R1[...] = factor
    first = (normed * ln1_gain + ln1_bias).astype(BF16)
    H1[...] = first

    def attend(r):
        bias = jnp.concatenate([SP[r, 64 + i:65 + i, :] for i in range(5)], axis=1)[:, 0:576]
        projected = dot_nt(H1[...], qkv_rows_of(r)) + bias
        both = projected[:, 0:384]
        value = projected[:, 384:576].astype(BF16)
        turned = both * COS[...] + swap_halves(both) * SIN[...]
        plain = SP[r, 0:64, :][:, 0:96]
        plain = jnp.concatenate([plain, plain], axis=1)
        block = jnp.where(feat_mask, jnp.concatenate([plain] * 6, axis=0), 0.0)
        f_high, f_low = split(block)
        FH[r] = f_high
        FL[r] = f_low
        t_high, t_low = split(turned)
        u = dot_nn(t_high, f_high) + dot_nn(t_high, f_low) + dot_nn(t_low, f_high)
        decay = jnp.exp(jnp.minimum(u, 0.0))
        EE[r] = decay
        phi32 = jnp.where(u > 0.0, u + 1.0, decay)
        phi = phi32.astype(BF16)
        PHI[r] = phi
        VV[r] = value
        masked = (phi.astype(F32) * key_mask).astype(BF16)
        pad = jnp.zeros((96, 192), F32)
        state = jnp.concatenate([dot_tn(masked, value)[96:192], pad], axis=0)
        total = jnp.concatenate([dot_tn(masked, jnp.ones((rows, 192), BF16))[96:192], pad], axis=0)
        state = jnp.where(head_mask, state, 0.0)
        total = jnp.where(head_mask, total, 0.0)
        ST[r] = state
        TT[r] = total
        s_high, s_low = split(state)
        k_high, k_low = split(total)
        numer = dot_nn(phi, s_high) + dot_nn(phi, s_low)
        inverse = 1.0 / (dot_nn(phi, k_high) + dot_nn(phi, k_low))
        attended = numer * inverse
        ATT[r] = attended
        INV[r] = inverse
        mixed = attended.astype(BF16)
        AB[r] = mixed
        X1[...] += dot_nn(mixed, W[r, 576:768, :])

    gather_a(1)
    forward(1, 3, 2)
    for load in loads:
        load.wait()
    attend(0)
    gather_a(second_rank)
    forward(3, 1, 2)
    send(wup_ref.at[own], W.at[6, own], zs.at[2], agr.at[6, 0], nz[2])
    for r in (1, 2, 3):
        gather_small(r)
    gather_b(1)
    gather_c(1)
    gather_a(third_rank)
    forward(2, 1, 3)
    send(wdown_ref.at[own], W.at[7, own], zs.at[0], agr.at[7, 0], nz[2])
    send(CC.at[0:rows], CC.at[rows:2 * rows], xs.at[0], xr.at[0], nz[1])
    for r in (1, 2, 3):
        small_done(r)
    gather_d(1)
    attend(1)
    gather_b(second_rank)
    gather_c(second_rank)
    gather_a(6)
    gather_d(second_rank)
    attend(second_rank)
    gather_b(third_rank)
    gather_a(7)
    gather_c(third_rank)
    gather_d(third_rank)
    attend(third_rank)

    middle = X1[...] + b_out
    X1[...] = middle
    normed, factor = normalize(middle)
    N2[...] = normed
    R2[...] = factor
    second = (normed * ln2_gain + ln2_bias).astype(BF16)
    H2[0:rows, :] = second
    send(H2.at[0:rows], H2.at[rows:2 * rows], xs.at[1], xr.at[1], nz[1])

    gather_b(6)
    gather_c(6)
    gather_b(7)
    gather_d(6)
    arrive(CC.at[rows:2 * rows], xr.at[0])
    up = (4, 6)
    down = (5, 7)
    DA[0] = dot_nt(CC[...], W[5])
    gather_c(7)

    def feed(q, s):
        part = pl.ds(s * rows, rows)
        bias = jnp.concatenate([SP[2 * q, 72 + i:73 + i, :] for i in range(6)], axis=1)
        pre = dot_nn(H2[part], W[up[q]]) + bias
        half = 0.5 * (1.0 + lax.erf(pre * (0.5 ** 0.5)))
        ACT[q, part] = (pre * half).astype(BF16)
        slope = half + pre * jnp.exp(-0.5 * pre * pre) * (0.5 / np.pi) ** 0.5
        DPRE[q, part] = (DA[q, part] * slope).astype(BF16)

    feed(0, 0)
    gather_d(7)
    DA[1] = dot_nt(CC[...], W[7])
    feed(1, 0)
    CT[...] = CC[...].T
    H1T[...] = H1[...].T
    arrive(H2.at[rows:2 * rows], xr.at[1])
    theirs = pl.ds(rows, rows)
    mine = pl.ds(0, rows)

    def store_block(g, left, right):
        for n in range(3):
            cols = slice(n * 256, n * 256 + 256)
            G[g, :, :, :, cols] = dot_nn(left, right[:, cols]).astype(BF16).reshape(4, 2, 96, 256)

    feed(0, 1)
    store_block(0, CT[...], ACT[0])
    reduce_1(0)
    feed(1, 1)
    HS[...] = (dot_nt(DPRE[0, theirs], W[4]) + dot_nt(DPRE[1, theirs], W[6])).astype(BF16)
    send(HS, HR, xs.at[2], xr.at[2], nz[1])

    store_block(1, CT[...], ACT[1])
    reduce_1(1)
    reduce_2(0)
    H2T[...] = H2[...].T
    store_block(2, H2T[...], DPRE[0])
    reduce_1(2)
    reduce_2(1)
    store_block(3, H2T[...], DPRE[1])
    reduce_1(3)
    reduce_2(2)
    OS[...] = (dot_nn(ACT[0, theirs], W[5]) + dot_nn(ACT[1, theirs], W[7])).astype(BF16)
    for q in range(2):
        EV[0, 4 + q:5 + q, :] = column_sum(DPRE[q].astype(F32))
    own_back = dot_nt(DPRE[0, mine], W[4]) + dot_nt(DPRE[1, mine], W[6])
    reduce_2(3)

    arrive(HR, xr.at[2])
    send(OS, OR, xs.at[3], xr.at[3], nz[1])
    own_back = own_back + HR[...].astype(F32)
    cot = CC[mine].astype(F32)
    EV[0, 1:2, :] = column_sum(own_back * N2[...])
    EV[0, 2:3, :] = column_sum(own_back)
    EV[0, 3:4, :] = column_sum(cot)
    dx1 = cot + norm_back(own_back, ln2_gain, N2[...], R2[...])
    DX1[...] = dx1
    branch = dx1.astype(BF16)
    GO[...] = branch
    EV[0, 0:1, :] = column_sum(branch.astype(F32))
    reduce_3(0)
    GOT[...] = GO[...].T
    DH1[...] = jnp.zeros(DH1.shape, F32)

    def attend_back(r):
        da = dot_nt(GO[...], W[r, 576:768, :])
        phi = PHI[r]
        dnum = da * INV[r]
        drest = -(dnum * ATT[r])
        n_high, n_low = split(dnum)
        d_high, d_low = split(drest)
        s_high, s_low = split(ST[r])
        k_high, k_low = split(TT[r])
        dphi = dot_nt(n_high, s_high) + dot_nt(n_high, s_low) + dot_nt(n_low, s_high)
        dphi += dot_nt(d_high, k_high) + dot_nt(d_high, k_low) + dot_nt(d_low, k_high)
        pad = jnp.zeros((96, 192), F32)
        dstate = jnp.where(head_mask, dot_tn(phi, n_high) + dot_tn(phi, n_low), 0.0)
        dtotal = jnp.where(head_mask, dot_tn(phi, d_high) + dot_tn(phi, d_low), 0.0)
        a_high, a_low = split(jnp.concatenate([pad, dstate[0:96]], axis=0))
        b_high, b_low = split(jnp.concatenate([pad, dtotal[0:96]], axis=0))
        ones = jnp.ones((16, 192), BF16)
        dkey = dot_nt(VV[r], a_high) + dot_nt(VV[r], a_low)
        dkey += (dot_nt(ones, b_high) + dot_nt(ones, b_low))[0:1, :]
        dphi += key_mask * dkey
        dvalue = key_mask * (dot_nn(phi, a_high) + dot_nn(phi, a_low))
        u_high, u_low = split(dphi * EE[r])
        back = dot_nt(u_high, FH[r]) + dot_nt(u_high, FL[r]) + dot_nt(u_low, FH[r])
        back = back * COS[...] - swap_halves(back) * SIN[...]
        DQ[:, 0:384] = back.astype(BF16)
        DQ[:, 384:576] = dvalue.astype(BF16)
        bias_sum = jnp.concatenate([column_sum(DQ[...].astype(F32)), jnp.zeros((1, 192), F32)], axis=1)
        if r == 0:
            LV[0, 2:3, :] = bias_sum
        else:
            EV[0, 5 + r:6 + r, :] = bias_sum
        DH1[...] += dot_nn(DQ[...], qkv_rows_of(r))

    def store_attention(r):
        g = 4 + r
        for n in range(2):
            cols = slice(n * 256, n * 256 + 256)
            G[g, :, :, :, cols] = dot_nn(H1T[...], DQ[:, cols]).astype(BF16).reshape(4, 2, 96, 256)
        edge = jnp.concatenate(
            [dot_nn(H1T[...], DQ[:, 512:576]), dot_nn(GOT[...], AB[r])], axis=1)
        G[g, :, :, :, 512:768] = edge.astype(BF16).reshape(4, 2, 96, 256)

    def small_1(V, k):
        send(V.at[0], V.at[1], vs.at[k, 0], vr.at[k, 0], nc)

    def small_2(V, k):
        arrive(V.at[1], vr.at[k, 0])
        V[2] = V[0] + V[1]
        send(V.at[2], V.at[3], vs.at[k, 1], vr.at[k, 1], nx)

    def small_3(V, k):
        arrive(V.at[3], vr.at[k, 1])
        V[4] = V[2] + V[3]
        send(V.at[4], V.at[5], vs.at[k, 2], vr.at[k, 2], ny)

    def small_4(V, k):
        arrive(V.at[5], vr.at[k, 2])
        V[6] = V[4] + V[5]
        for r in (1, 2, 3):
            send(V.at[6], V.at[6 + r], vs.at[k, 2 + r], vr.at[k, 2 + r], nz[r])

    def small_5(V, k):
        for r in (1, 2, 3):
            arrive(V.at[6 + r], vr.at[k, 2 + r])

    EV[0, 9:16, :] = jnp.zeros((7, 768), F32)
    LV[0, 3:8, :] = jnp.zeros((5, 768), F32)
    attend_back(3)
    store_attention(3)
    reduce_1(7)
    reduce_3(1)
    down_own = reduce_4(0)
    attend_back(2)
    store_attention(2)
    reduce_1(6)
    reduce_2(7)
    reduce_3(2)
    reduce_4(1)
    attend_back(1)
    small_1(EV, 0)
    store_attention(1)
    reduce_1(5)
    reduce_2(6)
    reduce_3(3)
    up_own = reduce_4(2)
    attend_back(0)
    small_2(EV, 0)
    store_attention(0)
    reduce_1(4)
    reduce_2(5)

    first_back = DH1[...]
    LV[0, 0:1, :] = column_sum(first_back * N1[...])
    LV[0, 1:2, :] = column_sum(first_back)
    small_1(LV, 1)
    reduce_2(4)
    small_2(LV, 1)
    reduce_3(7)
    reduce_4(3)
    gx_ref[...] = (DX1[...] + norm_back(first_back, ln1_gain, N1[...], R1[...]))[0:live]
    small_3(EV, 0)
    reduce_3(6)
    reduce_4(7)
    small_3(LV, 1)

    output = dot_nn(ACT[0, mine], W[5]) + dot_nn(ACT[1, mine], W[7])
    arrive(OR, xr.at[3])
    output = X1[...] + output + OR[...].astype(F32) + b_down
    y_ref[...] = output[0:live].astype(BF16)
    small_4(EV, 0)
    gd_ref[...] = down_own + landed(1)
    gu_ref[...] = up_own + landed(3)

    reduce_3(5)
    reduce_4(6)
    small_4(LV, 1)
    reduce_3(4)
    reduce_4(5)
    small_5(EV, 0)
    small_5(LV, 1)
    sv_ref[0:2, :] = LV[6, 0:2, :] + LV[7, 0:2, :] + LV[8, 0:2, :] + LV[9, 0:2, :]
    sv_ref[2:6, :] = EV[6, 0:4, :] + EV[7, 0:4, :] + EV[8, 0:4, :] + EV[9, 0:4, :]
    sv_ref[6:7, :] = EV[6, 4:5, :] + EV[8, 5:6, :]
    bias = LV[6, 2:3, :] + EV[7, 6:7, :] + EV[8, 7:8, :] + EV[9, 8:9, :]
    bias = [bias[:, s * 192 + h * 64:s * 192 + h * 64 + 64] for h in range(3) for s in range(3)]
    sv_ref[7:8, :] = jnp.concatenate(bias + [jnp.zeros((1, 192), F32)], axis=1)
    block = reduce_4(4)
    for r in (1, 2, 3):
        block = block + landed(4 + r)
    gq_ref[...] = jnp.concatenate(
        [block[:, s * 192 + h * 64:s * 192 + h * 64 + 64] for h in range(3) for s in range(3)], axis=1)
    go_ref[...] = block[:, 576:768].T
    for copy in sends:
        copy.wait_send()
    for condition, copy in late_sends:
        pl.when(condition)(copy.wait_send)


def write_outputs(y, gx, gq, go, gu, gd, sv, *outs):
    refs = (y, gx, gq, go, gu, gd)
    for source, target in zip(refs, outs[:6]):
        target[...] = source[...]
    for i, target in enumerate(outs[6:13]):
        target[...] = sv[i:i + 1, :].reshape(768)
    outs[13][...] = sv[7:8, 0:576].reshape(576)


def trig_table(live, rows, head_dim):
    half = head_dim // 2
    freq = (10000.0 ** (-np.arange(half, dtype=np.float32) * 2.0 / head_dim)).astype(np.float32)
    angle = (np.arange(rows, dtype=np.float32)[:, None] * freq[None, :]).astype(np.float64)
    cosine, sine = np.cos(angle), np.sin(angle)
    table = np.concatenate([cosine, cosine, -sine, sine], axis=1) * head_dim ** (-0.25)
    return table.astype(np.float32)


def local(
    n_dp, layer_input, lengths, ln1_gain, ln1_bias, w_qkv, b_qkv, features, w_out, b_out,
    ln2_gain, ln2_bias, w_up, b_up, w_down, b_down, cotangent,
):
    live, width = layer_input.shape
    rows = -(-live // 16) * 16
    trig = jnp.asarray(trig_table(live, rows, features.shape[1]))
    vmem = pl.BlockSpec(memory_space=pltpu.VMEM)
    smem = pl.BlockSpec(memory_space=pltpu.SMEM)
    anywhere = pl.BlockSpec(memory_space=pl.ANY)
    dma = pltpu.SemaphoreType.DMA

    def buf(*shape):
        return pltpu.VMEM(shape, BF16)

    def wide(*shape):
        return pltpu.VMEM(shape, F32)

    outs = pl.pallas_call(
        functools.partial(layer_kernel, live),
        out_shape=[
            jax.ShapeDtypeStruct((live, width), BF16),
            jax.ShapeDtypeStruct((live, width), F32),
            jax.ShapeDtypeStruct((96, 576), F32),
            jax.ShapeDtypeStruct((192, 96), F32),
            jax.ShapeDtypeStruct((96, 768), F32),
            jax.ShapeDtypeStruct((96, 768), F32),
            jax.ShapeDtypeStruct((8, 768), F32),
        ],
        in_specs=[vmem, vmem, smem] + [vmem] * 10 + [anywhere] * 4,
        out_specs=[vmem] * 7,
        scratch_shapes=[
            buf(8, 768, 768), wide(4, 80, 128), buf(2 * rows, 768), buf(2 * rows, 768),
            buf(768, 2 * rows), buf(768, 2 * rows), buf(rows, 768), buf(768, rows),
            buf(rows, 768), buf(768, rows), wide(rows, 768), wide(rows, 1), wide(rows, 768),
            wide(rows, 768), wide(rows, 1), wide(rows, 768), wide(rows, 768),
            wide(rows, 384), wide(rows, 384), buf(4, 384, 192), buf(4, 384, 192),
            buf(4, rows, 192), wide(4, rows, 192), buf(4, rows, 192), wide(4, rows, 192),
            wide(4, rows, 192), buf(4, rows, 192), wide(4, 192, 192), wide(4, 192, 192),
            wide(2, 2 * rows, 768), buf(2, 2 * rows, 768), buf(2, 2 * rows, 768), buf(rows, 576),
            buf(rows, 768), buf(rows, 768), buf(rows, 768), buf(rows, 768),
            buf(8, 4, 2, 96, 768), buf(8, 4, 96, 768), buf(8, 2, 48, 768), buf(8, 2, 48, 768),
            buf(8, 2, 48, 768), buf(8, 2, 48, 768), buf(8, 96, 768), buf(8, 96, 768),
            wide(10, 16, 768), wide(10, 8, 768),
            dma((4,)), dma((16,)), dma((8,)), dma((8, 8)), dma((8, 9)), dma((4,)), dma((4,)),
            dma((8, 8)), dma((8, 8)), dma((2, 6)), dma((2, 6)),
        ],
        compiler_params=pltpu.CompilerParams(
            collective_id=0, has_side_effects=True, vmem_limit_bytes=67043328),
    )(
        layer_input, cotangent, lengths, ln1_gain, ln1_bias, b_out, ln2_gain, ln2_bias, b_down,
        b_up, b_qkv, features.transpose(0, 2, 1), trig, w_qkv.T, w_out, w_up, w_down)
    outs = pl.pallas_call(
        write_outputs,
        out_shape=[jax.ShapeDtypeStruct(out.shape, out.dtype) for out in outs[:6]]
        + [jax.ShapeDtypeStruct((width,), F32)] * 7 + [jax.ShapeDtypeStruct((576,), F32)],
        in_specs=[vmem] * 7,
        out_specs=[vmem] * 14,
    )(*outs)
    output, grad_x, qkv_piece, out_piece, up_piece, down_piece, *common, up_bias, qkv_bias = outs
    down_piece = down_piece.T
    if n_dp != GROUP:
        member = lax.axis_index("dp") % GROUP

        def spread(piece, axis):
            shape = list(piece.shape)
            shape[axis] = shape[axis] * GROUP
            start = [0, 0]
            start[axis] = member * piece.shape[axis]
            whole = lax.dynamic_update_slice(jnp.zeros(shape, F32), piece, start)
            return lax.psum_scatter(whole, "dp", scatter_dimension=axis, tiled=True)

        qkv_piece, out_piece = spread(qkv_piece, 0), spread(out_piece, 1)
        up_piece, down_piece = spread(up_piece, 0), spread(down_piece, 1)
        common, up_bias, qkv_bias = jax.tree.map(
            lambda part: lax.psum(part, "dp") / GROUP, (common, up_bias, qkv_bias))
    return (
        output, grad_x, common[0], common[1], qkv_piece, qkv_bias, out_piece, common[2],
        common[3], common[4], up_piece, up_bias, down_piece, common[5],
    )


def solution(mesh):
    rows, cols = P(("dp", "mp"), None), P(None, "mp")
    placed = (
        rows, P("dp"), P(), P(), cols, P("mp"), P("mp", None, None), P("mp", None), P(),
        P(), P(), cols, P("mp"), P("mp", None), P(), rows,
    )
    return jax.shard_map(
        functools.partial(local, mesh.shape["dp"]),
        mesh=mesh,
        in_specs=placed,
        out_specs=(
            rows, rows, P(), P(), P("dp", "mp"), P("mp"), P("mp", "dp"), P(),
            P(), P(), P("dp", "mp"), P("mp"), P("mp", "dp"), P(),
        ),
        check_vma=False,
    )
```

```python
import functools

import jax
import jax.numpy as jnp
import numpy as np
from jax import lax
from jax.experimental import pallas as pl
from jax.experimental.pallas import tpu as pltpu
from jax.sharding import PartitionSpec as P

MESH = pl.DeviceIdType.MESH
BF16 = jnp.bfloat16
F32 = jnp.float32
EPSILON = 1e-05
GROUP = 8


def dot_nn(left, right):
    return lax.dot_general(left, right, (((1,), (0,)), ((), ())), preferred_element_type=F32)


def dot_nt(left, right):
    return lax.dot_general(left, right, (((1,), (1,)), ((), ())), preferred_element_type=F32)


def dot_tn(left, right):
    return lax.dot_general(left, right, (((0,), (0,)), ((), ())), preferred_element_type=F32)


def split(values):
    high = values.astype(BF16)
    return high, (values - high.astype(F32)).astype(BF16)


def normalize(values):
    centred = values - jnp.mean(values, axis=-1, keepdims=True)
    factor = lax.rsqrt(jnp.mean(centred * centred, axis=-1, keepdims=True) + EPSILON)
    return centred * factor, factor


def norm_back(grad, gain, normed, factor):
    hat = grad * gain
    return factor * (
        hat
        - jnp.mean(hat, axis=-1, keepdims=True)
        - normed * jnp.mean(hat * normed, axis=-1, keepdims=True)
    )


def column_sum(values):
    return jnp.sum(values, axis=0, keepdims=True)


def swap_halves(values):
    width = values.shape[1]
    lane = lax.broadcasted_iota(jnp.int32, values.shape, 1)
    return jnp.where(lane % 64 < 32, pltpu.roll(values, width - 32, 1), pltpu.roll(values, 32, 1))


def layer_kernel(live, *refs):
    (
        x_ref, c_ref, len_ref, ln1_gain_ref, ln1_bias_ref, b_out_ref, ln2_gain_ref, ln2_bias_ref,
        b_down_ref, b_up_ref, b_qkv_ref, feat_ref, trig_ref, wqkv_ref, wout_ref, wup_ref, wdown_ref,
        y_ref, gx_ref, gq_ref, go_ref, gu_ref, gd_ref, sv_ref,
        W, SP, CC, H2, CT, H2T, H1, H1T, GO, GOT, N1, R1, X1, N2, R2, DX1, DH1,
        COS, SIN, FH, FL, PHI, EE, VV, ATT, INV, AB, ST, TT, DA, ACT, DPRE, DQ,
        OS, OR, HS, HR, G, Q0, QX, QY, T2, Q2, U, ZR, BL, EV, LV,
        local_sem, zs, zr, ags, agr, xs, xr, rs, rr, vs, vr,
    ) = refs
    rows = CC.shape[0] // 2
    dp = lax.axis_index("dp")
    z = lax.axis_index("mp")
    member = dp % GROUP
    c = member % 2
    bx = (member // 2) % 2
    by = member // 4
    nx = (dp + 2 - 4 * bx, z)
    ny = (dp + 4 - 8 * by, z)
    nc = (dp + 1 - 2 * c, z)
    nz = (None, (dp, z + 1 - 2 * (z % 2)), (dp, (z + 2) % 4), (dp, 3 - z))

    def place(yy, xx, cc):
        return pl.multiple_of((yy * 4 + xx * 2 + cc) * 96, 96)

    sends = []
    done = set()

    def once(key, action, *args):
        if key not in done:
            done.add(key)
            action(*args)

    def send(src, dst, send_sem, recv_sem, device):
        copy = pltpu.make_async_remote_copy(
            src_ref=src, dst_ref=dst, send_sem=send_sem, recv_sem=recv_sem,
            device_id=device, device_id_type=MESH,
        )
        copy.start()
        sends.append(copy)

    def arrive(dst, recv_sem):
        pltpu.make_async_remote_copy(
            src_ref=dst, dst_ref=dst, send_sem=recv_sem, recv_sem=recv_sem,
            device_id=nc, device_id_type=MESH,
        ).wait_recv()

    barrier = pltpu.get_barrier_semaphore()
    for device in (nx, ny, nc, nz[1], nz[2], nz[3]):
        pl.semaphore_signal(barrier, inc=1, device_id=device, device_id_type=MESH)

    loads = [
        pltpu.make_async_copy(source, target, local_sem.at[i])
        for i, (source, target) in enumerate((
            (wqkv_ref, W.at[0, 0:576]), (wout_ref, W.at[0, 576:768]),
            (wup_ref, W.at[4]), (wdown_ref, W.at[5])))
    ]
    for load in loads:
        load.start()

    SP[0, 0:64, 0:96] = feat_ref[...].reshape(96, 64).T
    qkv_bias = b_qkv_ref[...].reshape(1, 576)
    qkv_bias = jnp.concatenate(
        [qkv_bias[:, h * 192 + s * 64:h * 192 + s * 64 + 64] for s in range(3) for h in range(3)]
        + [jnp.zeros((1, 64), F32)], axis=1)
    for i in range(5):
        SP[0, 64 + i:65 + i, :] = qkv_bias[:, i * 128:i * 128 + 128]
    up_bias = b_up_ref[...].reshape(1, 768)
    for i in range(6):
        SP[0, 72 + i:73 + i, :] = up_bias[:, i * 128:i * 128 + 128]
    CC[0:rows, :] = jnp.concatenate([c_ref[...].astype(F32), jnp.zeros((rows - live, 768), F32)], axis=0).astype(BF16)

    pl.semaphore_wait(barrier, 6)

    own = pl.ds(place(by, bx, c), 96)
    inner = jnp.logical_or(z == 1, z == 2)
    second_rank = jnp.where(inner, 3, 2)
    third_rank = jnp.where(inner, 2, 3)

    def send_if(condition, src, dst, send_sem, recv_sem, device):
        copy = pltpu.make_async_remote_copy(
            src_ref=src, dst_ref=dst, send_sem=send_sem, recv_sem=recv_sem,
            device_id=device, device_id_type=MESH,
        )

        @pl.when(condition)
        def _():
            copy.start()

        late_sends.append((condition, copy))

    late_sends = []
    in_qkv = member < 6
    out_rows = pl.ds(pl.multiple_of(jnp.maximum(own.start - 576, 0), 96), 96)
    qkv_rows = pl.ds(pl.multiple_of(jnp.minimum(own.start, 480), 96), 96)
    for r, condition in ((1, None), (3, inner)):
        for part, source in ((in_qkv, wqkv_ref.at[qkv_rows]), (jnp.logical_not(in_qkv), wout_ref.at[out_rows])):
            both = part if condition is None else jnp.logical_and(part, condition)
            send_if(both, source, W.at[r, own], zs.at[r], agr.at[r, 0], nz[r])
    half = pl.ds(pl.multiple_of(c * 40, 8), 40)
    other_half = pl.ds(pl.multiple_of((1 - c) * 40, 8), 40)

    def forward(b, to_rank, slot):
        send_if(inner, W.at[b, own], W.at[slot, own], zs.at[3 + slot + to_rank], agr.at[slot, 0], nz[to_rank])

    at_x = pl.ds(place(by, 1 - bx, c), 96)
    at_y = pl.ds(place(1 - by, bx, c), 96)
    at_d = pl.ds(place(1 - by, 1 - bx, c), 96)
    at_x0 = pl.ds(place(by, 1 - bx, c), 48)
    at_y1 = pl.ds(pl.multiple_of(place(1 - by, bx, c) + 48, 48), 48)
    at_d0 = pl.ds(place(1 - by, 1 - bx, c), 48)
    at_d1 = pl.ds(pl.multiple_of(place(1 - by, 1 - bx, c) + 48, 48), 48)

    def gather_a(b):
        arrive(W.at[b, own], agr.at[b, 0])
        send(W.at[b, own], W.at[b, own], ags.at[b, 0], agr.at[b, 1], nx)
        send(W.at[b, own], W.at[b, own], ags.at[b, 1], agr.at[b, 2], ny)
        send(W.at[b, own], W.at[b, own], ags.at[b, 2], agr.at[b, 5], nc)

    def gather_x(b):
        arrive(W.at[b, at_x], agr.at[b, 1])
        send(W.at[b, at_x0], W.at[b, at_x0], ags.at[b, 3], agr.at[b, 3], ny)
        send(W.at[b, at_x], W.at[b, at_x], ags.at[b, 4], agr.at[b, 6], nc)

    def gather_y(b):
        arrive(W.at[b, at_y], agr.at[b, 2])
        send(W.at[b, at_y1], W.at[b, at_y1], ags.at[b, 5], agr.at[b, 4], nx)
        send(W.at[b, at_y], W.at[b, at_y], ags.at[b, 6], agr.at[b, 7], nc)

    def gather_c(b):
        arrive(W.at[b, at_d0], agr.at[b, 3])
        arrive(W.at[b, at_d1], agr.at[b, 4])
        send(W.at[b, at_d], W.at[b, at_d], ags.at[b, 7], agr.at[b, 8], nc)

    def gather_small(r):
        arrive(SP.at[r, half], zr.at[r])
        send(SP.at[r, half], SP.at[r, half], zs.at[12 + r], zr.at[4 + r], nc)

    def small_done(r):
        arrive(SP.at[r, other_half], zr.at[4 + r])

    def qkv_rows_of(r):
        return jnp.concatenate(
            [W[r, h * 192 + s * 64:h * 192 + s * 64 + 64, :] for s in range(3) for h in range(3)], axis=0)

    def gather_d(b):
        for k, (yy, xx) in enumerate(((by, bx), (by, 1 - bx), (1 - by, bx), (1 - by, 1 - bx))):
            arrive(W.at[b, pl.ds(place(yy, xx, 1 - c), 96)], agr.at[b, 5 + k])

    rank = (0, 2, 0, 2, 0, 1, 2, 3)
    kept = {0: gd_ref, 2: gu_ref, 4: BL}

    def reduce_1(g):
        send(G.at[g, :, 1 - c], Q0.at[g], rs.at[g, 0], rr.at[g, 0], nc)

    def reduce_2(g):
        arrive(Q0.at[g], rr.at[g, 0])
        for i in range(4):
            Q0[g, i] = (Q0[g, i].astype(F32) + G[g, i, c].astype(F32)).astype(BF16)
        for i in range(2):
            send(Q0.at[g, 2 * i + 1 - bx, 0:48], QX.at[g, i], rs.at[g, 1 + i], rr.at[g, 1 + i], nx)
            send(Q0.at[g, 2 * (1 - by) + i, 48:96], QY.at[g, i], rs.at[g, 3 + i], rr.at[g, 3 + i], ny)

    def reduce_3(g):
        for i in range(2):
            arrive(QX.at[g, i], rr.at[g, 1 + i])
            arrive(QY.at[g, i], rr.at[g, 3 + i])
        T2[g, 0] = (Q0[g, 2 * (1 - by) + bx, 0:48].astype(F32) + QX[g, 1 - by].astype(F32)).astype(BF16)
        T2[g, 1] = (Q0[g, 2 * by + 1 - bx, 48:96].astype(F32) + QY[g, 1 - bx].astype(F32)).astype(BF16)
        send(T2.at[g, 0], Q2.at[g, 0], rs.at[g, 5], rr.at[g, 5], ny)
        send(T2.at[g, 1], Q2.at[g, 1], rs.at[g, 6], rr.at[g, 6], nx)

    def reduce_4(g):
        arrive(Q2.at[g, 0], rr.at[g, 5])
        arrive(Q2.at[g, 1], rr.at[g, 6])
        mine = 2 * by + bx
        first = Q0[g, mine, 0:48].astype(F32) + QX[g, by].astype(F32) + Q2[g, 0].astype(F32)
        second = Q0[g, mine, 48:96].astype(F32) + QY[g, bx].astype(F32) + Q2[g, 1].astype(F32)
        total = jnp.concatenate([first, second], axis=0)
        if rank[g] == 0:
            kept[g][...] = total
        else:
            U[g] = total.astype(BF16)
            send(U.at[g], ZR.at[g], rs.at[g, 7], rr.at[g, 7], nz[rank[g]])

    def landed(g):
        arrive(ZR.at[g], rr.at[g, 7])
        return ZR[g].astype(F32)

    ln1_gain, ln1_bias, b_out, ln2_gain, ln2_bias, b_down = (
        ref[...].reshape(1, 768)
        for ref in (ln1_gain_ref, ln1_bias_ref, b_out_ref, ln2_gain_ref, ln2_bias_ref, b_down_ref))
    position = lax.broadcasted_iota(jnp.int32, (rows, 1), 0)
    key_mask = (position < len_ref[z]).astype(F32)
    trig = trig_ref[...]
    COS[...] = jnp.concatenate([trig[:, 0:64]] * 6, axis=1)
    SIN[...] = jnp.concatenate([trig[:, 64:128]] * 6, axis=1)
    row_q = lax.broadcasted_iota(jnp.int32, (192, 192), 0)
    col_q = lax.broadcasted_iota(jnp.int32, (192, 192), 1)
    head_mask = jnp.logical_and(row_q < 96, row_q // 32 == col_q // 64)
    row_f = lax.broadcasted_iota(jnp.int32, (384, 192), 0)
    col_f = lax.broadcasted_iota(jnp.int32, (384, 192), 1)
    feat_mask = row_f // 64 == col_f // 32

    X1[...] = jnp.concatenate([x_ref[...].astype(F32), jnp.zeros((rows - live, 768), F32)], axis=0)
    normed, factor = normalize(X1[...])
    N1[...] = normed
    R1[...] = factor
    first = (normed * ln1_gain + ln1_bias).astype(BF16)
    H1[...] = first

    def attend(r):
        bias = jnp.concatenate([SP[r, 64 + i:65 + i, :] for i in range(5)], axis=1)[:, 0:576]
        projected = dot_nt(H1[...], qkv_rows_of(r)) + bias
        both = projected[:, 0:384]
        value = projected[:, 384:576].astype(BF16)
        turned = both * COS[...] + swap_halves(both) * SIN[...]
        plain = SP[r, 0:64, :][:, 0:96]
        plain = jnp.concatenate([plain, plain], axis=1)
        block = jnp.where(feat_mask, jnp.concatenate([plain] * 6, axis=0), 0.0)
        f_high, f_low = split(block)
        FH[r] = f_high
        FL[r] = f_low
        t_high, t_low = split(turned)
        u = dot_nn(t_high, f_high) + dot_nn(t_high, f_low) + dot_nn(t_low, f_high)
        decay = jnp.exp(jnp.minimum(u, 0.0))
        EE[r] = decay
        phi32 = jnp.where(u > 0.0, u + 1.0, decay)
        phi = phi32.astype(BF16)
        PHI[r] = phi
        VV[r] = value
        masked = (phi.astype(F32) * key_mask).astype(BF16)
        pad = jnp.zeros((96, 192), F32)
        state = jnp.concatenate([dot_tn(masked, value)[96:192], pad], axis=0)
        total = jnp.concatenate([dot_tn(masked, jnp.ones((rows, 192), BF16))[96:192], pad], axis=0)
        state = jnp.where(head_mask, state, 0.0)
        total = jnp.where(head_mask, total, 0.0)
        ST[r] = state
        TT[r] = total
        s_high, s_low = split(state)
        k_high, k_low = split(total)
        numer = dot_nn(phi, s_high) + dot_nn(phi, s_low)
        inverse = 1.0 / (dot_nn(phi, k_high) + dot_nn(phi, k_low))
        attended = numer * inverse
        ATT[r] = attended
        INV[r] = inverse
        mixed = attended.astype(BF16)
        AB[r] = mixed
        X1[...] += dot_nn(mixed, W[r, 576:768, :])

    theirs = pl.ds(rows, rows)
    mine_rows = pl.ds(0, rows)
    up = (4, 6)
    down = (5, 7)
    EV[0, 9:16, :] = jnp.zeros((7, 768), F32)
    LV[0, 3:8, :] = jnp.zeros((5, 768), F32)

    def share_small():
        for r in (1, 2, 3):
            send(SP.at[0, half], SP.at[r, half], zs.at[8 + r], zr.at[r], nz[r])

    def share_up():
        send(wup_ref.at[own], W.at[6, own], zs.at[2], agr.at[6, 0], nz[2])

    def share_down():
        send(wdown_ref.at[own], W.at[7, own], zs.at[0], agr.at[7, 0], nz[2])

    def share_cotangent():
        send(CC.at[0:rows], CC.at[rows:2 * rows], xs.at[0], xr.at[0], nz[1])

    def whole(b):
        for r in (2, 3) if b is second_rank or b is third_rank else (1,) if b == 1 else (2,):
            once(("small", r), small_done, r)
        gather_d(b)

    def loaded(i):
        once(("load", i), loads[i].wait)

    def cotangent_here():
        once("cotangent", arrive, CC.at[rows:2 * rows], xr.at[0])

    def second_here():
        once("second", arrive, H2.at[rows:2 * rows], xr.at[1])

    def attend_first():
        loaded(0)
        loaded(1)
        attend(0)

    def attend_next(b):
        whole(b)
        attend(b)

    def second_norm():
        middle = X1[...] + b_out
        X1[...] = middle
        normed, factor = normalize(middle)
        N2[...] = normed
        R2[...] = factor
        H2[0:rows, :] = (normed * ln2_gain + ln2_bias).astype(BF16)
        send(H2.at[0:rows], H2.at[rows:2 * rows], xs.at[1], xr.at[1], nz[1])

    def back_hidden(q):
        cotangent_here()
        if q == 0:
            loaded(3)
        else:
            gather_d(7)
        DA[q] = dot_nt(CC[...], W[down[q]])

    def feed(q, s):
        if s == 1:
            second_here()
        if q == 0:
            loaded(2)
        else:
            once("up", whole, 6)
        part = pl.ds(s * rows, rows)
        bias = jnp.concatenate([SP[2 * q, 72 + i:73 + i, :] for i in range(6)], axis=1)
        pre = dot_nn(H2[part], W[up[q]]) + bias
        half = 0.5 * (1.0 + lax.erf(pre * (0.5 ** 0.5)))
        ACT[q, part] = (pre * half).astype(BF16)
        slope = half + pre * jnp.exp(-0.5 * pre * pre) * (0.5 / np.pi) ** 0.5
        DPRE[q, part] = (DA[q, part] * slope).astype(BF16)

    def transpose_rows():
        cotangent_here()
        CT[...] = CC[...].T
        H1T[...] = H1[...].T

    def transpose_second():
        H2T[...] = H2[...].T

    def store_block(g):
        q = g % 2
        if g >= 2:
            once("turned", transpose_second)
        for n in range(3):
            cols = slice(n * 256, n * 256 + 256)
            if g < 2:
                block = dot_nn(CT[...], ACT[q, :, cols])
            else:
                block = dot_nn(H2T[...], DPRE[q, :, cols])
            G[g, :, :, :, cols] = block.astype(BF16).reshape(4, 2, 96, 256)
        reduce_1(g)

    def hidden_back():
        HS[...] = (dot_nt(DPRE[0, theirs], W[4]) + dot_nt(DPRE[1, theirs], W[6])).astype(BF16)
        send(HS, HR, xs.at[2], xr.at[2], nz[1])

    def hidden_out():
        OS[...] = (dot_nn(ACT[0, theirs], W[5]) + dot_nn(ACT[1, theirs], W[7])).astype(BF16)
        send(OS, OR, xs.at[3], xr.at[3], nz[1])
        for q in range(2):
            EV[0, 4 + q:5 + q, :] = column_sum(DPRE[q].astype(F32))

    def own_hidden_back():
        DH1[...] = dot_nt(DPRE[0, mine_rows], W[4]) + dot_nt(DPRE[1, mine_rows], W[6])

    def second_norm_back():
        arrive(HR, xr.at[2])
        own_back = DH1[...] + HR[...].astype(F32)
        cot = CC[mine_rows].astype(F32)
        EV[0, 1:2, :] = column_sum(own_back * N2[...])
        EV[0, 2:3, :] = column_sum(own_back)
        EV[0, 3:4, :] = column_sum(cot)
        dx1 = cot + norm_back(own_back, ln2_gain, N2[...], R2[...])
        DX1[...] = dx1
        branch = dx1.astype(BF16)
        GO[...] = branch
        EV[0, 0:1, :] = column_sum(branch.astype(F32))
        GOT[...] = GO[...].T

    def store_attention(r):
        g = 4 + r
        for n in range(2):
            cols = slice(n * 256, n * 256 + 256)
            G[g, :, :, :, cols] = dot_nn(H1T[...], DQ[:, cols]).astype(BF16).reshape(4, 2, 96, 256)
        edge = jnp.concatenate(
            [dot_nn(H1T[...], DQ[:, 512:576]), dot_nn(GOT[...], AB[r])], axis=1)
        G[g, :, :, :, 512:768] = edge.astype(BF16).reshape(4, 2, 96, 256)

    def attend_back(r):
        da = dot_nt(GO[...], W[r, 576:768, :])
        phi = PHI[r]
        dnum = da * INV[r]
        drest = -(dnum * ATT[r])
        n_high, n_low = split(dnum)
        d_high, d_low = split(drest)
        s_high, s_low = split(ST[r])
        k_high, k_low = split(TT[r])
        dphi = dot_nt(n_high, s_high) + dot_nt(n_high, s_low) + dot_nt(n_low, s_high)
        dphi += dot_nt(d_high, k_high) + dot_nt(d_high, k_low) + dot_nt(d_low, k_high)
        pad = jnp.zeros((96, 192), F32)
        dstate = jnp.where(head_mask, dot_tn(phi, n_high) + dot_tn(phi, n_low), 0.0)
        dtotal = jnp.where(head_mask, dot_tn(phi, d_high) + dot_tn(phi, d_low), 0.0)
        a_high, a_low = split(jnp.concatenate([pad, dstate[0:96]], axis=0))
        b_high, b_low = split(jnp.concatenate([pad, dtotal[0:96]], axis=0))
        ones = jnp.ones((16, 192), BF16)
        dkey = dot_nt(VV[r], a_high) + dot_nt(VV[r], a_low)
        dkey += (dot_nt(ones, b_high) + dot_nt(ones, b_low))[0:1, :]
        dphi += key_mask * dkey
        dvalue = key_mask * (dot_nn(phi, a_high) + dot_nn(phi, a_low))
        u_high, u_low = split(dphi * EE[r])
        back = dot_nt(u_high, FH[r]) + dot_nt(u_high, FL[r]) + dot_nt(u_low, FH[r])
        back = back * COS[...] - swap_halves(back) * SIN[...]
        DQ[:, 0:384] = back.astype(BF16)
        DQ[:, 384:576] = dvalue.astype(BF16)
        bias_sum = jnp.concatenate([column_sum(DQ[...].astype(F32)), jnp.zeros((1, 192), F32)], axis=1)
        if r == 0:
            LV[0, 2:3, :] = bias_sum
        else:
            EV[0, 5 + r:6 + r, :] = bias_sum
        grad = dot_nn(DQ[...], qkv_rows_of(r))
        if "back" in done:
            DH1[...] += grad
        else:
            DH1[...] = grad
        done.add("back")
        store_attention(r)
        reduce_1(4 + r)

    def small_1(V, k):
        send(V.at[0], V.at[1], vs.at[k, 0], vr.at[k, 0], nc)

    def small_2(V, k):
        arrive(V.at[1], vr.at[k, 0])
        V[2] = V[0] + V[1]
        send(V.at[2], V.at[3], vs.at[k, 1], vr.at[k, 1], nx)

    def small_3(V, k):
        arrive(V.at[3], vr.at[k, 1])
        V[4] = V[2] + V[3]
        send(V.at[4], V.at[5], vs.at[k, 2], vr.at[k, 2], ny)

    def small_4(V, k):
        arrive(V.at[5], vr.at[k, 2])
        V[6] = V[4] + V[5]
        for r in (1, 2, 3):
            send(V.at[6], V.at[6 + r], vs.at[k, 2 + r], vr.at[k, 2 + r], nz[r])

    def small_5(V, k):
        for r in (1, 2, 3):
            arrive(V.at[6 + r], vr.at[k, 2 + r])

    def first_norm_sums():
        first_back = DH1[...]
        LV[0, 0:1, :] = column_sum(first_back * N1[...])
        LV[0, 1:2, :] = column_sum(first_back)
        small_1(LV, 1)

    def input_grad():
        gx_ref[...] = (DX1[...] + norm_back(DH1[...], ln1_gain, N1[...], R1[...]))[0:live]

    def layer_output():
        output = dot_nn(ACT[0, mine_rows], W[5]) + dot_nn(ACT[1, mine_rows], W[7])
        arrive(OR, xr.at[3])
        output = X1[...] + output + OR[...].astype(F32) + b_down
        y_ref[...] = output[0:live].astype(BF16)

    def down_done():
        gd_ref[...] += landed(1)

    def up_done():
        gu_ref[...] += landed(3)

    def attention_done():
        block = BL[...]
        for r in (1, 2, 3):
            block = block + landed(4 + r)
        gq_ref[...] = jnp.concatenate(
            [block[:, s * 192 + h * 64:s * 192 + h * 64 + 64] for h in range(3) for s in range(3)], axis=1)
        go_ref[...] = block[:, 576:768].T

    share_small()
    gather_a(1)
    forward(1, 3, 2)
    gather_a(second_rank)
    share_down()
    forward(3, 1, 2)
    gather_y(1)
    gather_x(1)
    gather_a(third_rank)
    forward(2, 1, 3)
    gather_small(3)
    gather_x(second_rank)
    gather_c(1)
    share_up()
    gather_small(1)
    gather_y(second_rank)
    attend_first()
    share_cotangent()
    gather_y(third_rank)
    gather_x(third_rank)
    gather_small(2)
    gather_a(7)
    attend_next(1)
    gather_c(second_rank)
    attend_next(second_rank)
    gather_a(6)
    gather_c(third_rank)
    attend_next(third_rank)
    second_norm()
    gather_x(7)
    gather_y(7)
    back_hidden(0)
    gather_x(6)
    gather_y(6)
    gather_c(7)
    back_hidden(1)
    feed(0, 0)
    transpose_rows()
    gather_c(6)
    feed(1, 0)
    feed(1, 1)
    feed(0, 1)
    hidden_back()
    store_block(3)
    store_block(1)
    reduce_2(3)
    reduce_2(1)
    hidden_out()
    reduce_3(3)
    store_block(0)
    store_block(2)
    own_hidden_back()
    second_norm_back()
    reduce_3(1)
    reduce_2(2)
    attend_back(2)
    reduce_4(3)
    attend_back(1)
    reduce_2(6)
    reduce_2(5)
    reduce_4(1)
    attend_back(3)
    small_1(EV, 0)
    reduce_3(6)
    small_2(EV, 0)
    attend_back(0)
    reduce_2(7)
    reduce_4(6)
    first_norm_sums()
    small_3(EV, 0)
    reduce_3(2)
    reduce_3(5)
    reduce_3(7)
    small_2(LV, 1)
    reduce_2(0)
    layer_output()
    small_4(EV, 0)
    reduce_2(4)
    reduce_4(5)
    reduce_4(2)
    reduce_4(7)
    small_3(LV, 1)
    small_5(EV, 0)
    reduce_3(0)
    reduce_3(4)
    small_4(LV, 1)
    reduce_4(4)
    reduce_4(0)
    attention_done()
    up_done()
    input_grad()
    down_done()
    small_5(LV, 1)

    sv_ref[0:2, :] = LV[6, 0:2, :] + LV[7, 0:2, :] + LV[8, 0:2, :] + LV[9, 0:2, :]
    sv_ref[2:6, :] = EV[6, 0:4, :] + EV[7, 0:4, :] + EV[8, 0:4, :] + EV[9, 0:4, :]
    sv_ref[6:7, :] = EV[6, 4:5, :] + EV[8, 5:6, :]
    bias = LV[6, 2:3, :] + EV[7, 6:7, :] + EV[8, 7:8, :] + EV[9, 8:9, :]
    bias = [bias[:, s * 192 + h * 64:s * 192 + h * 64 + 64] for h in range(3) for s in range(3)]
    sv_ref[7:8, :] = jnp.concatenate(bias + [jnp.zeros((1, 192), F32)], axis=1)
    for copy in sends:
        copy.wait_send()
    for condition, copy in late_sends:
        pl.when(condition)(copy.wait_send)


def write_outputs(y, gx, gq, go, gu, gd, sv, *outs):
    refs = (y, gx, gq, go, gu, gd)
    for source, target in zip(refs, outs[:6]):
        target[...] = source[...]
    for i, target in enumerate(outs[6:13]):
        target[...] = sv[i:i + 1, :].reshape(768)
    outs[13][...] = sv[7:8, 0:576].reshape(576)


def trig_table(live, rows, head_dim):
    half = head_dim // 2
    freq = (10000.0 ** (-np.arange(half, dtype=np.float32) * 2.0 / head_dim)).astype(np.float32)
    angle = (np.arange(rows, dtype=np.float32)[:, None] * freq[None, :]).astype(np.float64)
    cosine, sine = np.cos(angle), np.sin(angle)
    table = np.concatenate([cosine, cosine, -sine, sine], axis=1) * head_dim ** (-0.25)
    return table.astype(np.float32)


def local(
    n_dp, layer_input, lengths, ln1_gain, ln1_bias, w_qkv, b_qkv, features, w_out, b_out,
    ln2_gain, ln2_bias, w_up, b_up, w_down, b_down, cotangent,
):
    live, width = layer_input.shape
    rows = -(-live // 16) * 16
    trig = jnp.asarray(trig_table(live, rows, features.shape[1]))
    vmem = pl.BlockSpec(memory_space=pltpu.VMEM)
    smem = pl.BlockSpec(memory_space=pltpu.SMEM)
    anywhere = pl.BlockSpec(memory_space=pl.ANY)
    dma = pltpu.SemaphoreType.DMA

    def buf(*shape):
        return pltpu.VMEM(shape, BF16)

    def wide(*shape):
        return pltpu.VMEM(shape, F32)

    outs = pl.pallas_call(
        functools.partial(layer_kernel, live),
        out_shape=[
            jax.ShapeDtypeStruct((live, width), BF16),
            jax.ShapeDtypeStruct((live, width), F32),
            jax.ShapeDtypeStruct((96, 576), F32),
            jax.ShapeDtypeStruct((192, 96), F32),
            jax.ShapeDtypeStruct((96, 768), F32),
            jax.ShapeDtypeStruct((96, 768), F32),
            jax.ShapeDtypeStruct((8, 768), F32),
        ],
        in_specs=[vmem, vmem, smem] + [vmem] * 10 + [anywhere] * 4,
        out_specs=[vmem] * 7,
        scratch_shapes=[
            buf(8, 768, 768), wide(4, 80, 128), buf(2 * rows, 768), buf(2 * rows, 768),
            buf(768, 2 * rows), buf(768, 2 * rows), buf(rows, 768), buf(768, rows),
            buf(rows, 768), buf(768, rows), wide(rows, 768), wide(rows, 1), wide(rows, 768),
            wide(rows, 768), wide(rows, 1), wide(rows, 768), wide(rows, 768),
            wide(rows, 384), wide(rows, 384), buf(4, 384, 192), buf(4, 384, 192),
            buf(4, rows, 192), wide(4, rows, 192), buf(4, rows, 192), wide(4, rows, 192),
            wide(4, rows, 192), buf(4, rows, 192), wide(4, 192, 192), wide(4, 192, 192),
            wide(2, 2 * rows, 768), buf(2, 2 * rows, 768), buf(2, 2 * rows, 768), buf(rows, 576),
            buf(rows, 768), buf(rows, 768), buf(rows, 768), buf(rows, 768),
            buf(8, 4, 2, 96, 768), buf(8, 4, 96, 768), buf(8, 2, 48, 768), buf(8, 2, 48, 768),
            buf(8, 2, 48, 768), buf(8, 2, 48, 768), buf(8, 96, 768), buf(8, 96, 768), wide(96, 768),
            wide(10, 16, 768), wide(10, 8, 768),
            dma((4,)), dma((16,)), dma((8,)), dma((8, 8)), dma((8, 9)), dma((4,)), dma((4,)),
            dma((8, 8)), dma((8, 8)), dma((2, 6)), dma((2, 6)),
        ],
        compiler_params=pltpu.CompilerParams(
            collective_id=0, has_side_effects=True, vmem_limit_bytes=67043328),
    )(
        layer_input, cotangent, lengths, ln1_gain, ln1_bias, b_out, ln2_gain, ln2_bias, b_down,
        b_up, b_qkv, features.transpose(0, 2, 1), trig, w_qkv.T, w_out, w_up, w_down)
    outs = pl.pallas_call(
        write_outputs,
        out_shape=[jax.ShapeDtypeStruct(out.shape, out.dtype) for out in outs[:6]]
        + [jax.ShapeDtypeStruct((width,), F32)] * 7 + [jax.ShapeDtypeStruct((576,), F32)],
        in_specs=[vmem] * 7,
        out_specs=[vmem] * 14,
    )(*outs)
    output, grad_x, qkv_piece, out_piece, up_piece, down_piece, *common, up_bias, qkv_bias = outs
    down_piece = down_piece.T
    if n_dp != GROUP:
        member = lax.axis_index("dp") % GROUP

        def spread(piece, axis):
            shape = list(piece.shape)
            shape[axis] = shape[axis] * GROUP
            start = [0, 0]
            start[axis] = member * piece.shape[axis]
            whole = lax.dynamic_update_slice(jnp.zeros(shape, F32), piece, start)
            return lax.psum_scatter(whole, "dp", scatter_dimension=axis, tiled=True)

        qkv_piece, out_piece = spread(qkv_piece, 0), spread(out_piece, 1)
        up_piece, down_piece = spread(up_piece, 0), spread(down_piece, 1)
        common, up_bias, qkv_bias = jax.tree.map(
            lambda part: lax.psum(part, "dp") / GROUP, (common, up_bias, qkv_bias))
    return (
        output, grad_x, common[0], common[1], qkv_piece, qkv_bias, out_piece, common[2],
        common[3], common[4], up_piece, up_bias, down_piece, common[5],
    )


def solution(mesh):
    rows, cols = P(("dp", "mp"), None), P(None, "mp")
    placed = (
        rows, P("dp"), P(), P(), cols, P("mp"), P("mp", None, None), P("mp", None), P(),
        P(), P(), cols, P("mp"), P("mp", None), P(), rows,
    )
    return jax.shard_map(
        functools.partial(local, mesh.shape["dp"]),
        mesh=mesh,
        in_specs=placed,
        out_specs=(
            rows, rows, P(), P(), P("dp", "mp"), P("mp"), P("mp", "dp"), P(),
            P(), P(), P("dp", "mp"), P("mp"), P("mp", "dp"), P(),
        ),
        check_vma=False,
    )
```

```python
import functools

import jax
import jax.numpy as jnp
import numpy as np
from jax import lax
from jax.experimental import pallas as pl
from jax.experimental.pallas import tpu as pltpu
from jax.sharding import PartitionSpec as P

MESH = pl.DeviceIdType.MESH
BF16 = jnp.bfloat16
F32 = jnp.float32
EPSILON = 1e-05
GROUP = 8


def dot_nn(left, right):
    return lax.dot_general(left, right, (((1,), (0,)), ((), ())), preferred_element_type=F32)


def dot_nt(left, right):
    return lax.dot_general(left, right, (((1,), (1,)), ((), ())), preferred_element_type=F32)


def dot_tn(left, right):
    return lax.dot_general(left, right, (((0,), (0,)), ((), ())), preferred_element_type=F32)


def split(values):
    high = values.astype(BF16)
    return high, (values - high.astype(F32)).astype(BF16)


def normalize(values):
    centred = values - jnp.mean(values, axis=-1, keepdims=True)
    factor = lax.rsqrt(jnp.mean(centred * centred, axis=-1, keepdims=True) + EPSILON)
    return centred * factor, factor


def norm_back(grad, gain, normed, factor):
    hat = grad * gain
    return factor * (
        hat
        - jnp.mean(hat, axis=-1, keepdims=True)
        - normed * jnp.mean(hat * normed, axis=-1, keepdims=True)
    )


def column_sum(values):
    return jnp.sum(values, axis=0, keepdims=True)


def swap_halves(values):
    width = values.shape[1]
    lane = lax.broadcasted_iota(jnp.int32, values.shape, 1)
    return jnp.where(lane % 64 < 32, pltpu.roll(values, width - 32, 1), pltpu.roll(values, 32, 1))


def layer_kernel(live, *refs):
    (
        x_ref, c_ref, len_ref, ln1_gain_ref, ln1_bias_ref, b_out_ref, ln2_gain_ref, ln2_bias_ref,
        b_down_ref, b_up_ref, b_qkv_ref, feat_ref, trig_ref, wqkv_ref, wout_ref, wup_ref, wdown_ref,
        y_ref, gx_ref, gq_ref, go_ref, gu_ref, gd_ref, sv_ref,
        W, SP, CC, H2, CT, H2T, H1, H1T, GO, GOT, N1, R1, X1, N2, R2, DX1, DH1,
        COS, SIN, FH, FL, PHI, EE, VV, ATT, INV, AB, ST, TT, DA, ACT, DPRE, DQ,
        OS, OR, HS, HR, G, Q0, QX, QY, T2, Q2, U, ZR, BL, EV, LV,
        local_sem, zs, zr, ags, agr, xs, xr, rs, rr, vs, vr,
    ) = refs
    rows = CC.shape[0] // 2
    dp = lax.axis_index("dp")
    z = lax.axis_index("mp")
    member = dp % GROUP
    c = member % 2
    bx = (member // 2) % 2
    by = member // 4
    nx = (dp + 2 - 4 * bx, z)
    ny = (dp + 4 - 8 * by, z)
    nc = (dp + 1 - 2 * c, z)
    nz = (None, (dp, z + 1 - 2 * (z % 2)), (dp, (z + 2) % 4), (dp, 3 - z))

    def place(yy, xx, cc):
        return pl.multiple_of((yy * 4 + xx * 2 + cc) * 96, 96)

    sends = []
    done = set()

    def once(key, action, *args):
        if key not in done:
            done.add(key)
            action(*args)

    def send(src, dst, send_sem, recv_sem, device):
        copy = pltpu.make_async_remote_copy(
            src_ref=src, dst_ref=dst, send_sem=send_sem, recv_sem=recv_sem,
            device_id=device, device_id_type=MESH,
        )
        copy.start()
        sends.append(copy)

    def arrive(dst, recv_sem):
        pltpu.make_async_remote_copy(
            src_ref=dst, dst_ref=dst, send_sem=recv_sem, recv_sem=recv_sem,
            device_id=nc, device_id_type=MESH,
        ).wait_recv()

    barrier = pltpu.get_barrier_semaphore()
    for device in (nx, ny, nc, nz[1], nz[2], nz[3]):
        pl.semaphore_signal(barrier, inc=1, device_id=device, device_id_type=MESH)

    loads = [
        pltpu.make_async_copy(source, target, local_sem.at[i])
        for i, (source, target) in enumerate((
            (wqkv_ref, W.at[0, 0:576]), (wout_ref, W.at[0, 576:768]),
            (wup_ref, W.at[4]), (wdown_ref, W.at[5])))
    ]
    for load in loads:
        load.start()

    SP[0, 0:64, 0:96] = feat_ref[...].reshape(96, 64).T
    qkv_bias = b_qkv_ref[...].reshape(1, 576)
    qkv_bias = jnp.concatenate(
        [qkv_bias[:, h * 192 + s * 64:h * 192 + s * 64 + 64] for s in range(3) for h in range(3)]
        + [jnp.zeros((1, 64), F32)], axis=1)
    for i in range(5):
        SP[0, 64 + i:65 + i, :] = qkv_bias[:, i * 128:i * 128 + 128]
    up_bias = b_up_ref[...].reshape(1, 768)
    for i in range(6):
        SP[0, 72 + i:73 + i, :] = up_bias[:, i * 128:i * 128 + 128]
    CC[0:rows, :] = jnp.concatenate([c_ref[...].astype(F32), jnp.zeros((rows - live, 768), F32)], axis=0).astype(BF16)

    pl.semaphore_wait(barrier, 6)

    own = pl.ds(place(by, bx, c), 96)
    inner = jnp.logical_or(z == 1, z == 2)
    second_rank = jnp.where(inner, 3, 2)
    third_rank = jnp.where(inner, 2, 3)

    def send_if(condition, src, dst, send_sem, recv_sem, device):
        copy = pltpu.make_async_remote_copy(
            src_ref=src, dst_ref=dst, send_sem=send_sem, recv_sem=recv_sem,
            device_id=device, device_id_type=MESH,
        )

        @pl.when(condition)
        def _():
            copy.start()

        late_sends.append((condition, copy))

    late_sends = []
    in_qkv = member < 6
    out_rows = pl.ds(pl.multiple_of(jnp.maximum(own.start - 576, 0), 96), 96)
    qkv_rows = pl.ds(pl.multiple_of(jnp.minimum(own.start, 480), 96), 96)
    for r, condition in ((1, None), (3, inner)):
        for h in (0, 1):
            here = pl.ds(pl.multiple_of(own.start + 48 * h, 48), 48)
            for part, ref, start in ((in_qkv, wqkv_ref, qkv_rows.start), (jnp.logical_not(in_qkv), wout_ref, out_rows.start)):
                both = part if condition is None else jnp.logical_and(part, condition)
                source = ref.at[pl.ds(pl.multiple_of(start + 48 * h, 48), 48)]
                send_if(both, source, W.at[r, here], zs.at[r + 16 * h], agr.at[r, h], nz[r])
    half = pl.ds(pl.multiple_of(c * 40, 8), 40)
    other_half = pl.ds(pl.multiple_of((1 - c) * 40, 8), 40)

    def forward(b, to_rank, slot, h):
        here = pl.ds(pl.multiple_of(own.start + 48 * h, 48), 48)
        send_if(inner, W.at[b, here], W.at[slot, here], zs.at[3 + slot + to_rank + 16 * h], agr.at[slot, h], nz[to_rank])

    at_d = pl.ds(place(1 - by, 1 - bx, c), 96)
    at_x0 = pl.ds(place(by, 1 - bx, c), 48)
    at_y1 = pl.ds(pl.multiple_of(place(1 - by, bx, c) + 48, 48), 48)
    at_d0 = pl.ds(place(1 - by, 1 - bx, c), 48)
    at_d1 = pl.ds(pl.multiple_of(place(1 - by, 1 - bx, c) + 48, 48), 48)

    def rows_at(yy, xx, cc, h):
        start = place(yy, xx, cc)
        return pl.ds(start, 96) if h is None else pl.ds(pl.multiple_of(start + 48 * h, 48), 48)

    def halves(b):
        return (None,) if isinstance(b, int) and b > 1 else (0, 1)

    def gather_a(b, h=None):
        k = h or 0
        part = W.at[b, rows_at(by, bx, c, h)]
        arrive(part, agr.at[b, k])
        send(part, part, ags.at[b, k], agr.at[b, 2 + k], nx)
        send(part, part, ags.at[b, 2 + k], agr.at[b, 4 + k], ny)
        send(part, part, ags.at[b, 4 + k], agr.at[b, 6 + k], nc)

    def gather_x(b, h=None):
        k = h or 0
        part = W.at[b, rows_at(by, 1 - bx, c, h)]
        arrive(part, agr.at[b, 2 + k])
        if h != 1:
            send(W.at[b, at_x0], W.at[b, at_x0], ags.at[b, 6], agr.at[b, 14], ny)
        send(part, part, ags.at[b, 8 + k], agr.at[b, 8 + k], nc)

    def gather_y(b, h=None):
        k = h or 0
        part = W.at[b, rows_at(1 - by, bx, c, h)]
        arrive(part, agr.at[b, 4 + k])
        if h != 0:
            send(W.at[b, at_y1], W.at[b, at_y1], ags.at[b, 7], agr.at[b, 15], nx)
        send(part, part, ags.at[b, 10 + k], agr.at[b, 10 + k], nc)

    def gather_c(b):
        arrive(W.at[b, at_d0], agr.at[b, 14])
        arrive(W.at[b, at_d1], agr.at[b, 15])
        send(W.at[b, at_d], W.at[b, at_d], ags.at[b, 12], agr.at[b, 12], nc)

    def gather_small(r):
        arrive(SP.at[r, half], zr.at[r])
        send(SP.at[r, half], SP.at[r, half], zs.at[12 + r], zr.at[4 + r], nc)

    def small_done(r):
        arrive(SP.at[r, other_half], zr.at[4 + r])

    def qkv_rows_of(r):
        return jnp.concatenate(
            [W[r, h * 192 + s * 64:h * 192 + s * 64 + 64, :] for s in range(3) for h in range(3)], axis=0)

    def gather_d(b):
        for n, (yy, xx) in enumerate(((by, bx), (by, 1 - bx), (1 - by, bx))):
            for h in halves(b):
                arrive(W.at[b, rows_at(yy, xx, 1 - c, h)], agr.at[b, 6 + 2 * n + (h or 0)])
        arrive(W.at[b, rows_at(1 - by, 1 - bx, 1 - c, None)], agr.at[b, 12])

    rank = (0, 2, 0, 2, 0, 1, 2, 3)
    kept = {0: gd_ref, 2: gu_ref, 4: BL}

    def reduce_1(g):
        send(G.at[g, :, 1 - c], Q0.at[g], rs.at[g, 0], rr.at[g, 0], nc)

    def reduce_2(g):
        arrive(Q0.at[g], rr.at[g, 0])
        for i in range(4):
            Q0[g, i] = (Q0[g, i].astype(F32) + G[g, i, c].astype(F32)).astype(BF16)
        for i in range(2):
            send(Q0.at[g, 2 * i + 1 - bx, 0:48], QX.at[g, i], rs.at[g, 1 + i], rr.at[g, 1 + i], nx)
            send(Q0.at[g, 2 * (1 - by) + i, 48:96], QY.at[g, i], rs.at[g, 3 + i], rr.at[g, 3 + i], ny)

    def reduce_3(g):
        for i in range(2):
            arrive(QX.at[g, i], rr.at[g, 1 + i])
            arrive(QY.at[g, i], rr.at[g, 3 + i])
        T2[g, 0] = (Q0[g, 2 * (1 - by) + bx, 0:48].astype(F32) + QX[g, 1 - by].astype(F32)).astype(BF16)
        T2[g, 1] = (Q0[g, 2 * by + 1 - bx, 48:96].astype(F32) + QY[g, 1 - bx].astype(F32)).astype(BF16)
        send(T2.at[g, 0], Q2.at[g, 0], rs.at[g, 5], rr.at[g, 5], ny)
        send(T2.at[g, 1], Q2.at[g, 1], rs.at[g, 6], rr.at[g, 6], nx)

    def reduce_4(g):
        arrive(Q2.at[g, 0], rr.at[g, 5])
        arrive(Q2.at[g, 1], rr.at[g, 6])
        mine = 2 * by + bx
        first = Q0[g, mine, 0:48].astype(F32) + QX[g, by].astype(F32) + Q2[g, 0].astype(F32)
        second = Q0[g, mine, 48:96].astype(F32) + QY[g, bx].astype(F32) + Q2[g, 1].astype(F32)
        total = jnp.concatenate([first, second], axis=0)
        if rank[g] == 0:
            kept[g][...] = total
        else:
            U[g] = total.astype(BF16)
            send(U.at[g], ZR.at[g], rs.at[g, 7], rr.at[g, 7], nz[rank[g]])

    def landed(g):
        arrive(ZR.at[g], rr.at[g, 7])
        return ZR[g].astype(F32)

    ln1_gain, ln1_bias, b_out, ln2_gain, ln2_bias, b_down = (
        ref[...].reshape(1, 768)
        for ref in (ln1_gain_ref, ln1_bias_ref, b_out_ref, ln2_gain_ref, ln2_bias_ref, b_down_ref))
    position = lax.broadcasted_iota(jnp.int32, (rows, 1), 0)
    key_mask = (position < len_ref[z]).astype(F32)
    trig = trig_ref[...]
    COS[...] = jnp.concatenate([trig[:, 0:64]] * 6, axis=1)
    SIN[...] = jnp.concatenate([trig[:, 64:128]] * 6, axis=1)
    row_q = lax.broadcasted_iota(jnp.int32, (192, 192), 0)
    col_q = lax.broadcasted_iota(jnp.int32, (192, 192), 1)
    head_mask = jnp.logical_and(row_q < 96, row_q // 32 == col_q // 64)
    row_f = lax.broadcasted_iota(jnp.int32, (384, 192), 0)
    col_f = lax.broadcasted_iota(jnp.int32, (384, 192), 1)
    feat_mask = row_f // 64 == col_f // 32

    X1[...] = jnp.concatenate([x_ref[...].astype(F32), jnp.zeros((rows - live, 768), F32)], axis=0)
    normed, factor = normalize(X1[...])
    N1[...] = normed
    R1[...] = factor
    first = (normed * ln1_gain + ln1_bias).astype(BF16)
    H1[...] = first

    def attend(r):
        bias = jnp.concatenate([SP[r, 64 + i:65 + i, :] for i in range(5)], axis=1)[:, 0:576]
        projected = dot_nt(H1[...], qkv_rows_of(r)) + bias
        both = projected[:, 0:384]
        value = projected[:, 384:576].astype(BF16)
        turned = both * COS[...] + swap_halves(both) * SIN[...]
        plain = SP[r, 0:64, :][:, 0:96]
        plain = jnp.concatenate([plain, plain], axis=1)
        block = jnp.where(feat_mask, jnp.concatenate([plain] * 6, axis=0), 0.0)
        f_high, f_low = split(block)
        FH[r] = f_high
        FL[r] = f_low
        t_high, t_low = split(turned)
        u = dot_nn(t_high, f_high) + dot_nn(t_high, f_low) + dot_nn(t_low, f_high)
        decay = jnp.exp(jnp.minimum(u, 0.0))
        EE[r] = decay
        phi32 = jnp.where(u > 0.0, u + 1.0, decay)
        phi = phi32.astype(BF16)
        PHI[r] = phi
        VV[r] = value
        masked = (phi.astype(F32) * key_mask).astype(BF16)
        pad = jnp.zeros((96, 192), F32)
        state = jnp.concatenate([dot_tn(masked, value)[96:192], pad], axis=0)
        total = jnp.concatenate([dot_tn(masked, jnp.ones((rows, 192), BF16))[96:192], pad], axis=0)
        state = jnp.where(head_mask, state, 0.0)
        total = jnp.where(head_mask, total, 0.0)
        ST[r] = state
        TT[r] = total
        s_high, s_low = split(state)
        k_high, k_low = split(total)
        numer = dot_nn(phi, s_high) + dot_nn(phi, s_low)
        inverse = 1.0 / (dot_nn(phi, k_high) + dot_nn(phi, k_low))
        attended = numer * inverse
        ATT[r] = attended
        INV[r] = inverse
        mixed = attended.astype(BF16)
        AB[r] = mixed
        X1[...] += dot_nn(mixed, W[r, 576:768, :])

    theirs = pl.ds(rows, rows)
    mine_rows = pl.ds(0, rows)
    up = (4, 6)
    down = (5, 7)
    EV[0, 9:16, :] = jnp.zeros((7, 768), F32)
    LV[0, 3:8, :] = jnp.zeros((5, 768), F32)

    def share_small():
        for r in (1, 2, 3):
            send(SP.at[0, half], SP.at[r, half], zs.at[8 + r], zr.at[r], nz[r])

    def share_up():
        send(wup_ref.at[own], W.at[6, own], zs.at[2], agr.at[6, 0], nz[2])

    def share_down():
        send(wdown_ref.at[own], W.at[7, own], zs.at[0], agr.at[7, 0], nz[2])

    def share_cotangent():
        send(CC.at[0:rows], CC.at[rows:2 * rows], xs.at[0], xr.at[0], nz[1])

    def whole(b):
        for r in (2, 3) if b is second_rank or b is third_rank else (1,) if b == 1 else (2,):
            once(("small", r), small_done, r)
        gather_d(b)

    def loaded(i):
        once(("load", i), loads[i].wait)

    def cotangent_here():
        once("cotangent", arrive, CC.at[rows:2 * rows], xr.at[0])

    cuts = ((0, 96), (96, rows))

    def second_here(k):
        lo, hi = cuts[k]
        once(("second", k), arrive, H2.at[rows + lo:rows + hi], xr.at[1 + 3 * k])

    def attend_first():
        loaded(0)
        loaded(1)
        attend(0)

    def attend_next(b):
        whole(b)
        attend(b)

    def second_norm(k):
        lo, hi = cuts[k]
        middle = X1[lo:hi] + b_out
        X1[lo:hi] = middle
        normed, factor = normalize(middle)
        N2[lo:hi] = normed
        R2[lo:hi] = factor
        H2[lo:hi, :] = (normed * ln2_gain + ln2_bias).astype(BF16)
        send(H2.at[lo:hi], H2.at[rows + lo:rows + hi], xs.at[1 + 3 * k], xr.at[1 + 3 * k], nz[1])

    def back_hidden(q):
        cotangent_here()
        if q == 0:
            loaded(3)
        else:
            gather_d(7)
        DA[q] = dot_nt(CC[...], W[down[q]])

    def feed(q, k=None):
        lo, hi = 0, rows
        if k is not None:
            second_here(k)
            lo, hi = rows + cuts[k][0], rows + cuts[k][1]
        if q == 0:
            loaded(2)
        else:
            once("up", whole, 6)
        part = pl.ds(lo, hi - lo)
        bias = jnp.concatenate([SP[2 * q, 72 + i:73 + i, :] for i in range(6)], axis=1)
        pre = dot_nn(H2[part], W[up[q]]) + bias
        half = 0.5 * (1.0 + lax.erf(pre * (0.5 ** 0.5)))
        ACT[q, part] = (pre * half).astype(BF16)
        slope = half + pre * jnp.exp(-0.5 * pre * pre) * (0.5 / np.pi) ** 0.5
        DPRE[q, part] = (DA[q, part] * slope).astype(BF16)

    def transpose_rows():
        cotangent_here()
        CT[...] = CC[...].T
        H1T[...] = H1[...].T

    def transpose_second():
        H2T[...] = H2[...].T

    def store_block(g):
        q = g % 2
        if g >= 2:
            once("turned", transpose_second)
        for n in range(3):
            cols = slice(n * 256, n * 256 + 256)
            if g < 2:
                block = dot_nn(CT[...], ACT[q, :, cols])
            else:
                block = dot_nn(H2T[...], DPRE[q, :, cols])
            G[g, :, :, :, cols] = block.astype(BF16).reshape(4, 2, 96, 256)
        reduce_1(g)

    def hidden_back(k):
        lo, hi = cuts[k]
        part = pl.ds(rows + lo, hi - lo)
        HS[lo:hi] = (dot_nt(DPRE[0, part], W[4]) + dot_nt(DPRE[1, part], W[6])).astype(BF16)
        send(HS.at[lo:hi], HR.at[lo:hi], xs.at[2 + 3 * k], xr.at[2 + 3 * k], nz[1])

    def hidden_out():
        OS[...] = (dot_nn(ACT[0, theirs], W[5]) + dot_nn(ACT[1, theirs], W[7])).astype(BF16)
        send(OS, OR, xs.at[3], xr.at[3], nz[1])
        for q in range(2):
            EV[0, 4 + q:5 + q, :] = column_sum(DPRE[q].astype(F32))

    def own_hidden_back():
        DH1[...] = dot_nt(DPRE[0, mine_rows], W[4]) + dot_nt(DPRE[1, mine_rows], W[6])

    def second_norm_back():
        for k, (lo, hi) in enumerate(cuts):
            arrive(HR.at[lo:hi], xr.at[2 + 3 * k])
        own_back = DH1[...] + HR[...].astype(F32)
        cot = CC[mine_rows].astype(F32)
        EV[0, 1:2, :] = column_sum(own_back * N2[...])
        EV[0, 2:3, :] = column_sum(own_back)
        EV[0, 3:4, :] = column_sum(cot)
        dx1 = cot + norm_back(own_back, ln2_gain, N2[...], R2[...])
        DX1[...] = dx1
        branch = dx1.astype(BF16)
        GO[...] = branch
        EV[0, 0:1, :] = column_sum(branch.astype(F32))
        GOT[...] = GO[...].T

    def store_attention(r):
        g = 4 + r
        for n in range(2):
            cols = slice(n * 256, n * 256 + 256)
            G[g, :, :, :, cols] = dot_nn(H1T[...], DQ[:, cols]).astype(BF16).reshape(4, 2, 96, 256)
        edge = jnp.concatenate(
            [dot_nn(H1T[...], DQ[:, 512:576]), dot_nn(GOT[...], AB[r])], axis=1)
        G[g, :, :, :, 512:768] = edge.astype(BF16).reshape(4, 2, 96, 256)

    def attend_back(r):
        da = dot_nt(GO[...], W[r, 576:768, :])
        phi = PHI[r]
        dnum = da * INV[r]
        drest = -(dnum * ATT[r])
        n_high, n_low = split(dnum)
        d_high, d_low = split(drest)
        s_high, s_low = split(ST[r])
        k_high, k_low = split(TT[r])
        dphi = dot_nt(n_high, s_high) + dot_nt(n_high, s_low) + dot_nt(n_low, s_high)
        dphi += dot_nt(d_high, k_high) + dot_nt(d_high, k_low) + dot_nt(d_low, k_high)
        pad = jnp.zeros((96, 192), F32)
        dstate = jnp.where(head_mask, dot_tn(phi, n_high) + dot_tn(phi, n_low), 0.0)
        dtotal = jnp.where(head_mask, dot_tn(phi, d_high) + dot_tn(phi, d_low), 0.0)
        a_high, a_low = split(jnp.concatenate([pad, dstate[0:96]], axis=0))
        b_high, b_low = split(jnp.concatenate([pad, dtotal[0:96]], axis=0))
        ones = jnp.ones((16, 192), BF16)
        dkey = dot_nt(VV[r], a_high) + dot_nt(VV[r], a_low)
        dkey += (dot_nt(ones, b_high) + dot_nt(ones, b_low))[0:1, :]
        dphi += key_mask * dkey
        dvalue = key_mask * (dot_nn(phi, a_high) + dot_nn(phi, a_low))
        u_high, u_low = split(dphi * EE[r])
        back = dot_nt(u_high, FH[r]) + dot_nt(u_high, FL[r]) + dot_nt(u_low, FH[r])
        back = back * COS[...] - swap_halves(back) * SIN[...]
        DQ[:, 0:384] = back.astype(BF16)
        DQ[:, 384:576] = dvalue.astype(BF16)
        bias_sum = jnp.concatenate([column_sum(DQ[...].astype(F32)), jnp.zeros((1, 192), F32)], axis=1)
        if r == 0:
            LV[0, 2:3, :] = bias_sum
        else:
            EV[0, 5 + r:6 + r, :] = bias_sum
        grad = dot_nn(DQ[...], qkv_rows_of(r))
        if "back" in done:
            DH1[...] += grad
        else:
            DH1[...] = grad
        done.add("back")
        store_attention(r)
        reduce_1(4 + r)

    def small_1(V, k):
        send(V.at[0], V.at[1], vs.at[k, 0], vr.at[k, 0], nc)

    def small_2(V, k):
        arrive(V.at[1], vr.at[k, 0])
        V[2] = V[0] + V[1]
        send(V.at[2], V.at[3], vs.at[k, 1], vr.at[k, 1], nx)

    def small_3(V, k):
        arrive(V.at[3], vr.at[k, 1])
        V[4] = V[2] + V[3]
        send(V.at[4], V.at[5], vs.at[k, 2], vr.at[k, 2], ny)

    def small_4(V, k):
        arrive(V.at[5], vr.at[k, 2])
        V[6] = V[4] + V[5]
        for r in (1, 2, 3):
            send(V.at[6], V.at[6 + r], vs.at[k, 2 + r], vr.at[k, 2 + r], nz[r])

    def small_5(V, k):
        for r in (1, 2, 3):
            arrive(V.at[6 + r], vr.at[k, 2 + r])

    def first_norm_sums():
        first_back = DH1[...]
        LV[0, 0:1, :] = column_sum(first_back * N1[...])
        LV[0, 1:2, :] = column_sum(first_back)
        small_1(LV, 1)

    def input_grad():
        gx_ref[...] = (DX1[...] + norm_back(DH1[...], ln1_gain, N1[...], R1[...]))[0:live]

    def layer_output():
        output = dot_nn(ACT[0, mine_rows], W[5]) + dot_nn(ACT[1, mine_rows], W[7])
        arrive(OR, xr.at[3])
        output = X1[...] + output + OR[...].astype(F32) + b_down
        y_ref[...] = output[0:live].astype(BF16)

    def down_done():
        gd_ref[...] += landed(1)

    def up_done():
        gu_ref[...] += landed(3)

    def attention_done():
        block = BL[...]
        for r in (1, 2, 3):
            block = block + landed(4 + r)
        gq_ref[...] = jnp.concatenate(
            [block[:, s * 192 + h * 64:s * 192 + h * 64 + 64] for h in range(3) for s in range(3)], axis=1)
        go_ref[...] = block[:, 576:768].T

    gather_a(1, 0)
    forward(1, 3, 2, 0)
    gather_a(second_rank, 0)
    forward(3, 1, 2, 0)
    gather_a(1, 1)
    forward(1, 3, 2, 1)
    share_down()
    gather_a(second_rank, 1)
    forward(3, 1, 2, 1)
    gather_x(1, 0)
    gather_y(1, 0)
    gather_a(third_rank, 0)
    forward(2, 1, 3, 0)
    gather_y(1, 1)
    gather_a(third_rank, 1)
    forward(2, 1, 3, 1)
    share_small()
    attend_first()
    gather_x(second_rank, 0)
    gather_x(1, 1)
    share_up()
    gather_x(third_rank, 0)
    gather_y(third_rank, 0)
    gather_y(second_rank, 0)
    gather_y(second_rank, 1)
    gather_y(third_rank, 1)
    gather_a(7)
    gather_small(1)
    gather_x(second_rank, 1)
    gather_x(third_rank, 1)
    gather_small(2)
    gather_c(1)
    gather_small(3)
    share_cotangent()
    gather_c(second_rank)
    attend_next(1)
    attend_next(second_rank)
    gather_a(6)
    gather_c(third_rank)
    attend_next(third_rank)
    gather_y(7)
    second_norm(0)
    gather_x(7)
    second_norm(1)
    gather_y(6)
    gather_x(6)
    back_hidden(0)
    feed(0)
    gather_c(7)
    transpose_rows()
    feed(0, 0)
    gather_c(6)
    back_hidden(1)
    feed(1)
    feed(1, 0)
    hidden_back(0)
    feed(1, 1)
    store_block(3)
    store_block(1)
    feed(0, 1)
    hidden_back(1)
    reduce_2(3)
    own_hidden_back()
    reduce_2(1)
    store_block(2)
    hidden_out()
    reduce_3(3)
    reduce_2(2)
    second_norm_back()
    attend_back(2)
    reduce_3(1)
    reduce_4(3)
    attend_back(3)
    reduce_2(6)
    attend_back(1)
    reduce_2(7)
    reduce_4(1)
    small_1(EV, 0)
    store_block(0)
    reduce_3(6)
    small_2(EV, 0)
    attend_back(0)
    reduce_2(5)
    reduce_4(6)
    small_3(EV, 0)
    first_norm_sums()
    reduce_3(7)
    reduce_3(5)
    reduce_2(4)
    small_2(LV, 1)
    reduce_2(0)
    layer_output()
    small_4(EV, 0)
    reduce_4(5)
    reduce_3(2)
    input_grad()
    reduce_4(7)
    small_3(LV, 1)
    reduce_3(0)
    reduce_3(4)
    small_4(LV, 1)
    reduce_4(4)
    reduce_4(0)
    reduce_4(2)
    small_5(EV, 0)
    down_done()
    up_done()
    attention_done()
    small_5(LV, 1)

    sv_ref[0:2, :] = LV[6, 0:2, :] + LV[7, 0:2, :] + LV[8, 0:2, :] + LV[9, 0:2, :]
    sv_ref[2:6, :] = EV[6, 0:4, :] + EV[7, 0:4, :] + EV[8, 0:4, :] + EV[9, 0:4, :]
    sv_ref[6:7, :] = EV[6, 4:5, :] + EV[8, 5:6, :]
    bias = LV[6, 2:3, :] + EV[7, 6:7, :] + EV[8, 7:8, :] + EV[9, 8:9, :]
    bias = [bias[:, s * 192 + h * 64:s * 192 + h * 64 + 64] for h in range(3) for s in range(3)]
    sv_ref[7:8, :] = jnp.concatenate(bias + [jnp.zeros((1, 192), F32)], axis=1)
    for copy in sends:
        copy.wait_send()
    for condition, copy in late_sends:
        pl.when(condition)(copy.wait_send)


def write_outputs(y, gx, gq, go, gu, gd, sv, *outs):
    refs = (y, gx, gq, go, gu, gd)
    for source, target in zip(refs, outs[:6]):
        target[...] = source[...]
    for i, target in enumerate(outs[6:13]):
        target[...] = sv[i:i + 1, :].reshape(768)
    outs[13][...] = sv[7:8, 0:576].reshape(576)


def trig_table(live, rows, head_dim):
    half = head_dim // 2
    freq = (10000.0 ** (-np.arange(half, dtype=np.float32) * 2.0 / head_dim)).astype(np.float32)
    angle = (np.arange(rows, dtype=np.float32)[:, None] * freq[None, :]).astype(np.float64)
    cosine, sine = np.cos(angle), np.sin(angle)
    table = np.concatenate([cosine, cosine, -sine, sine], axis=1) * head_dim ** (-0.25)
    return table.astype(np.float32)


def local(
    n_dp, layer_input, lengths, ln1_gain, ln1_bias, w_qkv, b_qkv, features, w_out, b_out,
    ln2_gain, ln2_bias, w_up, b_up, w_down, b_down, cotangent,
):
    live, width = layer_input.shape
    rows = -(-live // 16) * 16
    trig = jnp.asarray(trig_table(live, rows, features.shape[1]))
    vmem = pl.BlockSpec(memory_space=pltpu.VMEM)
    smem = pl.BlockSpec(memory_space=pltpu.SMEM)
    anywhere = pl.BlockSpec(memory_space=pl.ANY)
    dma = pltpu.SemaphoreType.DMA

    def buf(*shape):
        return pltpu.VMEM(shape, BF16)

    def wide(*shape):
        return pltpu.VMEM(shape, F32)

    outs = pl.pallas_call(
        functools.partial(layer_kernel, live),
        out_shape=[
            jax.ShapeDtypeStruct((live, width), BF16),
            jax.ShapeDtypeStruct((live, width), F32),
            jax.ShapeDtypeStruct((96, 576), F32),
            jax.ShapeDtypeStruct((192, 96), F32),
            jax.ShapeDtypeStruct((96, 768), F32),
            jax.ShapeDtypeStruct((96, 768), F32),
            jax.ShapeDtypeStruct((8, 768), F32),
        ],
        in_specs=[vmem, vmem, smem] + [vmem] * 10 + [anywhere] * 4,
        out_specs=[vmem] * 7,
        scratch_shapes=[
            buf(8, 768, 768), wide(4, 80, 128), buf(2 * rows, 768), buf(2 * rows, 768),
            buf(768, 2 * rows), buf(768, 2 * rows), buf(rows, 768), buf(768, rows),
            buf(rows, 768), buf(768, rows), wide(rows, 768), wide(rows, 1), wide(rows, 768),
            wide(rows, 768), wide(rows, 1), wide(rows, 768), wide(rows, 768),
            wide(rows, 384), wide(rows, 384), buf(4, 384, 192), buf(4, 384, 192),
            buf(4, rows, 192), wide(4, rows, 192), buf(4, rows, 192), wide(4, rows, 192),
            wide(4, rows, 192), buf(4, rows, 192), wide(4, 192, 192), wide(4, 192, 192),
            wide(2, 2 * rows, 768), buf(2, 2 * rows, 768), buf(2, 2 * rows, 768), buf(rows, 576),
            buf(rows, 768), buf(rows, 768), buf(rows, 768), buf(rows, 768),
            buf(8, 4, 2, 96, 768), buf(8, 4, 96, 768), buf(8, 2, 48, 768), buf(8, 2, 48, 768),
            buf(8, 2, 48, 768), buf(8, 2, 48, 768), buf(8, 96, 768), buf(8, 96, 768), wide(96, 768),
            wide(10, 16, 768), wide(10, 8, 768),
            dma((4,)), dma((32,)), dma((8,)), dma((8, 16)), dma((8, 16)), dma((6,)), dma((6,)),
            dma((8, 8)), dma((8, 8)), dma((2, 6)), dma((2, 6)),
        ],
        compiler_params=pltpu.CompilerParams(
            collective_id=0, has_side_effects=True, vmem_limit_bytes=67043328),
    )(
        layer_input, cotangent, lengths, ln1_gain, ln1_bias, b_out, ln2_gain, ln2_bias, b_down,
        b_up, b_qkv, features.transpose(0, 2, 1), trig, w_qkv.T, w_out, w_up, w_down)
    outs = pl.pallas_call(
        write_outputs,
        out_shape=[jax.ShapeDtypeStruct(out.shape, out.dtype) for out in outs[:6]]
        + [jax.ShapeDtypeStruct((width,), F32)] * 7 + [jax.ShapeDtypeStruct((576,), F32)],
        in_specs=[vmem] * 7,
        out_specs=[vmem] * 14,
    )(*outs)
    output, grad_x, qkv_piece, out_piece, up_piece, down_piece, *common, up_bias, qkv_bias = outs
    down_piece = down_piece.T
    if n_dp != GROUP:
        member = lax.axis_index("dp") % GROUP

        def spread(piece, axis):
            shape = list(piece.shape)
            shape[axis] = shape[axis] * GROUP
            start = [0, 0]
            start[axis] = member * piece.shape[axis]
            whole = lax.dynamic_update_slice(jnp.zeros(shape, F32), piece, start)
            return lax.psum_scatter(whole, "dp", scatter_dimension=axis, tiled=True)

        qkv_piece, out_piece = spread(qkv_piece, 0), spread(out_piece, 1)
        up_piece, down_piece = spread(up_piece, 0), spread(down_piece, 1)
        common, up_bias, qkv_bias = jax.tree.map(
            lambda part: lax.psum(part, "dp") / GROUP, (common, up_bias, qkv_bias))
    return (
        output, grad_x, common[0], common[1], qkv_piece, qkv_bias, out_piece, common[2],
        common[3], common[4], up_piece, up_bias, down_piece, common[5],
    )


def solution(mesh):
    rows, cols = P(("dp", "mp"), None), P(None, "mp")
    placed = (
        rows, P("dp"), P(), P(), cols, P("mp"), P("mp", None, None), P("mp", None), P(),
        P(), P(), cols, P("mp"), P("mp", None), P(), rows,
    )
    return jax.shard_map(
        functools.partial(local, mesh.shape["dp"]),
        mesh=mesh,
        in_specs=placed,
        out_specs=(
            rows, rows, P(), P(), P("dp", "mp"), P("mp"), P("mp", "dp"), P(),
            P(), P(), P("dp", "mp"), P("mp"), P("mp", "dp"), P(),
        ),
        check_vma=False,
    )
```

```python
import functools

import jax
import jax.numpy as jnp
import numpy as np
from jax import lax
from jax.experimental import pallas as pl
from jax.experimental.pallas import tpu as pltpu
from jax.sharding import PartitionSpec as P

MESH = pl.DeviceIdType.MESH
BF16 = jnp.bfloat16
F32 = jnp.float32
EPSILON = 1e-05
GROUP = 8


def dot_nn(left, right):
    return lax.dot_general(left, right, (((1,), (0,)), ((), ())), preferred_element_type=F32)


def dot_nt(left, right):
    return lax.dot_general(left, right, (((1,), (1,)), ((), ())), preferred_element_type=F32)


def dot_tn(left, right):
    return lax.dot_general(left, right, (((0,), (0,)), ((), ())), preferred_element_type=F32)


def split(values):
    high = values.astype(BF16)
    return high, (values - high.astype(F32)).astype(BF16)


def normalize(values):
    centred = values - jnp.mean(values, axis=-1, keepdims=True)
    factor = lax.rsqrt(jnp.mean(centred * centred, axis=-1, keepdims=True) + EPSILON)
    return centred * factor, factor


def norm_back(grad, gain, normed, factor):
    hat = grad * gain
    return factor * (
        hat
        - jnp.mean(hat, axis=-1, keepdims=True)
        - normed * jnp.mean(hat * normed, axis=-1, keepdims=True)
    )


def column_sum(values):
    return jnp.sum(values, axis=0, keepdims=True)


def swap_halves(values):
    width = values.shape[1]
    lane = lax.broadcasted_iota(jnp.int32, values.shape, 1)
    return jnp.where(lane % 64 < 32, pltpu.roll(values, width - 32, 1), pltpu.roll(values, 32, 1))


def layer_kernel(live, *refs):
    (
        wqkv_ref, wout_ref, wup_ref, wdown_ref,
        x_ref, c_ref, len_ref, ln1_gain_ref, ln1_bias_ref, b_out_ref, ln2_gain_ref, ln2_bias_ref,
        b_down_ref, b_up_ref, b_qkv_ref, feat_ref, trig_ref,
        y_ref, gx_ref, gq_ref, go_ref, gu_ref, gd_ref, sv_ref,
        W, SP, CC, H2, CT, H2T, H1, H1T, GO, GOT, N1, R1, X1, N2, R2, DX1, DH1,
        COS, SIN, FH, FL, PHI, EE, VV, ATT, INV, AB, ST, TT, DA, ACT, DPRE, DQ,
        OS, OR, HS, HR, G, Q0, QX, QY, T2, Q2, U, ZR, BL, EV, LV,
        local_sem, in_sem, out_sem, zs, zr, ags, agr, xs, xr, rs, rr, vs, vr,
    ) = refs[13:17] + refs[24:]
    rows = CC.shape[0] // 2
    dp = lax.axis_index("dp")
    z = lax.axis_index("mp")
    member = dp % GROUP
    c = member % 2
    bx = (member // 2) % 2
    by = member // 4
    nx = (dp + 2 - 4 * bx, z)
    ny = (dp + 4 - 8 * by, z)
    nc = (dp + 1 - 2 * c, z)
    nz = (None, (dp, z + 1 - 2 * (z % 2)), (dp, (z + 2) % 4), (dp, 3 - z))

    def place(yy, xx, cc):
        return pl.multiple_of((yy * 4 + xx * 2 + cc) * 96, 96)

    sends = []
    done = set()

    def once(key, action, *args):
        if key not in done:
            done.add(key)
            action(*args)

    def send(src, dst, send_sem, recv_sem, device):
        copy = pltpu.make_async_remote_copy(
            src_ref=src, dst_ref=dst, send_sem=send_sem, recv_sem=recv_sem,
            device_id=device, device_id_type=MESH,
        )
        copy.start()
        sends.append(copy)

    def arrive(dst, recv_sem):
        pltpu.make_async_remote_copy(
            src_ref=dst, dst_ref=dst, send_sem=recv_sem, recv_sem=recv_sem,
            device_id=nc, device_id_type=MESH,
        ).wait_recv()

    barrier = pltpu.get_barrier_semaphore()
    for device in (nx, ny, nc, nz[1], nz[2], nz[3]):
        pl.semaphore_signal(barrier, inc=1, device_id=device, device_id_type=MESH)

    takes = [
        pltpu.make_async_copy(source, target, in_sem.at[i])
        for i, (source, target) in enumerate(zip(refs[:13], refs[24:37]))
    ]
    for take in takes:
        take.start()
    gives = []

    def give(i):
        copy = pltpu.make_async_copy(refs[37 + i], refs[17 + i], out_sem.at[i])
        copy.start()
        gives.append(copy)

    loads = [
        pltpu.make_async_copy(source, target, local_sem.at[i])
        for i, (source, target) in enumerate((
            (wqkv_ref, W.at[0, 0:576]), (wout_ref, W.at[0, 576:768]),
            (wup_ref, W.at[4]), (wdown_ref, W.at[5])))
    ]
    for load in loads:
        load.start()

    pl.semaphore_wait(barrier, 6)

    own = pl.ds(place(by, bx, c), 96)
    inner = jnp.logical_or(z == 1, z == 2)
    second_rank = jnp.where(inner, 3, 2)
    third_rank = jnp.where(inner, 2, 3)

    def send_if(condition, src, dst, send_sem, recv_sem, device):
        copy = pltpu.make_async_remote_copy(
            src_ref=src, dst_ref=dst, send_sem=send_sem, recv_sem=recv_sem,
            device_id=device, device_id_type=MESH,
        )

        @pl.when(condition)
        def _():
            copy.start()

        late_sends.append((condition, copy))

    late_sends = []
    in_qkv = member < 6
    out_rows = pl.ds(pl.multiple_of(jnp.maximum(own.start - 576, 0), 96), 96)
    qkv_rows = pl.ds(pl.multiple_of(jnp.minimum(own.start, 480), 96), 96)
    for r, condition in ((1, None), (3, inner)):
        for h in (0, 1):
            here = pl.ds(pl.multiple_of(own.start + 48 * h, 48), 48)
            for part, ref, start in ((in_qkv, wqkv_ref, qkv_rows.start), (jnp.logical_not(in_qkv), wout_ref, out_rows.start)):
                both = part if condition is None else jnp.logical_and(part, condition)
                source = ref.at[pl.ds(pl.multiple_of(start + 48 * h, 48), 48)]
                send_if(both, source, W.at[r, here], zs.at[r + 16 * h], agr.at[r, h], nz[r])
    half = pl.ds(pl.multiple_of(c * 40, 8), 40)
    other_half = pl.ds(pl.multiple_of((1 - c) * 40, 8), 40)

    for take in takes:
        take.wait()
    SP[0, 0:64, 0:96] = feat_ref[...].reshape(96, 64).T
    qkv_bias = b_qkv_ref[...].reshape(1, 576)
    qkv_bias = jnp.concatenate(
        [qkv_bias[:, h * 192 + s * 64:h * 192 + s * 64 + 64] for s in range(3) for h in range(3)]
        + [jnp.zeros((1, 64), F32)], axis=1)
    for i in range(5):
        SP[0, 64 + i:65 + i, :] = qkv_bias[:, i * 128:i * 128 + 128]
    up_bias = b_up_ref[...].reshape(1, 768)
    for i in range(6):
        SP[0, 72 + i:73 + i, :] = up_bias[:, i * 128:i * 128 + 128]
    CC[0:rows, :] = jnp.concatenate([c_ref[...].astype(F32), jnp.zeros((rows - live, 768), F32)], axis=0).astype(BF16)

    def forward(b, to_rank, slot, h):
        here = pl.ds(pl.multiple_of(own.start + 48 * h, 48), 48)
        send_if(inner, W.at[b, here], W.at[slot, here], zs.at[3 + slot + to_rank + 16 * h], agr.at[slot, h], nz[to_rank])

    at_d = pl.ds(place(1 - by, 1 - bx, c), 96)
    at_x0 = pl.ds(place(by, 1 - bx, c), 48)
    at_y1 = pl.ds(pl.multiple_of(place(1 - by, bx, c) + 48, 48), 48)
    at_d0 = pl.ds(place(1 - by, 1 - bx, c), 48)
    at_d1 = pl.ds(pl.multiple_of(place(1 - by, 1 - bx, c) + 48, 48), 48)

    def rows_at(yy, xx, cc, h):
        start = place(yy, xx, cc)
        return pl.ds(start, 96) if h is None else pl.ds(pl.multiple_of(start + 48 * h, 48), 48)

    def halves(b):
        return (None,) if isinstance(b, int) and b > 1 else (0, 1)

    def gather_a(b, h=None):
        k = h or 0
        part = W.at[b, rows_at(by, bx, c, h)]
        arrive(part, agr.at[b, k])
        send(part, part, ags.at[b, k], agr.at[b, 2 + k], nx)
        send(part, part, ags.at[b, 2 + k], agr.at[b, 4 + k], ny)
        send(part, part, ags.at[b, 4 + k], agr.at[b, 6 + k], nc)

    def gather_x(b, h=None):
        k = h or 0
        part = W.at[b, rows_at(by, 1 - bx, c, h)]
        arrive(part, agr.at[b, 2 + k])
        if h != 1:
            send(W.at[b, at_x0], W.at[b, at_x0], ags.at[b, 6], agr.at[b, 14], ny)
        send(part, part, ags.at[b, 8 + k], agr.at[b, 8 + k], nc)

    def gather_y(b, h=None):
        k = h or 0
        part = W.at[b, rows_at(1 - by, bx, c, h)]
        arrive(part, agr.at[b, 4 + k])
        if h != 0:
            send(W.at[b, at_y1], W.at[b, at_y1], ags.at[b, 7], agr.at[b, 15], nx)
        send(part, part, ags.at[b, 10 + k], agr.at[b, 10 + k], nc)

    def gather_c(b):
        arrive(W.at[b, at_d0], agr.at[b, 14])
        arrive(W.at[b, at_d1], agr.at[b, 15])
        send(W.at[b, at_d], W.at[b, at_d], ags.at[b, 12], agr.at[b, 12], nc)

    def gather_small(r):
        arrive(SP.at[r, half], zr.at[r])
        send(SP.at[r, half], SP.at[r, half], zs.at[12 + r], zr.at[4 + r], nc)

    def small_done(r):
        arrive(SP.at[r, other_half], zr.at[4 + r])

    def qkv_rows_of(r):
        return jnp.concatenate(
            [W[r, h * 192 + s * 64:h * 192 + s * 64 + 64, :] for s in range(3) for h in range(3)], axis=0)

    def gather_d(b):
        for n, (yy, xx) in enumerate(((by, bx), (by, 1 - bx), (1 - by, bx))):
            for h in halves(b):
                arrive(W.at[b, rows_at(yy, xx, 1 - c, h)], agr.at[b, 6 + 2 * n + (h or 0)])
        arrive(W.at[b, rows_at(1 - by, 1 - bx, 1 - c, None)], agr.at[b, 12])

    rank = (0, 2, 0, 2, 0, 1, 2, 3)
    kept = {0: gd_ref, 2: gu_ref, 4: BL}

    def reduce_1(g):
        send(G.at[g, :, 1 - c], Q0.at[g], rs.at[g, 0], rr.at[g, 0], nc)

    def reduce_2(g):
        arrive(Q0.at[g], rr.at[g, 0])
        for i in range(4):
            Q0[g, i] = (Q0[g, i].astype(F32) + G[g, i, c].astype(F32)).astype(BF16)
        for i in range(2):
            send(Q0.at[g, 2 * i + 1 - bx, 0:48], QX.at[g, i], rs.at[g, 1 + i], rr.at[g, 1 + i], nx)
            send(Q0.at[g, 2 * (1 - by) + i, 48:96], QY.at[g, i], rs.at[g, 3 + i], rr.at[g, 3 + i], ny)

    def reduce_3(g):
        for i in range(2):
            arrive(QX.at[g, i], rr.at[g, 1 + i])
            arrive(QY.at[g, i], rr.at[g, 3 + i])
        T2[g, 0] = (Q0[g, 2 * (1 - by) + bx, 0:48].astype(F32) + QX[g, 1 - by].astype(F32)).astype(BF16)
        T2[g, 1] = (Q0[g, 2 * by + 1 - bx, 48:96].astype(F32) + QY[g, 1 - bx].astype(F32)).astype(BF16)
        send(T2.at[g, 0], Q2.at[g, 0], rs.at[g, 5], rr.at[g, 5], ny)
        send(T2.at[g, 1], Q2.at[g, 1], rs.at[g, 6], rr.at[g, 6], nx)

    def reduce_4(g):
        arrive(Q2.at[g, 0], rr.at[g, 5])
        arrive(Q2.at[g, 1], rr.at[g, 6])
        mine = 2 * by + bx
        first = Q0[g, mine, 0:48].astype(F32) + QX[g, by].astype(F32) + Q2[g, 0].astype(F32)
        second = Q0[g, mine, 48:96].astype(F32) + QY[g, bx].astype(F32) + Q2[g, 1].astype(F32)
        total = jnp.concatenate([first, second], axis=0)
        if rank[g] == 0:
            kept[g][...] = total
        else:
            U[g] = total.astype(BF16)
            send(U.at[g], ZR.at[g], rs.at[g, 7], rr.at[g, 7], nz[rank[g]])

    def landed(g):
        arrive(ZR.at[g], rr.at[g, 7])
        return ZR[g].astype(F32)

    ln1_gain, ln1_bias, b_out, ln2_gain, ln2_bias, b_down = (
        ref[...].reshape(1, 768)
        for ref in (ln1_gain_ref, ln1_bias_ref, b_out_ref, ln2_gain_ref, ln2_bias_ref, b_down_ref))
    position = lax.broadcasted_iota(jnp.int32, (rows, 1), 0)
    key_mask = (position < len_ref[z]).astype(F32)
    trig = trig_ref[...]
    COS[...] = jnp.concatenate([trig[:, 0:64]] * 6, axis=1)
    SIN[...] = jnp.concatenate([trig[:, 64:128]] * 6, axis=1)
    row_q = lax.broadcasted_iota(jnp.int32, (192, 192), 0)
    col_q = lax.broadcasted_iota(jnp.int32, (192, 192), 1)
    head_mask = jnp.logical_and(row_q < 96, row_q // 32 == col_q // 64)
    row_f = lax.broadcasted_iota(jnp.int32, (384, 192), 0)
    col_f = lax.broadcasted_iota(jnp.int32, (384, 192), 1)
    feat_mask = row_f // 64 == col_f // 32

    X1[...] = jnp.concatenate([x_ref[...].astype(F32), jnp.zeros((rows - live, 768), F32)], axis=0)
    normed, factor = normalize(X1[...])
    N1[...] = normed
    R1[...] = factor
    first = (normed * ln1_gain + ln1_bias).astype(BF16)
    H1[...] = first

    def attend(r):
        bias = jnp.concatenate([SP[r, 64 + i:65 + i, :] for i in range(5)], axis=1)[:, 0:576]
        projected = dot_nt(H1[...], qkv_rows_of(r)) + bias
        both = projected[:, 0:384]
        value = projected[:, 384:576].astype(BF16)
        turned = both * COS[...] + swap_halves(both) * SIN[...]
        plain = SP[r, 0:64, :][:, 0:96]
        plain = jnp.concatenate([plain, plain], axis=1)
        block = jnp.where(feat_mask, jnp.concatenate([plain] * 6, axis=0), 0.0)
        f_high, f_low = split(block)
        FH[r] = f_high
        FL[r] = f_low
        t_high, t_low = split(turned)
        u = dot_nn(t_high, f_high) + dot_nn(t_high, f_low) + dot_nn(t_low, f_high)
        decay = jnp.exp(jnp.minimum(u, 0.0))
        EE[r] = decay
        phi32 = jnp.where(u > 0.0, u + 1.0, decay)
        phi = phi32.astype(BF16)
        PHI[r] = phi
        VV[r] = value
        masked = (phi.astype(F32) * key_mask).astype(BF16)
        pad = jnp.zeros((96, 192), F32)
        state = jnp.concatenate([dot_tn(masked, value)[96:192], pad], axis=0)
        total = jnp.concatenate([dot_tn(masked, jnp.ones((rows, 192), BF16))[96:192], pad], axis=0)
        state = jnp.where(head_mask, state, 0.0)
        total = jnp.where(head_mask, total, 0.0)
        ST[r] = state
        TT[r] = total
        s_high, s_low = split(state)
        k_high, k_low = split(total)
        numer = dot_nn(phi, s_high) + dot_nn(phi, s_low)
        inverse = 1.0 / (dot_nn(phi, k_high) + dot_nn(phi, k_low))
        attended = numer * inverse
        ATT[r] = attended
        INV[r] = inverse
        mixed = attended.astype(BF16)
        AB[r] = mixed
        X1[...] += dot_nn(mixed, W[r, 576:768, :])

    theirs = pl.ds(rows, rows)
    mine_rows = pl.ds(0, rows)
    up = (4, 6)
    down = (5, 7)
    EV[0, 9:16, :] = jnp.zeros((7, 768), F32)
    LV[0, 3:8, :] = jnp.zeros((5, 768), F32)

    def share_small():
        for r in (1, 2, 3):
            send(SP.at[0, half], SP.at[r, half], zs.at[8 + r], zr.at[r], nz[r])

    def share_up():
        send(wup_ref.at[own], W.at[6, own], zs.at[2], agr.at[6, 0], nz[2])

    def share_down():
        send(wdown_ref.at[own], W.at[7, own], zs.at[0], agr.at[7, 0], nz[2])

    def share_cotangent():
        send(CC.at[0:rows], CC.at[rows:2 * rows], xs.at[0], xr.at[0], nz[1])

    def whole(b):
        for r in (2, 3) if b is second_rank or b is third_rank else (1,) if b == 1 else (2,):
            once(("small", r), small_done, r)
        gather_d(b)

    def loaded(i):
        once(("load", i), loads[i].wait)

    def cotangent_here():
        once("cotangent", arrive, CC.at[rows:2 * rows], xr.at[0])

    cuts = ((0, 96), (96, rows))

    def second_here(k):
        lo, hi = cuts[k]
        once(("second", k), arrive, H2.at[rows + lo:rows + hi], xr.at[1 + 3 * k])

    def attend_first():
        loaded(0)
        loaded(1)
        attend(0)

    def attend_next(b):
        whole(b)
        attend(b)

    def second_norm(k):
        lo, hi = cuts[k]
        middle = X1[lo:hi] + b_out
        X1[lo:hi] = middle
        normed, factor = normalize(middle)
        N2[lo:hi] = normed
        R2[lo:hi] = factor
        H2[lo:hi, :] = (normed * ln2_gain + ln2_bias).astype(BF16)
        send(H2.at[lo:hi], H2.at[rows + lo:rows + hi], xs.at[1 + 3 * k], xr.at[1 + 3 * k], nz[1])

    def back_hidden(q):
        cotangent_here()
        if q == 0:
            loaded(3)
        else:
            gather_d(7)
        DA[q] = dot_nt(CC[...], W[down[q]])

    def feed(q, k=None):
        lo, hi = 0, rows
        if k is not None:
            second_here(k)
            lo, hi = rows + cuts[k][0], rows + cuts[k][1]
        if q == 0:
            loaded(2)
        else:
            once("up", whole, 6)
        part = pl.ds(lo, hi - lo)
        bias = jnp.concatenate([SP[2 * q, 72 + i:73 + i, :] for i in range(6)], axis=1)
        pre = dot_nn(H2[part], W[up[q]]) + bias
        half = 0.5 * (1.0 + lax.erf(pre * (0.5 ** 0.5)))
        ACT[q, part] = (pre * half).astype(BF16)
        slope = half + pre * jnp.exp(-0.5 * pre * pre) * (0.5 / np.pi) ** 0.5
        DPRE[q, part] = (DA[q, part] * slope).astype(BF16)

    def transpose_rows():
        cotangent_here()
        CT[...] = CC[...].T
        H1T[...] = H1[...].T

    def transpose_second():
        H2T[...] = H2[...].T

    def store_block(g):
        q = g % 2
        if g >= 2:
            once("turned", transpose_second)
        for n in range(3):
            cols = slice(n * 256, n * 256 + 256)
            if g < 2:
                block = dot_nn(CT[...], ACT[q, :, cols])
            else:
                block = dot_nn(H2T[...], DPRE[q, :, cols])
            G[g, :, :, :, cols] = block.astype(BF16).reshape(4, 2, 96, 256)
        reduce_1(g)

    def hidden_back(k):
        lo, hi = cuts[k]
        part = pl.ds(rows + lo, hi - lo)
        HS[lo:hi] = (dot_nt(DPRE[0, part], W[4]) + dot_nt(DPRE[1, part], W[6])).astype(BF16)
        send(HS.at[lo:hi], HR.at[lo:hi], xs.at[2 + 3 * k], xr.at[2 + 3 * k], nz[1])

    def hidden_out():
        OS[...] = (dot_nn(ACT[0, theirs], W[5]) + dot_nn(ACT[1, theirs], W[7])).astype(BF16)
        send(OS, OR, xs.at[3], xr.at[3], nz[1])
        for q in range(2):
            EV[0, 4 + q:5 + q, :] = column_sum(DPRE[q].astype(F32))

    def own_hidden_back():
        DH1[...] = dot_nt(DPRE[0, mine_rows], W[4]) + dot_nt(DPRE[1, mine_rows], W[6])

    def second_norm_back():
        for k, (lo, hi) in enumerate(cuts):
            arrive(HR.at[lo:hi], xr.at[2 + 3 * k])
        own_back = DH1[...] + HR[...].astype(F32)
        cot = CC[mine_rows].astype(F32)
        EV[0, 1:2, :] = column_sum(own_back * N2[...])
        EV[0, 2:3, :] = column_sum(own_back)
        EV[0, 3:4, :] = column_sum(cot)
        dx1 = cot + norm_back(own_back, ln2_gain, N2[...], R2[...])
        DX1[...] = dx1
        branch = dx1.astype(BF16)
        GO[...] = branch
        EV[0, 0:1, :] = column_sum(branch.astype(F32))
        GOT[...] = GO[...].T

    def store_attention(r):
        g = 4 + r
        for n in range(2):
            cols = slice(n * 256, n * 256 + 256)
            G[g, :, :, :, cols] = dot_nn(H1T[...], DQ[:, cols]).astype(BF16).reshape(4, 2, 96, 256)
        edge = jnp.concatenate(
            [dot_nn(H1T[...], DQ[:, 512:576]), dot_nn(GOT[...], AB[r])], axis=1)
        G[g, :, :, :, 512:768] = edge.astype(BF16).reshape(4, 2, 96, 256)

    def attend_back(r):
        da = dot_nt(GO[...], W[r, 576:768, :])
        phi = PHI[r]
        dnum = da * INV[r]
        drest = -(dnum * ATT[r])
        n_high, n_low = split(dnum)
        d_high, d_low = split(drest)
        s_high, s_low = split(ST[r])
        k_high, k_low = split(TT[r])
        dphi = dot_nt(n_high, s_high) + dot_nt(n_high, s_low) + dot_nt(n_low, s_high)
        dphi += dot_nt(d_high, k_high) + dot_nt(d_high, k_low) + dot_nt(d_low, k_high)
        pad = jnp.zeros((96, 192), F32)
        dstate = jnp.where(head_mask, dot_tn(phi, n_high) + dot_tn(phi, n_low), 0.0)
        dtotal = jnp.where(head_mask, dot_tn(phi, d_high) + dot_tn(phi, d_low), 0.0)
        a_high, a_low = split(jnp.concatenate([pad, dstate[0:96]], axis=0))
        b_high, b_low = split(jnp.concatenate([pad, dtotal[0:96]], axis=0))
        ones = jnp.ones((16, 192), BF16)
        dkey = dot_nt(VV[r], a_high) + dot_nt(VV[r], a_low)
        dkey += (dot_nt(ones, b_high) + dot_nt(ones, b_low))[0:1, :]
        dphi += key_mask * dkey
        dvalue = key_mask * (dot_nn(phi, a_high) + dot_nn(phi, a_low))
        u_high, u_low = split(dphi * EE[r])
        back = dot_nt(u_high, FH[r]) + dot_nt(u_high, FL[r]) + dot_nt(u_low, FH[r])
        back = back * COS[...] - swap_halves(back) * SIN[...]
        DQ[:, 0:384] = back.astype(BF16)
        DQ[:, 384:576] = dvalue.astype(BF16)
        bias_sum = jnp.concatenate([column_sum(DQ[...].astype(F32)), jnp.zeros((1, 192), F32)], axis=1)
        if r == 0:
            LV[0, 2:3, :] = bias_sum
        else:
            EV[0, 5 + r:6 + r, :] = bias_sum
        grad = dot_nn(DQ[...], qkv_rows_of(r))
        if "back" in done:
            DH1[...] += grad
        else:
            DH1[...] = grad
        done.add("back")
        store_attention(r)
        reduce_1(4 + r)

    def small_1(V, k):
        send(V.at[0], V.at[1], vs.at[k, 0], vr.at[k, 0], nc)

    def small_2(V, k):
        arrive(V.at[1], vr.at[k, 0])
        V[2] = V[0] + V[1]
        send(V.at[2], V.at[3], vs.at[k, 1], vr.at[k, 1], nx)

    def small_3(V, k):
        arrive(V.at[3], vr.at[k, 1])
        V[4] = V[2] + V[3]
        send(V.at[4], V.at[5], vs.at[k, 2], vr.at[k, 2], ny)

    def small_4(V, k):
        arrive(V.at[5], vr.at[k, 2])
        V[6] = V[4] + V[5]
        for r in (1, 2, 3):
            send(V.at[6], V.at[6 + r], vs.at[k, 2 + r], vr.at[k, 2 + r], nz[r])

    def small_5(V, k):
        for r in (1, 2, 3):
            arrive(V.at[6 + r], vr.at[k, 2 + r])

    def first_norm_sums():
        first_back = DH1[...]
        LV[0, 0:1, :] = column_sum(first_back * N1[...])
        LV[0, 1:2, :] = column_sum(first_back)
        small_1(LV, 1)

    def input_grad():
        gx_ref[...] = (DX1[...] + norm_back(DH1[...], ln1_gain, N1[...], R1[...]))[0:live]
        give(1)

    def layer_output():
        output = dot_nn(ACT[0, mine_rows], W[5]) + dot_nn(ACT[1, mine_rows], W[7])
        arrive(OR, xr.at[3])
        output = X1[...] + output + OR[...].astype(F32) + b_down
        y_ref[...] = output[0:live].astype(BF16)
        give(0)

    def down_done():
        gd_ref[...] += landed(1)
        give(5)

    def up_done():
        gu_ref[...] += landed(3)
        give(4)

    def attention_done():
        block = BL[...]
        for r in (1, 2, 3):
            block = block + landed(4 + r)
        gq_ref[...] = jnp.concatenate(
            [block[:, s * 192 + h * 64:s * 192 + h * 64 + 64] for h in range(3) for s in range(3)], axis=1)
        give(2)
        go_ref[...] = block[:, 576:768].T
        give(3)

    gather_a(1, 0)
    forward(1, 3, 2, 0)
    gather_a(second_rank, 0)
    forward(3, 1, 2, 0)
    gather_a(1, 1)
    forward(1, 3, 2, 1)
    share_down()
    gather_a(second_rank, 1)
    forward(3, 1, 2, 1)
    gather_x(1, 0)
    gather_y(1, 0)
    gather_a(third_rank, 0)
    forward(2, 1, 3, 0)
    gather_y(1, 1)
    gather_a(third_rank, 1)
    forward(2, 1, 3, 1)
    share_small()
    attend_first()
    gather_x(second_rank, 0)
    gather_x(1, 1)
    share_up()
    gather_x(third_rank, 0)
    gather_y(third_rank, 0)
    gather_y(second_rank, 0)
    gather_y(second_rank, 1)
    gather_y(third_rank, 1)
    gather_a(7)
    gather_small(1)
    gather_x(second_rank, 1)
    gather_x(third_rank, 1)
    gather_small(2)
    gather_c(1)
    gather_small(3)
    share_cotangent()
    gather_c(second_rank)
    attend_next(1)
    attend_next(second_rank)
    gather_a(6)
    gather_c(third_rank)
    attend_next(third_rank)
    gather_y(7)
    second_norm(0)
    gather_x(7)
    second_norm(1)
    gather_y(6)
    gather_x(6)
    back_hidden(0)
    feed(0)
    gather_c(7)
    transpose_rows()
    feed(0, 0)
    gather_c(6)
    back_hidden(1)
    feed(1)
    feed(1, 0)
    hidden_back(0)
    feed(1, 1)
    store_block(3)
    store_block(1)
    feed(0, 1)
    hidden_back(1)
    reduce_2(3)
    own_hidden_back()
    reduce_2(1)
    store_block(2)
    hidden_out()
    reduce_3(3)
    reduce_2(2)
    second_norm_back()
    attend_back(2)
    reduce_3(1)
    reduce_4(3)
    attend_back(3)
    reduce_2(6)
    attend_back(1)
    reduce_2(7)
    reduce_4(1)
    small_1(EV, 0)
    store_block(0)
    reduce_3(6)
    small_2(EV, 0)
    attend_back(0)
    reduce_2(5)
    reduce_4(6)
    small_3(EV, 0)
    first_norm_sums()
    reduce_3(7)
    reduce_3(5)
    reduce_2(4)
    small_2(LV, 1)
    reduce_2(0)
    layer_output()
    small_4(EV, 0)
    reduce_4(5)
    reduce_3(2)
    input_grad()
    reduce_4(7)
    small_3(LV, 1)
    reduce_3(0)
    reduce_3(4)
    small_4(LV, 1)
    reduce_4(4)
    reduce_4(0)
    reduce_4(2)
    small_5(EV, 0)
    down_done()
    up_done()
    attention_done()
    small_5(LV, 1)

    sv_ref[0:2, :] = LV[6, 0:2, :] + LV[7, 0:2, :] + LV[8, 0:2, :] + LV[9, 0:2, :]
    sv_ref[2:6, :] = EV[6, 0:4, :] + EV[7, 0:4, :] + EV[8, 0:4, :] + EV[9, 0:4, :]
    sv_ref[6:7, :] = EV[6, 4:5, :] + EV[8, 5:6, :]
    bias = LV[6, 2:3, :] + EV[7, 6:7, :] + EV[8, 7:8, :] + EV[9, 8:9, :]
    bias = [bias[:, s * 192 + h * 64:s * 192 + h * 64 + 64] for h in range(3) for s in range(3)]
    sv_ref[7:8, :] = jnp.concatenate(bias + [jnp.zeros((1, 192), F32)], axis=1)
    give(6)
    for copy in sends:
        copy.wait_send()
    for condition, copy in late_sends:
        pl.when(condition)(copy.wait_send)
    for copy in gives:
        copy.wait()


def write_outputs(y, gx, gq, go, gu, gd, sv, *outs):
    refs = (y, gx, gq, go, gu, gd)
    for source, target in zip(refs, outs[:6]):
        target[...] = source[...]
    for i, target in enumerate(outs[6:13]):
        target[...] = sv[i:i + 1, :].reshape(768)
    outs[13][...] = sv[7:8, 0:576].reshape(576)


def trig_table(live, rows, head_dim):
    half = head_dim // 2
    freq = (10000.0 ** (-np.arange(half, dtype=np.float32) * 2.0 / head_dim)).astype(np.float32)
    angle = (np.arange(rows, dtype=np.float32)[:, None] * freq[None, :]).astype(np.float64)
    cosine, sine = np.cos(angle), np.sin(angle)
    table = np.concatenate([cosine, cosine, -sine, sine], axis=1) * head_dim ** (-0.25)
    return table.astype(np.float32)


def local(
    n_dp, layer_input, lengths, ln1_gain, ln1_bias, w_qkv, b_qkv, features, w_out, b_out,
    ln2_gain, ln2_bias, w_up, b_up, w_down, b_down, cotangent,
):
    live, width = layer_input.shape
    rows = -(-live // 16) * 16
    trig = jnp.asarray(trig_table(live, rows, features.shape[1]))
    vmem = pl.BlockSpec(memory_space=pltpu.VMEM)
    anywhere = pl.BlockSpec(memory_space=pl.ANY)
    dma = pltpu.SemaphoreType.DMA

    def buf(*shape):
        return pltpu.VMEM(shape, BF16)

    def wide(*shape):
        return pltpu.VMEM(shape, F32)

    outs = pl.pallas_call(
        functools.partial(layer_kernel, live),
        out_shape=[
            jax.ShapeDtypeStruct((live, width), BF16),
            jax.ShapeDtypeStruct((live, width), F32),
            jax.ShapeDtypeStruct((96, 576), F32),
            jax.ShapeDtypeStruct((192, 96), F32),
            jax.ShapeDtypeStruct((96, 768), F32),
            jax.ShapeDtypeStruct((96, 768), F32),
            jax.ShapeDtypeStruct((8, 768), F32),
        ],
        in_specs=[anywhere] * 17,
        out_specs=[anywhere] * 7,
        scratch_shapes=[
            buf(live, width), buf(live, width), pltpu.SMEM(lengths.shape, jnp.int32)] + [
            wide(width) for _ in range(6)] + [
            wide(*b_up.shape), wide(*b_qkv.shape), wide(features.shape[0], features.shape[2], features.shape[1]),
            wide(*trig.shape), buf(live, width), wide(live, width), wide(96, 576), wide(192, 96),
            wide(96, 768), wide(96, 768), wide(8, 768),
            buf(8, 768, 768), wide(4, 80, 128), buf(2 * rows, 768), buf(2 * rows, 768),
            buf(768, 2 * rows), buf(768, 2 * rows), buf(rows, 768), buf(768, rows),
            buf(rows, 768), buf(768, rows), wide(rows, 768), wide(rows, 1), wide(rows, 768),
            wide(rows, 768), wide(rows, 1), wide(rows, 768), wide(rows, 768),
            wide(rows, 384), wide(rows, 384), buf(4, 384, 192), buf(4, 384, 192),
            buf(4, rows, 192), wide(4, rows, 192), buf(4, rows, 192), wide(4, rows, 192),
            wide(4, rows, 192), buf(4, rows, 192), wide(4, 192, 192), wide(4, 192, 192),
            wide(2, 2 * rows, 768), buf(2, 2 * rows, 768), buf(2, 2 * rows, 768), buf(rows, 576),
            buf(rows, 768), buf(rows, 768), buf(rows, 768), buf(rows, 768),
            buf(8, 4, 2, 96, 768), buf(8, 4, 96, 768), buf(8, 2, 48, 768), buf(8, 2, 48, 768),
            buf(8, 2, 48, 768), buf(8, 2, 48, 768), buf(8, 96, 768), buf(8, 96, 768), wide(96, 768),
            wide(10, 16, 768), wide(10, 8, 768),
            dma((4,)), dma((13,)), dma((7,)), dma((32,)), dma((8,)), dma((8, 16)), dma((8, 16)), dma((6,)), dma((6,)),
            dma((8, 8)), dma((8, 8)), dma((2, 6)), dma((2, 6)),
        ],
        compiler_params=pltpu.CompilerParams(
            collective_id=0, has_side_effects=True, vmem_limit_bytes=67043328),
    )(
        layer_input, cotangent, lengths, ln1_gain, ln1_bias, b_out, ln2_gain, ln2_bias, b_down,
        b_up, b_qkv, features.transpose(0, 2, 1), trig, w_qkv.T, w_out, w_up, w_down)
    outs = pl.pallas_call(
        write_outputs,
        out_shape=[jax.ShapeDtypeStruct(out.shape, out.dtype) for out in outs[:6]]
        + [jax.ShapeDtypeStruct((width,), F32)] * 7 + [jax.ShapeDtypeStruct((576,), F32)],
        in_specs=[vmem] * 7,
        out_specs=[vmem] * 14,
    )(*outs)
    output, grad_x, qkv_piece, out_piece, up_piece, down_piece, *common, up_bias, qkv_bias = outs
    down_piece = down_piece.T
    if n_dp != GROUP:
        member = lax.axis_index("dp") % GROUP

        def spread(piece, axis):
            shape = list(piece.shape)
            shape[axis] = shape[axis] * GROUP
            start = [0, 0]
            start[axis] = member * piece.shape[axis]
            whole = lax.dynamic_update_slice(jnp.zeros(shape, F32), piece, start)
            return lax.psum_scatter(whole, "dp", scatter_dimension=axis, tiled=True)

        qkv_piece, out_piece = spread(qkv_piece, 0), spread(out_piece, 1)
        up_piece, down_piece = spread(up_piece, 0), spread(down_piece, 1)
        common, up_bias, qkv_bias = jax.tree.map(
            lambda part: lax.psum(part, "dp") / GROUP, (common, up_bias, qkv_bias))
    return (
        output, grad_x, common[0], common[1], qkv_piece, qkv_bias, out_piece, common[2],
        common[3], common[4], up_piece, up_bias, down_piece, common[5],
    )


def solution(mesh):
    rows, cols = P(("dp", "mp"), None), P(None, "mp")
    placed = (
        rows, P("dp"), P(), P(), cols, P("mp"), P("mp", None, None), P("mp", None), P(),
        P(), P(), cols, P("mp"), P("mp", None), P(), rows,
    )
    return jax.shard_map(
        functools.partial(local, mesh.shape["dp"]),
        mesh=mesh,
        in_specs=placed,
        out_specs=(
            rows, rows, P(), P(), P("dp", "mp"), P("mp"), P("mp", "dp"), P(),
            P(), P(), P("dp", "mp"), P("mp"), P("mp", "dp"), P(),
        ),
        check_vma=False,
    )
```

```python
import functools

import jax
import jax.numpy as jnp
import numpy as np
from jax import lax
from jax.experimental import pallas as pl
from jax.experimental.pallas import tpu as pltpu
from jax.sharding import PartitionSpec as P

MESH = pl.DeviceIdType.MESH
BF16 = jnp.bfloat16
F32 = jnp.float32
EPSILON = 1e-05
GROUP = 8


def dot_nn(left, right):
    return lax.dot_general(left, right, (((1,), (0,)), ((), ())), preferred_element_type=F32)


def dot_nt(left, right):
    return lax.dot_general(left, right, (((1,), (1,)), ((), ())), preferred_element_type=F32)


def dot_tn(left, right):
    return lax.dot_general(left, right, (((0,), (0,)), ((), ())), preferred_element_type=F32)


def split(values):
    high = values.astype(BF16)
    return high, (values - high.astype(F32)).astype(BF16)


def normalize(values):
    centred = values - jnp.mean(values, axis=-1, keepdims=True)
    factor = lax.rsqrt(jnp.mean(centred * centred, axis=-1, keepdims=True) + EPSILON)
    return centred * factor, factor


def norm_back(grad, gain, normed, factor):
    hat = grad * gain
    return factor * (
        hat
        - jnp.mean(hat, axis=-1, keepdims=True)
        - normed * jnp.mean(hat * normed, axis=-1, keepdims=True)
    )


def column_sum(values):
    return jnp.sum(values, axis=0, keepdims=True)


def swap_halves(values):
    width = values.shape[1]
    lane = lax.broadcasted_iota(jnp.int32, values.shape, 1)
    return jnp.where(lane % 64 < 32, pltpu.roll(values, width - 32, 1), pltpu.roll(values, 32, 1))


def layer_kernel(live, *refs):
    (
        wqkv_ref, wout_ref, wup_ref, wdown_ref,
        x_ref, c_ref, len_ref, ln1_gain_ref, ln1_bias_ref, b_out_ref, ln2_gain_ref, ln2_bias_ref,
        b_down_ref, b_up_ref, b_qkv_ref, feat_ref, trig_ref,
        y_ref, gx_ref, gq_ref, go_ref, gu_ref, gd_ref, sv_ref,
        W, SP, CC, H2, CT, H2T, H1, H1T, GO, GOT, N1, R1, X1, N2, R2, DX1, DH1,
        COS, SIN, FH, FL, PHI, EE, VV, ATT, INV, AB, ST, TT, DA, ACT, DPRE, DQ,
        OS, OR, HS, HR, G, Q0, QX, QY, T2, Q2, U, ZR, VS, VR, BL, EV, LV,
        local_sem, in_sem, out_sem, zs, zr, ags, agr, xs, xr, rs, rr, vs, vr,
    ) = refs[13:17] + refs[24:]
    rows = CC.shape[0] // 2
    dp = lax.axis_index("dp")
    z = lax.axis_index("mp")
    member = dp % GROUP
    c = member % 2
    bx = (member // 2) % 2
    by = member // 4
    nx = (dp + 2 - 4 * bx, z)
    ny = (dp + 4 - 8 * by, z)
    nc = (dp + 1 - 2 * c, z)
    nz = (None, (dp, z + 1 - 2 * (z % 2)), (dp, (z + 2) % 4), (dp, 3 - z))

    def place(yy, xx, cc):
        return pl.multiple_of((yy * 4 + xx * 2 + cc) * 96, 96)

    sends = []
    done = set()

    def once(key, action, *args):
        if key not in done:
            done.add(key)
            action(*args)

    def send(src, dst, send_sem, recv_sem, device):
        copy = pltpu.make_async_remote_copy(
            src_ref=src, dst_ref=dst, send_sem=send_sem, recv_sem=recv_sem,
            device_id=device, device_id_type=MESH,
        )
        copy.start()
        sends.append(copy)

    def arrive(dst, recv_sem):
        pltpu.make_async_remote_copy(
            src_ref=dst, dst_ref=dst, send_sem=recv_sem, recv_sem=recv_sem,
            device_id=nc, device_id_type=MESH,
        ).wait_recv()

    barrier = pltpu.get_barrier_semaphore()
    for device in (nx, ny, nc, nz[1], nz[2], nz[3]):
        pl.semaphore_signal(barrier, inc=1, device_id=device, device_id_type=MESH)

    takes = [
        pltpu.make_async_copy(source, target, in_sem.at[i])
        for i, (source, target) in enumerate(zip(refs[:13], refs[24:37]))
    ]
    for take in takes:
        take.start()
    gives = []

    def give(i):
        copy = pltpu.make_async_copy(refs[37 + i], refs[17 + i], out_sem.at[i])
        copy.start()
        gives.append(copy)

    loads = [
        pltpu.make_async_copy(source, target, local_sem.at[i])
        for i, (source, target) in enumerate((
            (wqkv_ref, W.at[0, 0:576]), (wout_ref, W.at[0, 576:768]),
            (wup_ref, W.at[4]), (wdown_ref, W.at[5])))
    ]
    for load in loads:
        load.start()

    pl.semaphore_wait(barrier, 6)

    own = pl.ds(place(by, bx, c), 96)
    inner = jnp.logical_or(z == 1, z == 2)
    second_rank = jnp.where(inner, 3, 2)
    third_rank = jnp.where(inner, 2, 3)

    def send_if(condition, src, dst, send_sem, recv_sem, device):
        copy = pltpu.make_async_remote_copy(
            src_ref=src, dst_ref=dst, send_sem=send_sem, recv_sem=recv_sem,
            device_id=device, device_id_type=MESH,
        )

        @pl.when(condition)
        def _():
            copy.start()

        late_sends.append((condition, copy))

    late_sends = []
    in_qkv = member < 6
    out_rows = pl.ds(pl.multiple_of(jnp.maximum(own.start - 576, 0), 96), 96)
    qkv_rows = pl.ds(pl.multiple_of(jnp.minimum(own.start, 480), 96), 96)
    for r, condition in ((1, None), (3, inner)):
        for h in (0, 1):
            here = pl.ds(pl.multiple_of(own.start + 48 * h, 48), 48)
            for part, ref, start in ((in_qkv, wqkv_ref, qkv_rows.start), (jnp.logical_not(in_qkv), wout_ref, out_rows.start)):
                both = part if condition is None else jnp.logical_and(part, condition)
                source = ref.at[pl.ds(pl.multiple_of(start + 48 * h, 48), 48)]
                send_if(both, source, W.at[r, here], zs.at[r + 16 * h], agr.at[r, h], nz[r])
    half = pl.ds(pl.multiple_of(c * 40, 8), 40)
    other_half = pl.ds(pl.multiple_of((1 - c) * 40, 8), 40)

    for take in takes:
        take.wait()
    SP[0, 0:64, 0:96] = feat_ref[...].reshape(96, 64).T
    qkv_bias = b_qkv_ref[...].reshape(1, 576)
    qkv_bias = jnp.concatenate(
        [qkv_bias[:, h * 192 + s * 64:h * 192 + s * 64 + 64] for s in range(3) for h in range(3)]
        + [jnp.zeros((1, 64), F32)], axis=1)
    for i in range(5):
        SP[0, 64 + i:65 + i, :] = qkv_bias[:, i * 128:i * 128 + 128]
    up_bias = b_up_ref[...].reshape(1, 768)
    for i in range(6):
        SP[0, 72 + i:73 + i, :] = up_bias[:, i * 128:i * 128 + 128]
    CC[0:rows, :] = jnp.concatenate([c_ref[...].astype(F32), jnp.zeros((rows - live, 768), F32)], axis=0).astype(BF16)

    def forward(b, to_rank, slot, h):
        here = pl.ds(pl.multiple_of(own.start + 48 * h, 48), 48)
        send_if(inner, W.at[b, here], W.at[slot, here], zs.at[3 + slot + to_rank + 16 * h], agr.at[slot, h], nz[to_rank])

    at_d = pl.ds(place(1 - by, 1 - bx, c), 96)
    at_x0 = pl.ds(place(by, 1 - bx, c), 48)
    at_y1 = pl.ds(pl.multiple_of(place(1 - by, bx, c) + 48, 48), 48)
    at_d0 = pl.ds(place(1 - by, 1 - bx, c), 48)
    at_d1 = pl.ds(pl.multiple_of(place(1 - by, 1 - bx, c) + 48, 48), 48)

    def rows_at(yy, xx, cc, h):
        start = place(yy, xx, cc)
        return pl.ds(start, 96) if h is None else pl.ds(pl.multiple_of(start + 48 * h, 48), 48)

    def halves(b):
        return (None,) if isinstance(b, int) and b > 1 else (0, 1)

    def gather_a(b, h=None):
        k = h or 0
        part = W.at[b, rows_at(by, bx, c, h)]
        arrive(part, agr.at[b, k])
        send(part, part, ags.at[b, k], agr.at[b, 2 + k], nx)
        send(part, part, ags.at[b, 2 + k], agr.at[b, 4 + k], ny)
        send(part, part, ags.at[b, 4 + k], agr.at[b, 6 + k], nc)

    def gather_x(b, h=None):
        k = h or 0
        part = W.at[b, rows_at(by, 1 - bx, c, h)]
        arrive(part, agr.at[b, 2 + k])
        if h != 1:
            send(W.at[b, at_x0], W.at[b, at_x0], ags.at[b, 6], agr.at[b, 14], ny)
        send(part, part, ags.at[b, 8 + k], agr.at[b, 8 + k], nc)

    def gather_y(b, h=None):
        k = h or 0
        part = W.at[b, rows_at(1 - by, bx, c, h)]
        arrive(part, agr.at[b, 4 + k])
        if h != 0:
            send(W.at[b, at_y1], W.at[b, at_y1], ags.at[b, 7], agr.at[b, 15], nx)
        send(part, part, ags.at[b, 10 + k], agr.at[b, 10 + k], nc)

    def gather_c(b):
        arrive(W.at[b, at_d0], agr.at[b, 14])
        arrive(W.at[b, at_d1], agr.at[b, 15])
        send(W.at[b, at_d], W.at[b, at_d], ags.at[b, 12], agr.at[b, 12], nc)

    def gather_small(r):
        arrive(SP.at[r, half], zr.at[r])
        send(SP.at[r, half], SP.at[r, half], zs.at[12 + r], zr.at[4 + r], nc)

    def small_done(r):
        arrive(SP.at[r, other_half], zr.at[4 + r])

    def qkv_rows_of(r):
        return jnp.concatenate(
            [W[r, h * 192 + s * 64:h * 192 + s * 64 + 64, :] for s in range(3) for h in range(3)], axis=0)

    def gather_d(b):
        for n, (yy, xx) in enumerate(((by, bx), (by, 1 - bx), (1 - by, bx))):
            for h in halves(b):
                arrive(W.at[b, rows_at(yy, xx, 1 - c, h)], agr.at[b, 6 + 2 * n + (h or 0)])
        arrive(W.at[b, rows_at(1 - by, 1 - bx, 1 - c, None)], agr.at[b, 12])

    rank = (0, 2, 0, 2, 0, 1, 2, 3)
    kept = {0: gd_ref, 2: gu_ref, 4: BL}

    def reduce_1(g):
        send(G.at[g, :, 1 - c], Q0.at[g], rs.at[g, 0], rr.at[g, 0], nc)

    def reduce_2(g):
        arrive(Q0.at[g], rr.at[g, 0])
        for i in range(4):
            Q0[g, i] = (Q0[g, i].astype(F32) + G[g, i, c].astype(F32)).astype(BF16)
        for i in range(2):
            send(Q0.at[g, 2 * i + 1 - bx, 0:48], QX.at[g, i], rs.at[g, 1 + i], rr.at[g, 1 + i], nx)
            send(Q0.at[g, 2 * (1 - by) + i, 48:96], QY.at[g, i], rs.at[g, 3 + i], rr.at[g, 3 + i], ny)

    def reduce_3(g):
        for i in range(2):
            arrive(QX.at[g, i], rr.at[g, 1 + i])
            arrive(QY.at[g, i], rr.at[g, 3 + i])
        T2[g, 0] = (Q0[g, 2 * (1 - by) + bx, 0:48].astype(F32) + QX[g, 1 - by].astype(F32)).astype(BF16)
        T2[g, 1] = (Q0[g, 2 * by + 1 - bx, 48:96].astype(F32) + QY[g, 1 - bx].astype(F32)).astype(BF16)
        send(T2.at[g, 0], Q2.at[g, 0], rs.at[g, 5], rr.at[g, 5], ny)
        send(T2.at[g, 1], Q2.at[g, 1], rs.at[g, 6], rr.at[g, 6], nx)

    def reduce_4(g):
        arrive(Q2.at[g, 0], rr.at[g, 5])
        arrive(Q2.at[g, 1], rr.at[g, 6])
        mine = 2 * by + bx
        first = Q0[g, mine, 0:48].astype(F32) + QX[g, by].astype(F32) + Q2[g, 0].astype(F32)
        second = Q0[g, mine, 48:96].astype(F32) + QY[g, bx].astype(F32) + Q2[g, 1].astype(F32)
        total = jnp.concatenate([first, second], axis=0)
        if rank[g] == 0:
            kept[g][...] = total
        else:
            U[g] = total.astype(BF16)
            if g < 4:
                send(U.at[g], ZR.at[g], rs.at[g, 7], rr.at[g, 7], nz[rank[g]])
            else:
                send_if(jnp.logical_not(inner), U.at[g], ZR.at[g], rs.at[g, 7], rr.at[g, 7], nz[1])

    def chain(g):
        source, landing, target, there, device = {
            7: (ZR.at[6], rr.at[6, 7], VR.at[0], rr.at[4, 7], nz[3]),
            6: (ZR.at[7], rr.at[7, 7], VR.at[1], rr.at[0, 7], nz[3]),
            5: (VR.at[1], rr.at[0, 7], ZR.at[5], rr.at[5, 7], nz[1]),
        }[g]

        @pl.when(inner)
        def _():
            arrive(source, landing)
            VS[g - 5] = (source[...].astype(F32) + U[g].astype(F32)).astype(BF16)

        send_if(inner, VS.at[g - 5], target, rs.at[g, 7], there, device)

    def landed(g):
        arrive(ZR.at[g], rr.at[g, 7])
        return ZR[g].astype(F32)

    ln1_gain, ln1_bias, b_out, ln2_gain, ln2_bias, b_down = (
        ref[...].reshape(1, 768)
        for ref in (ln1_gain_ref, ln1_bias_ref, b_out_ref, ln2_gain_ref, ln2_bias_ref, b_down_ref))
    position = lax.broadcasted_iota(jnp.int32, (rows, 1), 0)
    key_mask = (position < len_ref[z]).astype(F32)
    trig = trig_ref[...]
    COS[...] = jnp.concatenate([trig[:, 0:64]] * 6, axis=1)
    SIN[...] = jnp.concatenate([trig[:, 64:128]] * 6, axis=1)
    row_q = lax.broadcasted_iota(jnp.int32, (192, 192), 0)
    col_q = lax.broadcasted_iota(jnp.int32, (192, 192), 1)
    head_mask = jnp.logical_and(row_q < 96, row_q // 32 == col_q // 64)
    row_f = lax.broadcasted_iota(jnp.int32, (384, 192), 0)
    col_f = lax.broadcasted_iota(jnp.int32, (384, 192), 1)
    feat_mask = row_f // 64 == col_f // 32

    X1[...] = jnp.concatenate([x_ref[...].astype(F32), jnp.zeros((rows - live, 768), F32)], axis=0)
    normed, factor = normalize(X1[...])
    N1[...] = normed
    R1[...] = factor
    first = (normed * ln1_gain + ln1_bias).astype(BF16)
    H1[...] = first

    def attend(r):
        bias = jnp.concatenate([SP[r, 64 + i:65 + i, :] for i in range(5)], axis=1)[:, 0:576]
        projected = dot_nt(H1[...], qkv_rows_of(r)) + bias
        both = projected[:, 0:384]
        value = projected[:, 384:576].astype(BF16)
        turned = both * COS[...] + swap_halves(both) * SIN[...]
        plain = SP[r, 0:64, :][:, 0:96]
        plain = jnp.concatenate([plain, plain], axis=1)
        block = jnp.where(feat_mask, jnp.concatenate([plain] * 6, axis=0), 0.0)
        f_high, f_low = split(block)
        FH[r] = f_high
        FL[r] = f_low
        t_high, t_low = split(turned)
        u = dot_nn(t_high, f_high) + dot_nn(t_high, f_low) + dot_nn(t_low, f_high)
        decay = jnp.exp(jnp.minimum(u, 0.0))
        EE[r] = decay
        phi32 = jnp.where(u > 0.0, u + 1.0, decay)
        phi = phi32.astype(BF16)
        PHI[r] = phi
        VV[r] = value
        masked = (phi.astype(F32) * key_mask).astype(BF16)
        pad = jnp.zeros((96, 192), F32)
        state = jnp.concatenate([dot_tn(masked, value)[96:192], pad], axis=0)
        total = jnp.concatenate([dot_tn(masked, jnp.ones((rows, 192), BF16))[96:192], pad], axis=0)
        state = jnp.where(head_mask, state, 0.0)
        total = jnp.where(head_mask, total, 0.0)
        ST[r] = state
        TT[r] = total
        s_high, s_low = split(state)
        k_high, k_low = split(total)
        numer = dot_nn(phi, s_high) + dot_nn(phi, s_low)
        inverse = 1.0 / (dot_nn(phi, k_high) + dot_nn(phi, k_low))
        attended = numer * inverse
        ATT[r] = attended
        INV[r] = inverse
        mixed = attended.astype(BF16)
        AB[r] = mixed
        X1[...] += dot_nn(mixed, W[r, 576:768, :])

    theirs = pl.ds(rows, rows)
    mine_rows = pl.ds(0, rows)
    up = (4, 6)
    down = (5, 7)
    EV[0, 9:16, :] = jnp.zeros((7, 768), F32)
    LV[0, 3:8, :] = jnp.zeros((5, 768), F32)

    def share_small():
        for r in (1, 2, 3):
            send(SP.at[0, half], SP.at[r, half], zs.at[8 + r], zr.at[r], nz[r])

    def share_up():
        send(wup_ref.at[own], W.at[6, own], zs.at[2], agr.at[6, 0], nz[2])

    def share_down():
        send(wdown_ref.at[own], W.at[7, own], zs.at[0], agr.at[7, 0], nz[2])

    def share_cotangent():
        send(CC.at[0:rows], CC.at[rows:2 * rows], xs.at[0], xr.at[0], nz[1])

    def whole(b):
        for r in (2, 3) if b is second_rank or b is third_rank else (1,) if b == 1 else (2,):
            once(("small", r), small_done, r)
        gather_d(b)

    def loaded(i):
        once(("load", i), loads[i].wait)

    def cotangent_here():
        once("cotangent", arrive, CC.at[rows:2 * rows], xr.at[0])

    cuts = ((0, 96), (96, rows))

    def second_here(k):
        lo, hi = cuts[k]
        once(("second", k), arrive, H2.at[rows + lo:rows + hi], xr.at[1 + 3 * k])

    def attend_first():
        loaded(0)
        loaded(1)
        attend(0)

    def attend_next(b):
        whole(b)
        attend(b)

    def second_norm(k):
        lo, hi = cuts[k]
        middle = X1[lo:hi] + b_out
        X1[lo:hi] = middle
        normed, factor = normalize(middle)
        N2[lo:hi] = normed
        R2[lo:hi] = factor
        H2[lo:hi, :] = (normed * ln2_gain + ln2_bias).astype(BF16)
        send(H2.at[lo:hi], H2.at[rows + lo:rows + hi], xs.at[1 + 3 * k], xr.at[1 + 3 * k], nz[1])

    def back_hidden(q):
        cotangent_here()
        if q == 0:
            loaded(3)
        else:
            gather_d(7)
        DA[q] = dot_nt(CC[...], W[down[q]])

    def feed(q, k=None):
        lo, hi = 0, rows
        if k is not None:
            second_here(k)
            lo, hi = rows + cuts[k][0], rows + cuts[k][1]
        if q == 0:
            loaded(2)
        else:
            once("up", whole, 6)
        part = pl.ds(lo, hi - lo)
        bias = jnp.concatenate([SP[2 * q, 72 + i:73 + i, :] for i in range(6)], axis=1)
        pre = dot_nn(H2[part], W[up[q]]) + bias
        half = 0.5 * (1.0 + lax.erf(pre * (0.5 ** 0.5)))
        ACT[q, part] = (pre * half).astype(BF16)
        slope = half + pre * jnp.exp(-0.5 * pre * pre) * (0.5 / np.pi) ** 0.5
        DPRE[q, part] = (DA[q, part] * slope).astype(BF16)

    def transpose_rows():
        cotangent_here()
        CT[...] = CC[...].T
        H1T[...] = H1[...].T

    def transpose_second():
        H2T[...] = H2[...].T

    def store_block(g):
        q = g % 2
        if g >= 2:
            once("turned", transpose_second)
        for n in range(3):
            cols = slice(n * 256, n * 256 + 256)
            if g < 2:
                block = dot_nn(CT[...], ACT[q, :, cols])
            else:
                block = dot_nn(H2T[...], DPRE[q, :, cols])
            G[g, :, :, :, cols] = block.astype(BF16).reshape(4, 2, 96, 256)
        reduce_1(g)

    def hidden_back(k):
        lo, hi = cuts[k]
        part = pl.ds(rows + lo, hi - lo)
        HS[lo:hi] = (dot_nt(DPRE[0, part], W[4]) + dot_nt(DPRE[1, part], W[6])).astype(BF16)
        send(HS.at[lo:hi], HR.at[lo:hi], xs.at[2 + 3 * k], xr.at[2 + 3 * k], nz[1])

    def hidden_out():
        OS[...] = (dot_nn(ACT[0, theirs], W[5]) + dot_nn(ACT[1, theirs], W[7])).astype(BF16)
        send(OS, OR, xs.at[3], xr.at[3], nz[1])
        for q in range(2):
            EV[0, 4 + q:5 + q, :] = column_sum(DPRE[q].astype(F32))

    def own_hidden_back():
        DH1[...] = dot_nt(DPRE[0, mine_rows], W[4]) + dot_nt(DPRE[1, mine_rows], W[6])

    def second_norm_back():
        for k, (lo, hi) in enumerate(cuts):
            arrive(HR.at[lo:hi], xr.at[2 + 3 * k])
        own_back = DH1[...] + HR[...].astype(F32)
        cot = CC[mine_rows].astype(F32)
        EV[0, 1:2, :] = column_sum(own_back * N2[...])
        EV[0, 2:3, :] = column_sum(own_back)
        EV[0, 3:4, :] = column_sum(cot)
        dx1 = cot + norm_back(own_back, ln2_gain, N2[...], R2[...])
        DX1[...] = dx1
        branch = dx1.astype(BF16)
        GO[...] = branch
        EV[0, 0:1, :] = column_sum(branch.astype(F32))
        GOT[...] = GO[...].T

    def store_attention(r):
        g = 4 + r
        for n in range(2):
            cols = slice(n * 256, n * 256 + 256)
            G[g, :, :, :, cols] = dot_nn(H1T[...], DQ[:, cols]).astype(BF16).reshape(4, 2, 96, 256)
        edge = jnp.concatenate(
            [dot_nn(H1T[...], DQ[:, 512:576]), dot_nn(GOT[...], AB[r])], axis=1)
        G[g, :, :, :, 512:768] = edge.astype(BF16).reshape(4, 2, 96, 256)

    def attend_back(r):
        da = dot_nt(GO[...], W[r, 576:768, :])
        phi = PHI[r]
        dnum = da * INV[r]
        drest = -(dnum * ATT[r])
        n_high, n_low = split(dnum)
        d_high, d_low = split(drest)
        s_high, s_low = split(ST[r])
        k_high, k_low = split(TT[r])
        dphi = dot_nt(n_high, s_high) + dot_nt(n_high, s_low) + dot_nt(n_low, s_high)
        dphi += dot_nt(d_high, k_high) + dot_nt(d_high, k_low) + dot_nt(d_low, k_high)
        pad = jnp.zeros((96, 192), F32)
        dstate = jnp.where(head_mask, dot_tn(phi, n_high) + dot_tn(phi, n_low), 0.0)
        dtotal = jnp.where(head_mask, dot_tn(phi, d_high) + dot_tn(phi, d_low), 0.0)
        a_high, a_low = split(jnp.concatenate([pad, dstate[0:96]], axis=0))
        b_high, b_low = split(jnp.concatenate([pad, dtotal[0:96]], axis=0))
        ones = jnp.ones((16, 192), BF16)
        dkey = dot_nt(VV[r], a_high) + dot_nt(VV[r], a_low)
        dkey += (dot_nt(ones, b_high) + dot_nt(ones, b_low))[0:1, :]
        dphi += key_mask * dkey
        dvalue = key_mask * (dot_nn(phi, a_high) + dot_nn(phi, a_low))
        u_high, u_low = split(dphi * EE[r])
        back = dot_nt(u_high, FH[r]) + dot_nt(u_high, FL[r]) + dot_nt(u_low, FH[r])
        back = back * COS[...] - swap_halves(back) * SIN[...]
        DQ[:, 0:384] = back.astype(BF16)
        DQ[:, 384:576] = dvalue.astype(BF16)
        bias_sum = jnp.concatenate([column_sum(DQ[...].astype(F32)), jnp.zeros((1, 192), F32)], axis=1)
        if r == 0:
            LV[0, 2:3, :] = bias_sum
        else:
            EV[0, 5 + r:6 + r, :] = bias_sum
        grad = dot_nn(DQ[...], qkv_rows_of(r))
        if "back" in done:
            DH1[...] += grad
        else:
            DH1[...] = grad
        done.add("back")
        store_attention(r)
        reduce_1(4 + r)

    def small_1(V, k):
        send(V.at[0], V.at[1], vs.at[k, 0], vr.at[k, 0], nc)

    def small_2(V, k):
        arrive(V.at[1], vr.at[k, 0])
        V[2] = V[0] + V[1]
        send(V.at[2], V.at[3], vs.at[k, 1], vr.at[k, 1], nx)

    def small_3(V, k):
        arrive(V.at[3], vr.at[k, 1])
        V[4] = V[2] + V[3]
        send(V.at[4], V.at[5], vs.at[k, 2], vr.at[k, 2], ny)

    def small_4(V, k):
        arrive(V.at[5], vr.at[k, 2])
        V[6] = V[4] + V[5]
        for r in (1, 2, 3):
            send(V.at[6], V.at[6 + r], vs.at[k, 2 + r], vr.at[k, 2 + r], nz[r])

    def small_5(V, k):
        for r in (1, 2, 3):
            arrive(V.at[6 + r], vr.at[k, 2 + r])

    def first_norm_sums():
        first_back = DH1[...]
        LV[0, 0:1, :] = column_sum(first_back * N1[...])
        LV[0, 1:2, :] = column_sum(first_back)
        small_1(LV, 1)

    def input_grad():
        gx_ref[...] = (DX1[...] + norm_back(DH1[...], ln1_gain, N1[...], R1[...]))[0:live]
        give(1)

    def layer_output():
        output = dot_nn(ACT[0, mine_rows], W[5]) + dot_nn(ACT[1, mine_rows], W[7])
        arrive(OR, xr.at[3])
        output = X1[...] + output + OR[...].astype(F32) + b_down
        y_ref[...] = output[0:live].astype(BF16)
        give(0)

    def down_done():
        gd_ref[...] += landed(1)
        give(5)

    def up_done():
        gu_ref[...] += landed(3)
        give(4)

    def attention_done():
        @pl.when(inner)
        def _():
            arrive(VR.at[0], rr.at[4, 7])
            BL[...] += VR[0].astype(F32)

        block = BL[...] + landed(5)
        gq_ref[...] = jnp.concatenate(
            [block[:, s * 192 + h * 64:s * 192 + h * 64 + 64] for h in range(3) for s in range(3)], axis=1)
        give(2)
        go_ref[...] = block[:, 576:768].T
        give(3)

    share_small()
    gather_a(1, 0)
    forward(1, 3, 2, 0)
    gather_a(second_rank, 0)
    forward(3, 1, 2, 0)
    gather_a(second_rank, 1)
    forward(3, 1, 2, 1)
    gather_a(1, 1)
    forward(1, 3, 2, 1)
    share_down()
    gather_a(third_rank, 0)
    forward(2, 1, 3, 0)
    gather_y(second_rank, 1)
    share_up()
    gather_x(second_rank, 0)
    gather_small(1)
    gather_a(third_rank, 1)
    forward(2, 1, 3, 1)
    gather_x(1, 0)
    gather_y(1, 1)
    attend_first()
    gather_y(second_rank, 0)
    share_cotangent()
    gather_small(3)
    gather_x(second_rank, 1)
    gather_x(1, 1)
    gather_c(second_rank)
    gather_y(1, 0)
    gather_x(third_rank, 0)
    gather_y(third_rank, 1)
    gather_small(2)
    gather_y(third_rank, 0)
    gather_a(7)
    gather_x(third_rank, 1)
    gather_c(1)
    attend_next(second_rank)
    gather_a(6)
    gather_c(third_rank)
    attend_next(1)
    attend_next(third_rank)
    second_norm(0)
    second_norm(1)
    gather_y(7)
    gather_x(7)
    gather_y(6)
    gather_x(6)
    back_hidden(0)
    gather_c(7)
    back_hidden(1)
    transpose_rows()
    gather_c(6)
    feed(0)
    feed(0, 0)
    feed(1)
    feed(1, 0)
    hidden_back(0)
    feed(1, 1)
    store_block(1)
    feed(0, 1)
    reduce_2(1)
    hidden_back(1)
    store_block(3)
    store_block(2)
    own_hidden_back()
    reduce_2(3)
    hidden_out()
    reduce_3(1)
    reduce_2(2)
    second_norm_back()
    attend_back(3)
    attend_back(2)
    reduce_4(1)
    reduce_3(3)
    reduce_2(7)
    attend_back(1)
    small_1(EV, 0)
    small_2(EV, 0)
    reduce_2(6)
    attend_back(0)
    reduce_4(3)
    reduce_3(7)
    first_norm_sums()
    small_2(LV, 1)
    store_block(0)
    small_3(EV, 0)
    reduce_2(5)
    reduce_3(6)
    reduce_4(7)
    small_3(LV, 1)
    small_4(EV, 0)
    reduce_2(4)
    reduce_3(5)
    reduce_4(6)
    input_grad()
    chain(6)
    layer_output()
    reduce_2(0)
    small_4(LV, 1)
    reduce_4(5)
    small_5(EV, 0)
    reduce_3(4)
    chain(7)
    reduce_3(2)
    chain(5)
    reduce_3(0)
    reduce_4(2)
    reduce_4(4)
    up_done()
    small_5(LV, 1)
    attention_done()
    reduce_4(0)
    down_done()

    sv_ref[0:2, :] = LV[6, 0:2, :] + LV[7, 0:2, :] + LV[8, 0:2, :] + LV[9, 0:2, :]
    sv_ref[2:6, :] = EV[6, 0:4, :] + EV[7, 0:4, :] + EV[8, 0:4, :] + EV[9, 0:4, :]
    sv_ref[6:7, :] = EV[6, 4:5, :] + EV[8, 5:6, :]
    bias = LV[6, 2:3, :] + EV[7, 6:7, :] + EV[8, 7:8, :] + EV[9, 8:9, :]
    bias = [bias[:, s * 192 + h * 64:s * 192 + h * 64 + 64] for h in range(3) for s in range(3)]
    sv_ref[7:8, :] = jnp.concatenate(bias + [jnp.zeros((1, 192), F32)], axis=1)
    give(6)
    for copy in sends:
        copy.wait_send()
    for condition, copy in late_sends:
        pl.when(condition)(copy.wait_send)
    for copy in gives:
        copy.wait()


def write_outputs(y, gx, gq, go, gu, gd, sv, *outs):
    refs = (y, gx, gq, go, gu, gd)
    for source, target in zip(refs, outs[:6]):
        target[...] = source[...]
    for i, target in enumerate(outs[6:13]):
        target[...] = sv[i:i + 1, :].reshape(768)
    outs[13][...] = sv[7:8, 0:576].reshape(576)


def trig_table(live, rows, head_dim):
    half = head_dim // 2
    freq = (10000.0 ** (-np.arange(half, dtype=np.float32) * 2.0 / head_dim)).astype(np.float32)
    angle = (np.arange(rows, dtype=np.float32)[:, None] * freq[None, :]).astype(np.float64)
    cosine, sine = np.cos(angle), np.sin(angle)
    table = np.concatenate([cosine, cosine, -sine, sine], axis=1) * head_dim ** (-0.25)
    return table.astype(np.float32)


def local(
    n_dp, layer_input, lengths, ln1_gain, ln1_bias, w_qkv, b_qkv, features, w_out, b_out,
    ln2_gain, ln2_bias, w_up, b_up, w_down, b_down, cotangent,
):
    live, width = layer_input.shape
    rows = -(-live // 16) * 16
    trig = jnp.asarray(trig_table(live, rows, features.shape[1]))
    vmem = pl.BlockSpec(memory_space=pltpu.VMEM)
    anywhere = pl.BlockSpec(memory_space=pl.ANY)
    dma = pltpu.SemaphoreType.DMA

    def buf(*shape):
        return pltpu.VMEM(shape, BF16)

    def wide(*shape):
        return pltpu.VMEM(shape, F32)

    outs = pl.pallas_call(
        functools.partial(layer_kernel, live),
        out_shape=[
            jax.ShapeDtypeStruct((live, width), BF16),
            jax.ShapeDtypeStruct((live, width), F32),
            jax.ShapeDtypeStruct((96, 576), F32),
            jax.ShapeDtypeStruct((192, 96), F32),
            jax.ShapeDtypeStruct((96, 768), F32),
            jax.ShapeDtypeStruct((96, 768), F32),
            jax.ShapeDtypeStruct((8, 768), F32),
        ],
        in_specs=[anywhere] * 17,
        out_specs=[anywhere] * 7,
        scratch_shapes=[
            buf(live, width), buf(live, width), pltpu.SMEM(lengths.shape, jnp.int32)] + [
            wide(width) for _ in range(6)] + [
            wide(*b_up.shape), wide(*b_qkv.shape), wide(features.shape[0], features.shape[2], features.shape[1]),
            wide(*trig.shape), buf(live, width), wide(live, width), wide(96, 576), wide(192, 96),
            wide(96, 768), wide(96, 768), wide(8, 768),
            buf(8, 768, 768), wide(4, 80, 128), buf(2 * rows, 768), buf(2 * rows, 768),
            buf(768, 2 * rows), buf(768, 2 * rows), buf(rows, 768), buf(768, rows),
            buf(rows, 768), buf(768, rows), wide(rows, 768), wide(rows, 1), wide(rows, 768),
            wide(rows, 768), wide(rows, 1), wide(rows, 768), wide(rows, 768),
            wide(rows, 384), wide(rows, 384), buf(4, 384, 192), buf(4, 384, 192),
            buf(4, rows, 192), wide(4, rows, 192), buf(4, rows, 192), wide(4, rows, 192),
            wide(4, rows, 192), buf(4, rows, 192), wide(4, 192, 192), wide(4, 192, 192),
            wide(2, 2 * rows, 768), buf(2, 2 * rows, 768), buf(2, 2 * rows, 768), buf(rows, 576),
            buf(rows, 768), buf(rows, 768), buf(rows, 768), buf(rows, 768),
            buf(8, 4, 2, 96, 768), buf(8, 4, 96, 768), buf(8, 2, 48, 768), buf(8, 2, 48, 768),
            buf(8, 2, 48, 768), buf(8, 2, 48, 768), buf(8, 96, 768), buf(8, 96, 768), buf(3, 96, 768), buf(2, 96, 768), wide(96, 768),
            wide(10, 16, 768), wide(10, 8, 768),
            dma((4,)), dma((13,)), dma((7,)), dma((32,)), dma((8,)), dma((8, 16)), dma((8, 16)), dma((6,)), dma((6,)),
            dma((8, 8)), dma((8, 8)), dma((2, 6)), dma((2, 6)),
        ],
        compiler_params=pltpu.CompilerParams(
            collective_id=0, has_side_effects=True, vmem_limit_bytes=67043328),
    )(
        layer_input, cotangent, lengths, ln1_gain, ln1_bias, b_out, ln2_gain, ln2_bias, b_down,
        b_up, b_qkv, features.transpose(0, 2, 1), trig, w_qkv.T, w_out, w_up, w_down)
    outs = pl.pallas_call(
        write_outputs,
        out_shape=[jax.ShapeDtypeStruct(out.shape, out.dtype) for out in outs[:6]]
        + [jax.ShapeDtypeStruct((width,), F32)] * 7 + [jax.ShapeDtypeStruct((576,), F32)],
        in_specs=[vmem] * 7,
        out_specs=[vmem] * 14,
    )(*outs)
    output, grad_x, qkv_piece, out_piece, up_piece, down_piece, *common, up_bias, qkv_bias = outs
    down_piece = down_piece.T
    if n_dp != GROUP:
        member = lax.axis_index("dp") % GROUP

        def spread(piece, axis):
            shape = list(piece.shape)
            shape[axis] = shape[axis] * GROUP
            start = [0, 0]
            start[axis] = member * piece.shape[axis]
            whole = lax.dynamic_update_slice(jnp.zeros(shape, F32), piece, start)
            return lax.psum_scatter(whole, "dp", scatter_dimension=axis, tiled=True)

        qkv_piece, out_piece = spread(qkv_piece, 0), spread(out_piece, 1)
        up_piece, down_piece = spread(up_piece, 0), spread(down_piece, 1)
        common, up_bias, qkv_bias = jax.tree.map(
            lambda part: lax.psum(part, "dp") / GROUP, (common, up_bias, qkv_bias))
    return (
        output, grad_x, common[0], common[1], qkv_piece, qkv_bias, out_piece, common[2],
        common[3], common[4], up_piece, up_bias, down_piece, common[5],
    )


def solution(mesh):
    rows, cols = P(("dp", "mp"), None), P(None, "mp")
    placed = (
        rows, P("dp"), P(), P(), cols, P("mp"), P("mp", None, None), P("mp", None), P(),
        P(), P(), cols, P("mp"), P("mp", None), P(), rows,
    )
    return jax.shard_map(
        functools.partial(local, mesh.shape["dp"]),
        mesh=mesh,
        in_specs=placed,
        out_specs=(
            rows, rows, P(), P(), P("dp", "mp"), P("mp"), P("mp", "dp"), P(),
            P(), P(), P("dp", "mp"), P("mp"), P("mp", "dp"), P(),
        ),
        check_vma=False,
    )
```

```python
import functools

import jax
import jax.numpy as jnp
import numpy as np
from jax import lax
from jax.experimental import pallas as pl
from jax.experimental.pallas import tpu as pltpu
from jax.sharding import PartitionSpec as P

MESH = pl.DeviceIdType.MESH
BF16 = jnp.bfloat16
F32 = jnp.float32
EPSILON = 1e-05
GROUP = 8


def dot_nn(left, right):
    return lax.dot_general(left, right, (((1,), (0,)), ((), ())), preferred_element_type=F32)


def dot_nt(left, right):
    return lax.dot_general(left, right, (((1,), (1,)), ((), ())), preferred_element_type=F32)


def dot_tn(left, right):
    return lax.dot_general(left, right, (((0,), (0,)), ((), ())), preferred_element_type=F32)


def split(values):
    high = values.astype(BF16)
    return high, (values - high.astype(F32)).astype(BF16)


def normalize(values):
    centred = values - jnp.mean(values, axis=-1, keepdims=True)
    factor = lax.rsqrt(jnp.mean(centred * centred, axis=-1, keepdims=True) + EPSILON)
    return centred * factor, factor


def norm_back(grad, gain, normed, factor):
    hat = grad * gain
    return factor * (
        hat
        - jnp.mean(hat, axis=-1, keepdims=True)
        - normed * jnp.mean(hat * normed, axis=-1, keepdims=True)
    )


def column_sum(values):
    return jnp.sum(values, axis=0, keepdims=True)


def swap_halves(values):
    width = values.shape[1]
    lane = lax.broadcasted_iota(jnp.int32, values.shape, 1)
    return jnp.where(lane % 64 < 32, pltpu.roll(values, width - 32, 1), pltpu.roll(values, 32, 1))


def layer_kernel(live, *refs):
    (
        wqkv_ref, wout_ref, wup_ref, wdown_ref,
        x_ref, c_ref, len_ref, ln1_gain_ref, ln1_bias_ref, b_out_ref, ln2_gain_ref, ln2_bias_ref,
        b_down_ref, b_up_ref, b_qkv_ref, feat_ref, trig_ref,
        y_ref, gx_ref, gq_ref, go_ref, gu_ref, gd_ref, sv_ref,
        W, SP, CC, H2, CT, H2T, H1, H1T, GO, GOT, N1, R1, X1, N2, R2, DX1, DH1,
        COS, SIN, FH, FL, PHI, EE, VV, ATT, INV, AB, ST, TT, DA, ACT, DPRE, DQ,
        OS, OR, HS, HR, G, Q0, QX, QY, T2, Q2, U, ZR, VS, VR, BL, EV, LV,
        local_sem, in_sem, out_sem, zs, zr, ags, agr, xs, xr, rs, rr, vs, vr,
    ) = refs[13:17] + refs[24:]
    rows = CC.shape[0] // 2
    dp = lax.axis_index("dp")
    z = lax.axis_index("mp")
    member = dp % GROUP
    c = member % 2
    bx = (member // 2) % 2
    by = member // 4
    nx = (dp + 2 - 4 * bx, z)
    ny = (dp + 4 - 8 * by, z)
    nc = (dp + 1 - 2 * c, z)
    nz = (None, (dp, z + 1 - 2 * (z % 2)), (dp, (z + 2) % 4), (dp, 3 - z))

    def place(yy, xx, cc):
        return pl.multiple_of((yy * 4 + xx * 2 + cc) * 96, 96)

    sends = []
    done = set()

    def once(key, action, *args):
        if key not in done:
            done.add(key)
            action(*args)

    def send(src, dst, send_sem, recv_sem, device):
        copy = pltpu.make_async_remote_copy(
            src_ref=src, dst_ref=dst, send_sem=send_sem, recv_sem=recv_sem,
            device_id=device, device_id_type=MESH,
        )
        copy.start()
        sends.append(copy)

    def arrive(dst, recv_sem):
        pltpu.make_async_remote_copy(
            src_ref=dst, dst_ref=dst, send_sem=recv_sem, recv_sem=recv_sem,
            device_id=nc, device_id_type=MESH,
        ).wait_recv()

    barrier = pltpu.get_barrier_semaphore()
    for device in (nx, ny, nc, nz[1], nz[2], nz[3]):
        pl.semaphore_signal(barrier, inc=1, device_id=device, device_id_type=MESH)

    takes = [
        pltpu.make_async_copy(source, target, in_sem.at[i])
        for i, (source, target) in enumerate(zip(refs[:13], refs[24:37]))
    ]
    for take in takes:
        take.start()
    gives = []

    def give(i):
        copy = pltpu.make_async_copy(refs[37 + i], refs[17 + i], out_sem.at[i])
        copy.start()
        gives.append(copy)

    loads = [
        pltpu.make_async_copy(source, target, local_sem.at[i])
        for i, (source, target) in enumerate((
            (wqkv_ref, W.at[0, 0:576]), (wout_ref, W.at[0, 576:768]),
            (wup_ref, W.at[4]), (wdown_ref, W.at[5])))
    ]
    for load in loads:
        load.start()

    pl.semaphore_wait(barrier, 6)

    own = pl.ds(place(by, bx, c), 96)
    inner = jnp.logical_or(z == 1, z == 2)
    second_rank = jnp.where(inner, 3, 2)
    third_rank = jnp.where(inner, 2, 3)

    def send_if(condition, src, dst, send_sem, recv_sem, device):
        copy = pltpu.make_async_remote_copy(
            src_ref=src, dst_ref=dst, send_sem=send_sem, recv_sem=recv_sem,
            device_id=device, device_id_type=MESH,
        )

        @pl.when(condition)
        def _():
            copy.start()

        late_sends.append((condition, copy))

    late_sends = []
    in_qkv = member < 6
    out_rows = pl.ds(pl.multiple_of(jnp.maximum(own.start - 576, 0), 96), 96)
    qkv_rows = pl.ds(pl.multiple_of(jnp.minimum(own.start, 480), 96), 96)
    for r, condition in ((1, None), (3, inner)):
        for h in (0, 1):
            here = pl.ds(pl.multiple_of(own.start + 48 * h, 48), 48)
            for part, ref, start in ((in_qkv, wqkv_ref, qkv_rows.start), (jnp.logical_not(in_qkv), wout_ref, out_rows.start)):
                both = part if condition is None else jnp.logical_and(part, condition)
                source = ref.at[pl.ds(pl.multiple_of(start + 48 * h, 48), 48)]
                send_if(both, source, W.at[r, here], zs.at[r + 16 * h], agr.at[r, h], nz[r])
    half = pl.ds(pl.multiple_of(c * 40, 8), 40)
    other_half = pl.ds(pl.multiple_of((1 - c) * 40, 8), 40)

    for take in takes:
        take.wait()
    SP[0, 0:64, 0:96] = feat_ref[...].reshape(96, 64).T
    qkv_bias = b_qkv_ref[...].reshape(1, 576)
    qkv_bias = jnp.concatenate(
        [qkv_bias[:, h * 192 + s * 64:h * 192 + s * 64 + 64] for s in range(3) for h in range(3)]
        + [jnp.zeros((1, 64), F32)], axis=1)
    for i in range(5):
        SP[0, 64 + i:65 + i, :] = qkv_bias[:, i * 128:i * 128 + 128]
    up_bias = b_up_ref[...].reshape(1, 768)
    for i in range(6):
        SP[0, 72 + i:73 + i, :] = up_bias[:, i * 128:i * 128 + 128]
    CC[0:rows, :] = jnp.concatenate([c_ref[...].astype(F32), jnp.zeros((rows - live, 768), F32)], axis=0).astype(BF16)

    def forward(b, to_rank, slot, h):
        here = pl.ds(pl.multiple_of(own.start + 48 * h, 48), 48)
        send_if(inner, W.at[b, here], W.at[slot, here], zs.at[3 + slot + to_rank + 16 * h], agr.at[slot, h], nz[to_rank])

    at_d = pl.ds(place(1 - by, 1 - bx, c), 96)
    at_x0 = pl.ds(place(by, 1 - bx, c), 48)
    at_y1 = pl.ds(pl.multiple_of(place(1 - by, bx, c) + 48, 48), 48)
    at_d0 = pl.ds(place(1 - by, 1 - bx, c), 48)
    at_d1 = pl.ds(pl.multiple_of(place(1 - by, 1 - bx, c) + 48, 48), 48)

    def rows_at(yy, xx, cc, h):
        start = place(yy, xx, cc)
        return pl.ds(start, 96) if h is None else pl.ds(pl.multiple_of(start + 48 * h, 48), 48)

    def halves(b):
        return (None,) if isinstance(b, int) and b > 1 else (0, 1)

    def gather_a(b, h=None):
        k = h or 0
        part = W.at[b, rows_at(by, bx, c, h)]
        arrive(part, agr.at[b, k])
        send(part, part, ags.at[b, k], agr.at[b, 2 + k], nx)
        send(part, part, ags.at[b, 2 + k], agr.at[b, 4 + k], ny)
        send(part, part, ags.at[b, 4 + k], agr.at[b, 6 + k], nc)

    def gather_x(b, h=None):
        k = h or 0
        part = W.at[b, rows_at(by, 1 - bx, c, h)]
        arrive(part, agr.at[b, 2 + k])
        if h != 1:
            send(W.at[b, at_x0], W.at[b, at_x0], ags.at[b, 6], agr.at[b, 14], ny)
        send(part, part, ags.at[b, 8 + k], agr.at[b, 8 + k], nc)

    def gather_y(b, h=None):
        k = h or 0
        part = W.at[b, rows_at(1 - by, bx, c, h)]
        arrive(part, agr.at[b, 4 + k])
        if h != 0:
            send(W.at[b, at_y1], W.at[b, at_y1], ags.at[b, 7], agr.at[b, 15], nx)
        send(part, part, ags.at[b, 10 + k], agr.at[b, 10 + k], nc)

    def gather_c(b):
        arrive(W.at[b, at_d0], agr.at[b, 14])
        arrive(W.at[b, at_d1], agr.at[b, 15])
        send(W.at[b, at_d], W.at[b, at_d], ags.at[b, 12], agr.at[b, 12], nc)

    def gather_small(r):
        arrive(SP.at[r, half], zr.at[r])
        send(SP.at[r, half], SP.at[r, half], zs.at[12 + r], zr.at[4 + r], nc)

    def small_done(r):
        arrive(SP.at[r, other_half], zr.at[4 + r])

    def qkv_rows_of(r):
        return jnp.concatenate(
            [W[r, h * 192 + s * 64:h * 192 + s * 64 + 64, :] for s in range(3) for h in range(3)], axis=0)

    def gather_d(b):
        for n, (yy, xx) in enumerate(((by, bx), (by, 1 - bx), (1 - by, bx))):
            for h in halves(b):
                arrive(W.at[b, rows_at(yy, xx, 1 - c, h)], agr.at[b, 6 + 2 * n + (h or 0)])
        arrive(W.at[b, rows_at(1 - by, 1 - bx, 1 - c, None)], agr.at[b, 12])

    rank = (0, 2, 0, 2, 0, 1, 2, 3)
    kept = {0: gd_ref, 2: gu_ref, 4: BL}

    def reduce_1(g):
        send(G.at[g, :, 1 - c], Q0.at[g], rs.at[g, 0], rr.at[g, 0], nc)

    def reduce_2(g):
        arrive(Q0.at[g], rr.at[g, 0])
        for i in range(4):
            Q0[g, i] = (Q0[g, i].astype(F32) + G[g, i, c].astype(F32)).astype(BF16)
        for i in range(2):
            send(Q0.at[g, 2 * i + 1 - bx, 0:48], QX.at[g, i], rs.at[g, 1 + i], rr.at[g, 1 + i], nx)
            send(Q0.at[g, 2 * (1 - by) + i, 48:96], QY.at[g, i], rs.at[g, 3 + i], rr.at[g, 3 + i], ny)

    def reduce_3(g):
        for i in range(2):
            arrive(QX.at[g, i], rr.at[g, 1 + i])
            arrive(QY.at[g, i], rr.at[g, 3 + i])
        T2[g, 0] = (Q0[g, 2 * (1 - by) + bx, 0:48].astype(F32) + QX[g, 1 - by].astype(F32)).astype(BF16)
        T2[g, 1] = (Q0[g, 2 * by + 1 - bx, 48:96].astype(F32) + QY[g, 1 - bx].astype(F32)).astype(BF16)
        send(T2.at[g, 0], Q2.at[g, 0], rs.at[g, 5], rr.at[g, 5], ny)
        send(T2.at[g, 1], Q2.at[g, 1], rs.at[g, 6], rr.at[g, 6], nx)

    def reduce_4(g):
        arrive(Q2.at[g, 0], rr.at[g, 5])
        arrive(Q2.at[g, 1], rr.at[g, 6])
        mine = 2 * by + bx
        first = Q0[g, mine, 0:48].astype(F32) + QX[g, by].astype(F32) + Q2[g, 0].astype(F32)
        second = Q0[g, mine, 48:96].astype(F32) + QY[g, bx].astype(F32) + Q2[g, 1].astype(F32)
        total = jnp.concatenate([first, second], axis=0)
        if rank[g] == 0:
            kept[g][...] = total
        else:
            U[g] = total.astype(BF16)
            if g < 4:
                send(U.at[g], ZR.at[g], rs.at[g, 7], rr.at[g, 7], nz[rank[g]])
            else:
                send_if(jnp.logical_not(inner), U.at[g], ZR.at[g], rs.at[g, 7], rr.at[g, 7], nz[1])

    def chain(g):
        source, landing, target, there, device = {
            7: (ZR.at[6], rr.at[6, 7], VR.at[0], rr.at[4, 7], nz[3]),
            6: (ZR.at[7], rr.at[7, 7], VR.at[1], rr.at[0, 7], nz[3]),
            5: (VR.at[1], rr.at[0, 7], ZR.at[5], rr.at[5, 7], nz[1]),
        }[g]

        @pl.when(inner)
        def _():
            arrive(source, landing)
            VS[g - 5] = (source[...].astype(F32) + U[g].astype(F32)).astype(BF16)

        send_if(inner, VS.at[g - 5], target, rs.at[g, 7], there, device)

    def landed(g):
        arrive(ZR.at[g], rr.at[g, 7])
        return ZR[g].astype(F32)

    ln1_gain, ln1_bias, b_out, ln2_gain, ln2_bias, b_down = (
        ref[...].reshape(1, 768)
        for ref in (ln1_gain_ref, ln1_bias_ref, b_out_ref, ln2_gain_ref, ln2_bias_ref, b_down_ref))
    position = lax.broadcasted_iota(jnp.int32, (rows, 1), 0)
    key_mask = (position < len_ref[z]).astype(F32)
    trig = trig_ref[...]
    COS[...] = jnp.concatenate([trig[:, 0:64]] * 6, axis=1)
    SIN[...] = jnp.concatenate([trig[:, 64:128]] * 6, axis=1)
    row_q = lax.broadcasted_iota(jnp.int32, (192, 192), 0)
    col_q = lax.broadcasted_iota(jnp.int32, (192, 192), 1)
    head_mask = jnp.logical_and(row_q < 96, row_q // 32 == col_q // 64)
    row_f = lax.broadcasted_iota(jnp.int32, (384, 192), 0)
    col_f = lax.broadcasted_iota(jnp.int32, (384, 192), 1)
    feat_mask = row_f // 64 == col_f // 32

    X1[...] = jnp.concatenate([x_ref[...].astype(F32), jnp.zeros((rows - live, 768), F32)], axis=0)
    normed, factor = normalize(X1[...])
    N1[...] = normed
    R1[...] = factor
    first = (normed * ln1_gain + ln1_bias).astype(BF16)
    H1[...] = first

    def attend(r):
        bias = jnp.concatenate([SP[r, 64 + i:65 + i, :] for i in range(5)], axis=1)[:, 0:576]
        projected = dot_nt(H1[...], qkv_rows_of(r)) + bias
        both = projected[:, 0:384]
        value = projected[:, 384:576].astype(BF16)
        turned = both * COS[...] + swap_halves(both) * SIN[...]
        plain = SP[r, 0:64, :][:, 0:96]
        plain = jnp.concatenate([plain, plain], axis=1)
        block = jnp.where(feat_mask, jnp.concatenate([plain] * 6, axis=0), 0.0)
        f_high, f_low = split(block)
        FH[r] = f_high
        FL[r] = f_low
        t_high, t_low = split(turned)
        u = dot_nn(t_high, f_high) + dot_nn(t_high, f_low) + dot_nn(t_low, f_high)
        decay = jnp.exp(jnp.minimum(u, 0.0))
        EE[r] = decay
        phi32 = jnp.where(u > 0.0, u + 1.0, decay)
        phi = phi32.astype(BF16)
        PHI[r] = phi
        VV[r] = value
        masked = (phi.astype(F32) * key_mask).astype(BF16)
        pad = jnp.zeros((96, 192), F32)
        state = jnp.concatenate([dot_tn(masked, value)[96:192], pad], axis=0)
        total = jnp.concatenate([dot_tn(masked, jnp.ones((rows, 192), BF16))[96:192], pad], axis=0)
        state = jnp.where(head_mask, state, 0.0)
        total = jnp.where(head_mask, total, 0.0)
        ST[r] = state
        TT[r] = total
        s_high, s_low = split(state)
        k_high, k_low = split(total)
        numer = dot_nn(phi, s_high) + dot_nn(phi, s_low)
        inverse = 1.0 / (dot_nn(phi, k_high) + dot_nn(phi, k_low))
        attended = numer * inverse
        ATT[r] = attended
        INV[r] = inverse
        mixed = attended.astype(BF16)
        AB[r] = mixed
        X1[...] += dot_nn(mixed, W[r, 576:768, :])

    theirs = pl.ds(rows, rows)
    mine_rows = pl.ds(0, rows)
    up = (4, 6)
    down = (5, 7)
    EV[0, 9:16, :] = jnp.zeros((7, 768), F32)
    LV[0, 3:8, :] = jnp.zeros((5, 768), F32)

    def share_small():
        for r in (1, 2, 3):
            send(SP.at[0, half], SP.at[r, half], zs.at[8 + r], zr.at[r], nz[r])

    def share_up():
        send(wup_ref.at[own], W.at[6, own], zs.at[2], agr.at[6, 0], nz[2])

    def share_down():
        send(wdown_ref.at[own], W.at[7, own], zs.at[0], agr.at[7, 0], nz[2])

    def share_cotangent():
        send(CC.at[0:rows], CC.at[rows:2 * rows], xs.at[0], xr.at[0], nz[1])

    def whole(b):
        for r in (2, 3) if b is second_rank or b is third_rank else (1,) if b == 1 else (2,):
            once(("small", r), small_done, r)
        gather_d(b)

    def loaded(i):
        once(("load", i), loads[i].wait)

    def cotangent_here():
        once("cotangent", arrive, CC.at[rows:2 * rows], xr.at[0])

    cuts = ((0, 96), (96, rows))

    def second_here(k):
        lo, hi = cuts[k]
        once(("second", k), arrive, H2.at[rows + lo:rows + hi], xr.at[1 + 3 * k])

    def attend_first():
        loaded(0)
        loaded(1)
        attend(0)

    def attend_next(b):
        whole(b)
        attend(b)

    def second_norm(k):
        lo, hi = cuts[k]
        middle = X1[lo:hi] + b_out
        X1[lo:hi] = middle
        normed, factor = normalize(middle)
        N2[lo:hi] = normed
        R2[lo:hi] = factor
        H2[lo:hi, :] = (normed * ln2_gain + ln2_bias).astype(BF16)
        send(H2.at[lo:hi], H2.at[rows + lo:rows + hi], xs.at[1 + 3 * k], xr.at[1 + 3 * k], nz[1])

    def back_hidden(q):
        cotangent_here()
        if q == 0:
            loaded(3)
        else:
            gather_d(7)
        DA[q] = dot_nt(CC[...], W[down[q]])

    def feed(q, k=None):
        lo, hi = 0, rows
        if k is not None:
            second_here(k)
            lo, hi = rows + cuts[k][0], rows + cuts[k][1]
        if q == 0:
            loaded(2)
        else:
            once("up", whole, 6)
        part = pl.ds(lo, hi - lo)
        bias = jnp.concatenate([SP[2 * q, 72 + i:73 + i, :] for i in range(6)], axis=1)
        pre = dot_nn(H2[part], W[up[q]]) + bias
        half = 0.5 * (1.0 + lax.erf(pre * (0.5 ** 0.5)))
        ACT[q, part] = (pre * half).astype(BF16)
        slope = half + pre * jnp.exp(-0.5 * pre * pre) * (0.5 / np.pi) ** 0.5
        DPRE[q, part] = (DA[q, part] * slope).astype(BF16)

    def transpose_rows():
        cotangent_here()
        CT[...] = CC[...].T
        H1T[...] = H1[...].T

    def transpose_second():
        H2T[...] = H2[...].T

    def store_block(g):
        q = g % 2
        if g >= 2:
            once("turned", transpose_second)
        for n in range(3):
            cols = slice(n * 256, n * 256 + 256)
            if g < 2:
                block = dot_nn(CT[...], ACT[q, :, cols])
            else:
                block = dot_nn(H2T[...], DPRE[q, :, cols])
            G[g, :, :, :, cols] = block.astype(BF16).reshape(4, 2, 96, 256)
        reduce_1(g)

    def hidden_back(k):
        lo, hi = cuts[k]
        part = pl.ds(rows + lo, hi - lo)
        HS[lo:hi] = (dot_nt(DPRE[0, part], W[4]) + dot_nt(DPRE[1, part], W[6])).astype(BF16)
        send(HS.at[lo:hi], HR.at[lo:hi], xs.at[2 + 3 * k], xr.at[2 + 3 * k], nz[1])

    def hidden_out():
        OS[...] = (dot_nn(ACT[0, theirs], W[5]) + dot_nn(ACT[1, theirs], W[7])).astype(BF16)
        send(OS, OR, xs.at[3], xr.at[3], nz[1])
        for q in range(2):
            EV[0, 4 + q:5 + q, :] = column_sum(DPRE[q].astype(F32))

    def own_hidden_back():
        DH1[...] = dot_nt(DPRE[0, mine_rows], W[4]) + dot_nt(DPRE[1, mine_rows], W[6])

    def second_norm_back():
        for k, (lo, hi) in enumerate(cuts):
            arrive(HR.at[lo:hi], xr.at[2 + 3 * k])
        own_back = DH1[...] + HR[...].astype(F32)
        cot = CC[mine_rows].astype(F32)
        EV[0, 1:2, :] = column_sum(own_back * N2[...])
        EV[0, 2:3, :] = column_sum(own_back)
        EV[0, 3:4, :] = column_sum(cot)
        dx1 = cot + norm_back(own_back, ln2_gain, N2[...], R2[...])
        DX1[...] = dx1
        branch = dx1.astype(BF16)
        GO[...] = branch
        EV[0, 0:1, :] = column_sum(branch.astype(F32))
        GOT[...] = GO[...].T

    def store_attention(r):
        g = 4 + r
        for n in range(2):
            cols = slice(n * 256, n * 256 + 256)
            G[g, :, :, :, cols] = dot_nn(H1T[...], DQ[:, cols]).astype(BF16).reshape(4, 2, 96, 256)
        edge = jnp.concatenate(
            [dot_nn(H1T[...], DQ[:, 512:576]), dot_nn(GOT[...], AB[r])], axis=1)
        G[g, :, :, :, 512:768] = edge.astype(BF16).reshape(4, 2, 96, 256)

    def attend_back(r):
        da = dot_nt(GO[...], W[r, 576:768, :])
        phi = PHI[r]
        dnum = da * INV[r]
        drest = -(dnum * ATT[r])
        n_high, n_low = split(dnum)
        d_high, d_low = split(drest)
        s_high, s_low = split(ST[r])
        k_high, k_low = split(TT[r])
        dphi = dot_nt(n_high, s_high) + dot_nt(n_high, s_low) + dot_nt(n_low, s_high)
        dphi += dot_nt(d_high, k_high) + dot_nt(d_high, k_low) + dot_nt(d_low, k_high)
        pad = jnp.zeros((96, 192), F32)
        dstate = jnp.where(head_mask, dot_tn(phi, n_high) + dot_tn(phi, n_low), 0.0)
        dtotal = jnp.where(head_mask, dot_tn(phi, d_high) + dot_tn(phi, d_low), 0.0)
        a_high, a_low = split(jnp.concatenate([pad, dstate[0:96]], axis=0))
        b_high, b_low = split(jnp.concatenate([pad, dtotal[0:96]], axis=0))
        ones = jnp.ones((16, 192), BF16)
        dkey = dot_nt(VV[r], a_high) + dot_nt(VV[r], a_low)
        dkey += (dot_nt(ones, b_high) + dot_nt(ones, b_low))[0:1, :]
        dphi += key_mask * dkey
        dvalue = key_mask * (dot_nn(phi, a_high) + dot_nn(phi, a_low))
        u_high, u_low = split(dphi * EE[r])
        back = dot_nt(u_high, FH[r]) + dot_nt(u_high, FL[r]) + dot_nt(u_low, FH[r])
        back = back * COS[...] - swap_halves(back) * SIN[...]
        DQ[:, 0:384] = back.astype(BF16)
        DQ[:, 384:576] = dvalue.astype(BF16)
        bias_sum = jnp.concatenate([column_sum(DQ[...].astype(F32)), jnp.zeros((1, 192), F32)], axis=1)
        if r == 0:
            LV[0, 2:3, :] = bias_sum
        else:
            EV[0, 5 + r:6 + r, :] = bias_sum
        grad = dot_nn(DQ[...], qkv_rows_of(r))
        if "back" in done:
            DH1[...] += grad
        else:
            DH1[...] = grad
        done.add("back")
        store_attention(r)
        reduce_1(4 + r)

    def small_1(V, k):
        send(V.at[0], V.at[1], vs.at[k, 0], vr.at[k, 0], nc)

    def small_2(V, k):
        arrive(V.at[1], vr.at[k, 0])
        V[2] = V[0] + V[1]
        send(V.at[2], V.at[3], vs.at[k, 1], vr.at[k, 1], nx)

    def small_3(V, k):
        arrive(V.at[3], vr.at[k, 1])
        V[4] = V[2] + V[3]
        send(V.at[4], V.at[5], vs.at[k, 2], vr.at[k, 2], ny)

    def small_4(V, k):
        arrive(V.at[5], vr.at[k, 2])
        V[6] = V[4] + V[5]
        for r in (1, 2, 3):
            send(V.at[6], V.at[6 + r], vs.at[k, 2 + r], vr.at[k, 2 + r], nz[r])

    def small_5(V, k):
        for r in (1, 2, 3):
            arrive(V.at[6 + r], vr.at[k, 2 + r])

    def first_norm_sums():
        first_back = DH1[...]
        LV[0, 0:1, :] = column_sum(first_back * N1[...])
        LV[0, 1:2, :] = column_sum(first_back)
        small_1(LV, 1)

    def input_grad():
        gx_ref[...] = (DX1[...] + norm_back(DH1[...], ln1_gain, N1[...], R1[...]))[0:live]
        give(1)

    def layer_output():
        output = dot_nn(ACT[0, mine_rows], W[5]) + dot_nn(ACT[1, mine_rows], W[7])
        arrive(OR, xr.at[3])
        output = X1[...] + output + OR[...].astype(F32) + b_down
        y_ref[...] = output[0:live].astype(BF16)
        give(0)

    def down_done():
        gd_ref[...] += landed(1)
        give(5)

    def up_done():
        gu_ref[...] += landed(3)
        give(4)

    def attention_done():
        @pl.when(inner)
        def _():
            arrive(VR.at[0], rr.at[4, 7])
            BL[...] += VR[0].astype(F32)

        block = BL[...] + landed(5)
        gq_ref[...] = jnp.concatenate(
            [block[:, s * 192 + h * 64:s * 192 + h * 64 + 64] for h in range(3) for s in range(3)], axis=1)
        give(2)
        go_ref[...] = block[:, 576:768].T
        give(3)

    gather_a(second_rank, 0)
    forward(3, 1, 2, 0)
    gather_a(1, 0)
    forward(1, 3, 2, 0)
    gather_a(1, 1)
    forward(1, 3, 2, 1)
    share_down()
    gather_a(second_rank, 1)
    forward(3, 1, 2, 1)
    gather_a(third_rank, 0)
    forward(2, 1, 3, 0)
    gather_y(1, 1)
    gather_y(second_rank, 0)
    gather_x(1, 0)
    share_small()
    gather_x(1, 1)
    gather_a(third_rank, 1)
    forward(2, 1, 3, 1)
    gather_x(second_rank, 0)
    gather_y(1, 0)
    gather_y(second_rank, 1)
    gather_x(third_rank, 0)
    share_up()
    gather_small(1)
    gather_x(second_rank, 1)
    attend_first()
    gather_y(third_rank, 1)
    gather_c(1)
    gather_x(third_rank, 1)
    gather_small(3)
    gather_a(7)
    gather_y(third_rank, 0)
    gather_small(2)
    share_cotangent()
    attend_next(1)
    gather_c(second_rank)
    gather_c(third_rank)
    gather_a(6)
    attend_next(second_rank)
    attend_next(third_rank)
    second_norm(0)
    gather_x(7)
    gather_y(7)
    second_norm(1)
    gather_y(6)
    transpose_rows()
    gather_x(6)
    back_hidden(0)
    feed(0)
    gather_c(7)
    gather_c(6)
    back_hidden(1)
    feed(0, 0)
    feed(1)
    feed(1, 0)
    hidden_back(0)
    feed(1, 1)
    store_block(3)
    feed(0, 1)
    hidden_back(1)
    own_hidden_back()
    reduce_2(3)
    store_block(1)
    store_block(2)
    reduce_2(1)
    reduce_2(2)
    store_block(0)
    hidden_out()
    second_norm_back()
    attend_back(3)
    reduce_3(1)
    reduce_3(3)
    attend_back(2)
    reduce_2(7)
    reduce_4(1)
    reduce_2(6)
    attend_back(0)
    reduce_3(2)
    attend_back(1)
    first_norm_sums()
    small_1(EV, 0)
    reduce_4(3)
    small_2(LV, 1)
    reduce_3(7)
    small_2(EV, 0)
    reduce_3(6)
    small_3(LV, 1)
    reduce_2(5)
    reduce_4(7)
    small_3(EV, 0)
    reduce_2(0)
    input_grad()
    small_4(LV, 1)
    reduce_4(6)
    chain(6)
    reduce_3(5)
    small_4(EV, 0)
    reduce_2(4)
    reduce_4(5)
    reduce_4(2)
    layer_output()
    small_5(LV, 1)
    reduce_3(0)
    up_done()
    chain(5)
    chain(7)
    reduce_3(4)
    reduce_4(0)
    down_done()
    small_5(EV, 0)
    reduce_4(4)
    attention_done()

    sv_ref[0:2, :] = LV[6, 0:2, :] + LV[7, 0:2, :] + LV[8, 0:2, :] + LV[9, 0:2, :]
    sv_ref[2:6, :] = EV[6, 0:4, :] + EV[7, 0:4, :] + EV[8, 0:4, :] + EV[9, 0:4, :]
    sv_ref[6:7, :] = EV[6, 4:5, :] + EV[8, 5:6, :]
    bias = LV[6, 2:3, :] + EV[7, 6:7, :] + EV[8, 7:8, :] + EV[9, 8:9, :]
    bias = [bias[:, s * 192 + h * 64:s * 192 + h * 64 + 64] for h in range(3) for s in range(3)]
    sv_ref[7:8, :] = jnp.concatenate(bias + [jnp.zeros((1, 192), F32)], axis=1)
    give(6)
    for copy in sends:
        copy.wait_send()
    for condition, copy in late_sends:
        pl.when(condition)(copy.wait_send)
    for copy in gives:
        copy.wait()


def write_outputs(y, gx, gq, go, gu, gd, sv, *outs):
    refs = (y, gx, gq, go, gu, gd)
    for source, target in zip(refs, outs[:6]):
        target[...] = source[...]
    for i, target in enumerate(outs[6:13]):
        target[...] = sv[i:i + 1, :].reshape(768)
    outs[13][...] = sv[7:8, 0:576].reshape(576)


def trig_table(live, rows, head_dim):
    half = head_dim // 2
    freq = (10000.0 ** (-np.arange(half, dtype=np.float32) * 2.0 / head_dim)).astype(np.float32)
    angle = (np.arange(rows, dtype=np.float32)[:, None] * freq[None, :]).astype(np.float64)
    cosine, sine = np.cos(angle), np.sin(angle)
    table = np.concatenate([cosine, cosine, -sine, sine], axis=1) * head_dim ** (-0.25)
    return table.astype(np.float32)


def local(
    n_dp, layer_input, lengths, ln1_gain, ln1_bias, w_qkv, b_qkv, features, w_out, b_out,
    ln2_gain, ln2_bias, w_up, b_up, w_down, b_down, cotangent,
):
    live, width = layer_input.shape
    rows = -(-live // 16) * 16
    trig = jnp.asarray(trig_table(live, rows, features.shape[1]))
    vmem = pl.BlockSpec(memory_space=pltpu.VMEM)
    anywhere = pl.BlockSpec(memory_space=pl.ANY)
    dma = pltpu.SemaphoreType.DMA

    def buf(*shape):
        return pltpu.VMEM(shape, BF16)

    def wide(*shape):
        return pltpu.VMEM(shape, F32)

    outs = pl.pallas_call(
        functools.partial(layer_kernel, live),
        out_shape=[
            jax.ShapeDtypeStruct((live, width), BF16),
            jax.ShapeDtypeStruct((live, width), F32),
            jax.ShapeDtypeStruct((96, 576), F32),
            jax.ShapeDtypeStruct((192, 96), F32),
            jax.ShapeDtypeStruct((96, 768), F32),
            jax.ShapeDtypeStruct((96, 768), F32),
            jax.ShapeDtypeStruct((8, 768), F32),
        ],
        in_specs=[anywhere] * 17,
        out_specs=[anywhere] * 7,
        scratch_shapes=[
            buf(live, width), buf(live, width), pltpu.SMEM(lengths.shape, jnp.int32)] + [
            wide(width) for _ in range(6)] + [
            wide(*b_up.shape), wide(*b_qkv.shape), wide(features.shape[0], features.shape[2], features.shape[1]),
            wide(*trig.shape), buf(live, width), wide(live, width), wide(96, 576), wide(192, 96),
            wide(96, 768), wide(96, 768), wide(8, 768),
            buf(8, 768, 768), wide(4, 80, 128), buf(2 * rows, 768), buf(2 * rows, 768),
            buf(768, 2 * rows), buf(768, 2 * rows), buf(rows, 768), buf(768, rows),
            buf(rows, 768), buf(768, rows), wide(rows, 768), wide(rows, 1), wide(rows, 768),
            wide(rows, 768), wide(rows, 1), wide(rows, 768), wide(rows, 768),
            wide(rows, 384), wide(rows, 384), buf(4, 384, 192), buf(4, 384, 192),
            buf(4, rows, 192), wide(4, rows, 192), buf(4, rows, 192), wide(4, rows, 192),
            wide(4, rows, 192), buf(4, rows, 192), wide(4, 192, 192), wide(4, 192, 192),
            wide(2, 2 * rows, 768), buf(2, 2 * rows, 768), buf(2, 2 * rows, 768), buf(rows, 576),
            buf(rows, 768), buf(rows, 768), buf(rows, 768), buf(rows, 768),
            buf(8, 4, 2, 96, 768), buf(8, 4, 96, 768), buf(8, 2, 48, 768), buf(8, 2, 48, 768),
            buf(8, 2, 48, 768), buf(8, 2, 48, 768), buf(8, 96, 768), buf(8, 96, 768), buf(3, 96, 768), buf(2, 96, 768), wide(96, 768),
            wide(10, 16, 768), wide(10, 8, 768),
            dma((4,)), dma((13,)), dma((7,)), dma((32,)), dma((8,)), dma((8, 16)), dma((8, 16)), dma((6,)), dma((6,)),
            dma((8, 8)), dma((8, 8)), dma((2, 6)), dma((2, 6)),
        ],
        compiler_params=pltpu.CompilerParams(
            collective_id=0, has_side_effects=True, vmem_limit_bytes=67043328),
    )(
        layer_input, cotangent, lengths, ln1_gain, ln1_bias, b_out, ln2_gain, ln2_bias, b_down,
        b_up, b_qkv, features.transpose(0, 2, 1), trig, w_qkv.T, w_out, w_up, w_down)
    outs = pl.pallas_call(
        write_outputs,
        out_shape=[jax.ShapeDtypeStruct(out.shape, out.dtype) for out in outs[:6]]
        + [jax.ShapeDtypeStruct((width,), F32)] * 7 + [jax.ShapeDtypeStruct((576,), F32)],
        in_specs=[vmem] * 7,
        out_specs=[vmem] * 14,
    )(*outs)
    output, grad_x, qkv_piece, out_piece, up_piece, down_piece, *common, up_bias, qkv_bias = outs
    down_piece = down_piece.T
    if n_dp != GROUP:
        member = lax.axis_index("dp") % GROUP

        def spread(piece, axis):
            shape = list(piece.shape)
            shape[axis] = shape[axis] * GROUP
            start = [0, 0]
            start[axis] = member * piece.shape[axis]
            whole = lax.dynamic_update_slice(jnp.zeros(shape, F32), piece, start)
            return lax.psum_scatter(whole, "dp", scatter_dimension=axis, tiled=True)

        qkv_piece, out_piece = spread(qkv_piece, 0), spread(out_piece, 1)
        up_piece, down_piece = spread(up_piece, 0), spread(down_piece, 1)
        common, up_bias, qkv_bias = jax.tree.map(
            lambda part: lax.psum(part, "dp") / GROUP, (common, up_bias, qkv_bias))
    return (
        output, grad_x, common[0], common[1], qkv_piece, qkv_bias, out_piece, common[2],
        common[3], common[4], up_piece, up_bias, down_piece, common[5],
    )


def solution(mesh):
    rows, cols = P(("dp", "mp"), None), P(None, "mp")
    placed = (
        rows, P("dp"), P(), P(), cols, P("mp"), P("mp", None, None), P("mp", None), P(),
        P(), P(), cols, P("mp"), P("mp", None), P(), rows,
    )
    return jax.shard_map(
        functools.partial(local, mesh.shape["dp"]),
        mesh=mesh,
        in_specs=placed,
        out_specs=(
            rows, rows, P(), P(), P("dp", "mp"), P("mp"), P("mp", "dp"), P(),
            P(), P(), P("dp", "mp"), P("mp"), P("mp", "dp"), P(),
        ),
        check_vma=False,
    )
```
